32 devices in a mesh: seq: 4 (over y, x), wt: 8 (over z, core).
Axes of the slice: x: 2, y: 2, z: 4, core: 2. Of those that a mesh axis runs over, the one named last changes fastest.
Arguments:
- layer_in: bfloat16 [8, 4096, 768], P('wt', 'seq'), may hold values from -6 to 6
- norm_gain: bfloat16 [768], P(('seq', 'wt')), may hold values from 0.099609375 to 1.8984375
- in_weight: bfloat16 [768, 3376], P(('seq', 'wt')), may hold values from -0.21875 to 0.21875
- conv_weight: bfloat16 [7, 1792], P(None, ('seq', 'wt')), may hold values from -2 to 2
- conv_bias: bfloat16 [1792], P(('seq', 'wt')), may hold values from -3 to 3
- head_params: float32 [3, 24], replicated, may hold values from -6.91 to 2.78, as said below
- out_gain: bfloat16 [1536], P(('seq', 'wt')), may hold values from 0.099609375 to 1.8984375
- out_weight: bfloat16 [1536, 768], P(('seq', 'wt')), may hold values from -0.15625 to 0.15625
- out_cotangent: bfloat16 [8, 4096, 768], P('wt', 'seq'), may hold values from -6 to 6
Outputs:
- layer_out: bfloat16 [8, 4096, 768], P('wt', 'seq')
- in_grad: float32 [8, 4096, 768], P('wt', 'seq')
- norm_gain_grad: float32 [768], P(('seq', 'wt'))
- in_weight_grad: float32 [768, 3376], P(('seq', 'wt'))
- conv_weight_grad: float32 [7, 1792], P(None, ('seq', 'wt'))
- conv_bias_grad: float32 [1792], P(('seq', 'wt'))
- head_grad: float32 [3, 24], replicated
- out_gain_grad: float32 [1536], P(('seq', 'wt'))
- out_weight_grad: float32 [1536, 768], P(('seq', 'wt'))
The draws below stay inside these ranges and needn't reach their ends.
Inputs may be any that keep to these rules, and one draw needn't show every extreme that they name: `head_params`: row 1 entries are at least 0 and row 2 entries are positive.
All inputs are finite; a program needn't handle non-finite values.
Results may differ from the reference program's by a relative error of at most 0.011.
Values may be sent and summed in bfloat16 or wider, within the bound.
No kernel may reach another device: no remote copies, remote signals or barrier semaphores. Data moves between devices by JAX's collectives and lax.ppermute only.
A program may use at most 384 MiB of HBM per device.

```python
import math
import jax
import jax.numpy as jnp
from jax import lax

D = 768
HEADS = 24
HDIM = 64
STRETCH = 128
TAPS = 7
E = 1536
CHANNELS = 1792
PROJ = 3376
LEN = 4096
SEQS = 8


def draw_head_params(key, part):
    key_bias, key_decay, key_skip = jax.random.split(key, 3)
    step_log = jax.random.uniform(key_bias, (HEADS,), jnp.float32, math.log(0.001), math.log(0.1))
    step_init = jnp.exp(step_log)
    step_bias = step_init + jnp.log(-jnp.expm1(-step_init))
    decay_log = jnp.log(jax.random.uniform(key_decay, (HEADS,), jnp.float32, 1.0, 16.0))
    skip_coef = jax.random.uniform(key_skip, (HEADS,), jnp.float32, 0.5, 1.5)
    return jnp.stack([step_bias, decay_log, skip_coef]).astype(jnp.float32)


def block_levels(stream_key, extent, cuts, smallest, top_value):
    def one(position, shards_of):
        steps = jax.random.uniform(jax.random.fold_in(jax.random.fold_in(stream_key, 6), position), (shards_of,), jnp.float32, smallest / len(cuts), top_value / len(cuts))
        return jnp.repeat(jnp.exp(steps), extent[position] // shards_of).reshape((-1,) + (1,) * (len(extent) - position - 1))

    factor_of = one(*cuts[0])
    for cut in cuts[1:]:
        factor_of = factor_of * one(*cut)
    return factor_of


def scatter_about(rng, dims, width, limit, cuts=(), kind=jnp.bfloat16):
    values = width * jax.random.normal(rng, dims, jnp.float32)
    if cuts:
        values = values * block_levels(rng, dims, cuts, -0.22, 0.18)
    return jnp.clip(values, -limit, limit).astype(kind)


def setup_inputs(seed: int = 0) -> dict:
    keys = jax.random.split(jax.random.key(seed), 10)
    layer_in = scatter_about(keys[0], (SEQS, LEN, D), 1.0, 6.0, ((0, 8), (1, 4)))
    norm_gain = jnp.clip(1.0 + 0.18 * jax.random.normal(keys[1], (D,), jnp.float32), 0.099609375, 1.8984375).astype(jnp.bfloat16)
    in_weight = scatter_about(keys[2], (D, PROJ), D ** -0.5, 0.21875, ((0, 32),))
    conv_weight = scatter_about(keys[3], (TAPS, CHANNELS), TAPS ** -0.5, 2.0, ((1, 32),))
    conv_bias = scatter_about(keys[4], (CHANNELS,), 0.5, 3.0, ((0, 32),))
    head_params = draw_head_params(jax.random.fold_in(keys[9], 71), 0)
    out_gain = jnp.clip(1.0 + 0.18 * jax.random.normal(keys[6], (E,), jnp.float32), 0.099609375, 1.8984375).astype(jnp.bfloat16)
    out_weight = scatter_about(keys[7], (E, D), E ** -0.5, 0.15625, ((0, 32),))
    out_cotangent = scatter_about(keys[8], (SEQS, LEN, D), 1.0, 6.0, ((0, 8), (1, 4)))
    return dict(layer_in=layer_in, norm_gain=norm_gain, in_weight=in_weight, conv_weight=conv_weight, conv_bias=conv_bias, head_params=head_params, out_gain=out_gain, out_weight=out_weight, out_cotangent=out_cotangent)


EPSILON = 1e-05
HIGHEST = lax.Precision.HIGHEST

@jax.custom_vjp
def low(v):
    return lax.optimization_barrier(v.astype(jnp.bfloat16)).astype(jnp.float32)

@jax.custom_vjp
def low_back(v):
    return v

def low_keep(v):
    return (low(v), None)

def low_pass(kept, grad):
    return (grad,)

def back_keep(v):
    return (v, None)

def back_low(kept, grad):
    return (low(grad),)
low.defvjp(low_keep, low_pass)
low_back.defvjp(back_keep, back_low)

def one_head(values, step_sizes, decays, gram_blocks, b_blocks, c_blocks):
    blocks = gram_blocks.shape[0]
    block_len = gram_blocks.shape[1]
    channels = values.shape[-1]
    value_blocks = values.reshape(blocks, block_len, channels)
    step_blocks = step_sizes.reshape(blocks, block_len)
    decay_blocks = decays.reshape(blocks, block_len)
    running = jnp.cumsum(decay_blocks, axis=1)
    before = running - decay_blocks
    totals = running[:, -1]
    below_diag = lax.broadcasted_iota(jnp.int32, (block_len, block_len), 0) > lax.broadcasted_iota(jnp.int32, (block_len, block_len), 1)
    exponent = before[:, :, None] - running[:, None, :]
    within = jnp.where(below_diag, jnp.exp(jnp.where(below_diag, exponent, 0.0)), 0.0)
    weights = gram_blocks * within * step_blocks[:, None, :]
    local_part = jnp.einsum('cij,cjp->cip', weights, value_blocks, precision=HIGHEST)
    to_end = jnp.exp(totals[:, None] - running) * step_blocks
    block_states = jnp.einsum('cjn,cjp->cnp', b_blocks, value_blocks * to_end[:, :, None], precision=HIGHEST)
    prefix = jnp.cumsum(totals) - totals
    earlier = lax.broadcasted_iota(jnp.int32, (blocks, blocks), 0) > lax.broadcasted_iota(jnp.int32, (blocks, blocks), 1)
    carried = prefix[:, None] - prefix[None, :] - totals[None, :]
    across = jnp.where(earlier, jnp.exp(jnp.where(earlier, carried, 0.0)), 0.0)
    entering = jnp.einsum('cd,dnp->cnp', across, block_states, precision=HIGHEST)
    from_past = jnp.exp(before)[:, :, None] * jnp.einsum('cin,cnp->cip', c_blocks, entering, precision=HIGHEST)
    return (local_part + from_past).reshape(blocks * block_len, channels)

def direction(values, step_sizes, decays, b_maps, c_maps):
    blocks = values.shape[0] // STRETCH
    b_blocks = b_maps.reshape(blocks, STRETCH, b_maps.shape[-1])
    c_blocks = c_maps.reshape(blocks, STRETCH, c_maps.shape[-1])
    gram_blocks = jnp.einsum('cin,cjn->cij', c_blocks, b_blocks, precision=HIGHEST)
    checked = jax.checkpoint(one_head)

    def per_head(pieces):
        return checked(pieces[0], pieces[1], pieces[2], gram_blocks, b_blocks, c_blocks)
    outputs = lax.map(per_head, (jnp.transpose(values, (1, 0, 2)), jnp.transpose(step_sizes), jnp.transpose(decays)))
    return jnp.transpose(outputs, (1, 0, 2))

def mixer(values, rate_table, state_maps):
    state_size = state_maps.shape[-1] // 4
    b_fwd = state_maps[:, :state_size]
    b_rev = state_maps[:, state_size:2 * state_size]
    c_fwd = state_maps[:, 2 * state_size:3 * state_size]
    c_rev = state_maps[:, 3 * state_size:]
    forward_part = direction(values, rate_table[:, :, 0], rate_table[:, :, 2], b_fwd, c_fwd)
    reverse_part = direction(values[::-1], rate_table[::-1, :, 1], rate_table[::-1, :, 3], b_rev[::-1], c_rev[::-1])[::-1]
    return forward_part + reverse_part

def one_seq(tokens, norm_gain, in_weight, conv_weight, conv_bias, head_params, out_gain, out_weight):
    length = tokens.shape[0]
    half_taps = TAPS // 2
    inverse_in = lax.rsqrt(lax.optimization_barrier(jnp.mean(tokens * tokens, axis=-1, keepdims=True)) + EPSILON)
    normed = low(tokens * inverse_in * norm_gain)
    projected = low_back(jnp.dot(normed, in_weight, precision=HIGHEST))
    gate_in = projected[:, :E]
    conv_in = low(projected[:, E:E + CHANNELS])
    step_raw = projected[:, E + CHANNELS:].reshape(length, 2, HEADS)
    padded = jnp.pad(conv_in, ((half_taps, half_taps), (0, 0)))
    pre_act = conv_bias + sum((conv_weight[offset] * padded[offset:offset + length] for offset in range(TAPS)))
    activated = jax.nn.silu(pre_act)
    inner_values = activated[:, :E]
    state_maps = low(activated[:, E:])
    step_sizes = jax.nn.softplus(step_raw + head_params[0])
    decay_logs = -jnp.exp(head_params[1]) * step_sizes
    rate_table = low(low_back(jnp.transpose(jnp.concatenate([step_sizes, decay_logs], axis=1), (0, 2, 1))))
    inner_low = low(low_back(inner_values))
    mixed = low(low_back(mixer(inner_low.reshape(length, HEADS, HDIM), rate_table, state_maps)))
    skip_row = jnp.repeat(head_params[2], HDIM)
    combined = mixed.reshape(length, E) + skip_row * inner_values
    gated_pre = combined * jax.nn.silu(gate_in)
    inverse_out = lax.rsqrt(lax.optimization_barrier(jnp.mean(gated_pre * gated_pre, axis=-1, keepdims=True)) + EPSILON)
    gated = low(gated_pre * inverse_out * out_gain)
    return tokens + jnp.dot(gated, out_weight, precision=HIGHEST)

def forward(tokens_all, norm_gain, in_weight, conv_weight, conv_bias, head_params, out_gain, out_weight):
    checked = jax.checkpoint(one_seq)

    def per_sequence(tokens):
        return checked(tokens, norm_gain, in_weight, conv_weight, conv_bias, head_params, out_gain, out_weight)
    return lax.map(per_sequence, tokens_all)

def reference(layer_in, norm_gain, in_weight, conv_weight, conv_bias, head_params, out_gain, out_weight, out_cotangent):
    result, pullback = jax.vjp(forward, layer_in.astype(jnp.float32), norm_gain.astype(jnp.float32), in_weight.astype(jnp.float32), conv_weight.astype(jnp.float32), conv_bias.astype(jnp.float32), head_params.astype(jnp.float32), out_gain.astype(jnp.float32), out_weight.astype(jnp.float32))
    grads = pullback(out_cotangent.astype(jnp.float32))
    return (result.astype(jnp.bfloat16), grads[0], grads[1], grads[2], grads[3], grads[4], grads[5], grads[6], grads[7])
```

```python
import functools

import jax
import jax.numpy as jnp
from jax import lax
from jax.experimental import pallas as pl
from jax.experimental.pallas import tpu as pltpu
from jax.sharding import PartitionSpec as P

HEADS = 24
HDIM = 64
STATE = 64
STRETCH = 128
TAPS = 7
E = 1536
CHANNELS = 1792
PAIRS = HEADS // 2
LANES = 128
WIDE = 1920
EDGE = 8
EPSILON = 1e-05
LOG2E = 1.4426950408889634

F32 = jnp.float32
BF16 = jnp.bfloat16
NT = (((1,), (1,)), ((), ()))
TN = (((0,), (0,)), ((), ()))


def dot(a, b):
    return jnp.dot(a, b, preferred_element_type=F32)


def dot_nt(a, b):
    return lax.dot_general(a, b, NT, preferred_element_type=F32)


def params(limit=56):
    return pltpu.CompilerParams(vmem_limit_bytes=limit << 20)


def cost(flops, moved, trans=0):
    return pl.CostEstimate(flops=int(flops), bytes_accessed=int(moved), transcendentals=int(trans))


def whole(shape):
    return pl.BlockSpec(shape, lambda *_: (0,) * len(shape))


def swap(x, axis, q):
    n = lax.axis_size(axis)
    return lax.ppermute(x, axis, [(i, i ^ q) for i in range(n)])


def gather_z(x):
    return jnp.stack([x] + [swap(x, "wt", 2 * q) for q in range(1, lax.axis_size("wt") // 2)])


def gather_seq(x):
    return jnp.stack([x] + [swap(x, "seq", q) for q in range(1, lax.axis_size("seq"))])


def gather_core(x):
    return jnp.stack([x, swap(x, "wt", 1)], axis=2)


def scatter_sum(g):
    low = lambda t: t.astype(BF16)
    up = lambda t: t.astype(F32)
    a = up(g[:, :, 0]) + up(swap(low(g[:, :, 1]), "wt", 1))
    b = a[0]
    got = [swap(low(a[q]), "seq", q) for q in range(1, a.shape[0])]
    for t in got:
        b = b + up(t)
    c = b[0]
    got = [swap(low(b[q]), "wt", 2 * q) for q in range(1, b.shape[0])]
    for t in got:
        c = c + up(t)
    return c


def tree_sum(parts):
    while len(parts) > 1:
        parts = [parts[i] + parts[i + 1] for i in range(0, len(parts), 2)]
    return parts[0]


def sum_everywhere(x):
    ns, nw = lax.axis_size("seq"), lax.axis_size("wt")
    x = tree_sum([x] + [swap(x, "seq", q) for q in range(1, ns)])
    x = tree_sum([x] + [swap(x, "wt", 2 * q) for q in range(1, nw // 2)])
    return x + swap(x, "wt", 1)


def reorder_kernel(me_ref, x_ref, o_ref):
    for p in range(x_ref.shape[0]):
        o_ref[p] = x_ref[jnp.bitwise_xor(me_ref[0], p)]


def reorder(me, x):
    return pl.pallas_call(
        reorder_kernel,
        grid=(1,),
        out_shape=jax.ShapeDtypeStruct(x.shape, x.dtype),
        in_specs=[pl.BlockSpec(memory_space=pltpu.SMEM), whole(x.shape)],
        out_specs=whole(x.shape),
        compiler_params=params(),
        cost_estimate=cost(0, 4 * x.size),
        name="reorder",
    )(me, x)


def conv_kernel(nx_ref, w_ref, taps_ref, conv_ref, act_ref, slope_ref, dt_ref, pad_ref):
    j = pl.program_id(0)
    length = act_ref.shape[0]
    r = dot(nx_ref[...], w_ref[...])

    @pl.when(j == CHANNELS // LANES)
    def _():
        dt_ref[...] = r[:length]

    @pl.when(j < CHANNELS // LANES)
    def _():
        low = r.astype(BF16)
        conv_ref[...] = low
        f = low.astype(F32)
        pad_ref[EDGE : EDGE + length] = f[:length]
        pad_ref[0:EDGE] = f[length : length + EDGE]
        pad_ref[EDGE + length :] = f[length + EDGE :]
        step = 128
        for c in range(length // step):
            pre = jnp.broadcast_to(taps_ref[TAPS : TAPS + 1, :], (step, LANES))
            for k in range(TAPS):
                start = c * step + k + EDGE - TAPS // 2
                pre = pre + taps_ref[k : k + 1, :] * pad_ref[start : start + step]
            sig = jax.nn.sigmoid(pre)
            rows = slice(c * step, (c + 1) * step)
            act_ref[rows] = (pre * sig).astype(BF16)
            slope_ref[rows] = (sig * (1.0 + pre * (1.0 - sig))).astype(BF16)


def conv_forward(normed, weight, taps):
    ext, d = normed.shape
    length = ext - 2 * EDGE
    blocks = CHANNELS // LANES
    last = blocks - 1
    col = lambda j: (0, jnp.minimum(j, last))
    return pl.pallas_call(
        conv_kernel,
        grid=(blocks + 1,),
        in_specs=[
            whole((ext, d)),
            pl.BlockSpec((d, LANES), lambda j: (0, j)),
            pl.BlockSpec((8, LANES), col),
        ],
        out_specs=[
            pl.BlockSpec((ext, LANES), col),
            pl.BlockSpec((length, LANES), col),
            pl.BlockSpec((length, LANES), col),
            whole((length, LANES)),
        ],
        out_shape=[
            jax.ShapeDtypeStruct((ext, CHANNELS), BF16),
            jax.ShapeDtypeStruct((length, CHANNELS), BF16),
            jax.ShapeDtypeStruct((length, CHANNELS), BF16),
            jax.ShapeDtypeStruct((length, LANES), F32),
        ],
        scratch_shapes=[pltpu.VMEM((ext, LANES), F32)],
        compiler_params=params(),
        cost_estimate=cost(2 * ext * d * WIDE, 16 << 20),
        name="conv_forward",
    )(normed, weight, taps)


def iota(shape, dim):
    return lax.broadcasted_iota(jnp.int32, shape, dim)


def fill_expand(exp_ref):
    for c in range(2 * E // LANES):
        row = jnp.bitwise_and(iota((2 * LANES, LANES), 0), LANES - 1)
        lane = iota((2 * LANES, LANES), 1)
        head = 2 * c + jnp.where(lane >= HDIM, 1, 0)
        exp_ref[:, c * LANES : (c + 1) * LANES] = jnp.where(row == head, 1.0, 0.0).astype(BF16)


def two_parts(x):
    hi = x.astype(BF16)
    lo = (x - hi.astype(F32)).astype(BF16)
    return jnp.concatenate([hi, lo], axis=1)


def spread(parts, exp_ref, chunk):
    return dot(parts, exp_ref[:, chunk * LANES : (chunk + 1) * LANES])


def spread_rows(row, exp_ref):
    both = dot(two_parts(row), exp_ref[...])
    return both[:, :E], both[:, E:]


def step_sizes(dtraw, hp_ref):
    lane = iota(dtraw.shape, 1)
    pre = jnp.where(lane < 2 * HEADS, dtraw + hp_ref[0:1, :], 0.0)
    dt = jnp.maximum(pre, 0.0) + jnp.log1p(jnp.exp(-jnp.abs(pre)))
    return pre, dt, hp_ref[1:2, :] * dt


def states_kernel(
    act_ref, dtraw_ref, hp_ref, u_ref, v_ref, ut_ref, vt_ref, eu_ref, wv_ref, tot_ref, s_ref, pay_ref,
    exp_ref, dev_ref, cum_ref,
):
    b = pl.program_id(0)
    nb = pl.num_programs(0)

    @pl.when(b == 0)
    def _():
        fill_expand(exp_ref)
        dev_ref[...] = jnp.zeros_like(dev_ref)
        cum_ref[...] = jnp.zeros_like(cum_ref)

    sq = (STRETCH, LANES)
    lane = iota(sq, 1)
    forward = lane < HEADS
    _, dt, lg = step_sizes(dtraw_ref[...], hp_ref)
    dtb = dt.astype(BF16).astype(F32)
    lgb = lg.astype(BF16)
    upto = jnp.where(iota(sq, 0) >= iota(sq, 1), 1.0, 0.0).astype(BF16)
    run = dot(upto, lgb)
    before = run - lgb.astype(F32)
    total = run[STRETCH - 1 : STRETCH, :] * LOG2E
    logdt = jnp.where(dtb > 0.0, jnp.log(jnp.where(dtb > 0.0, dtb, 1.0)) * LOG2E, -1e30)
    u = jnp.where(forward, before, -run) * LOG2E
    v = jnp.where(forward, -run, before) * LOG2E + logdt
    u_ref[...] = u
    v_ref[...] = v
    ut_ref[0] = u.T
    vt_ref[0] = v.T
    eu = jnp.exp2(u + jnp.where(forward, 0.0, total))
    wv = jnp.exp2(v + jnp.where(forward, total, 0.0))
    eu_ref[...] = eu
    wv_ref[...] = wv
    total8 = jnp.broadcast_to(total, (8, LANES))
    tot_ref[0] = total8

    bt = act_ref[:, E : E + LANES].T
    w2 = two_parts(wv)
    dec_f, _ = spread_rows(jnp.exp2(total8), exp_ref)
    _, pre_r = spread_rows(jnp.exp2(cum_ref[...]), exp_ref)
    for p in range(PAIRS):
        cols = slice(p * LANES, (p + 1) * LANES)
        x = act_ref[:, cols].astype(F32)
        zf = (x * spread(w2, exp_ref, p)).astype(BF16)
        zr = (x * spread(w2, exp_ref, PAIRS + p)).astype(BF16)
        sf = dot(bt[:STATE], zf)
        sr = dot(bt[STATE:], zr)
        s_ref[0, :STATE, cols] = sf.astype(BF16)
        s_ref[0, STATE:, cols] = sr.astype(BF16)
        dev_ref[:STATE, cols] = dec_f[0:1, cols] * dev_ref[:STATE, cols] + sf
        dev_ref[STATE:, cols] = dev_ref[STATE:, cols] + pre_r[0:1, cols] * sr
    cum_ref[...] = cum_ref[...] + total8

    @pl.when(b == nb - 1)
    def _():
        write_payload(pay_ref, dev_ref, cum_ref, exp_ref)


def write_payload(pay_ref, dev_ref, cum_ref, exp_ref):
    cum_f, cum_r = spread_rows(cum_ref[...], exp_ref)
    pay_ref[0, :STATE] = dev_ref[:STATE].astype(BF16)
    pay_ref[1, :STATE] = dev_ref[STATE:].astype(BF16)
    pay_ref[0, STATE:] = jnp.concatenate([cum_f, cum_f], axis=0).astype(BF16)
    pay_ref[1, STATE:] = jnp.concatenate([cum_r, cum_r], axis=0).astype(BF16)


PAY = STATE + 16


def block_states(act, dtraw, hp):
    length = act.shape[0]
    nb = length // STRETCH
    sq = pl.BlockSpec((STRETCH, LANES), lambda b: (b, 0))
    cube = pl.BlockSpec((1, STRETCH, LANES), lambda b: (b, 0, 0))
    flat = jax.ShapeDtypeStruct((length, LANES), F32)
    deep = jax.ShapeDtypeStruct((nb, LANES, STRETCH), F32)
    return pl.pallas_call(
        states_kernel,
        grid=(nb,),
        in_specs=[pl.BlockSpec((STRETCH, CHANNELS), lambda b: (b, 0)), sq, whole((8, LANES))],
        out_specs=[
            sq, sq, cube, cube, sq, sq,
            pl.BlockSpec((1, 8, LANES), lambda b: (b, 0, 0)),
            pl.BlockSpec((1, 2 * STATE, E), lambda b: (b, 0, 0)),
            whole((2, PAY, E)),
        ],
        out_shape=[
            flat, flat, deep, deep, flat, flat,
            jax.ShapeDtypeStruct((nb, 8, LANES), F32),
            jax.ShapeDtypeStruct((nb, 2 * STATE, E), BF16),
            jax.ShapeDtypeStruct((2, PAY, E), BF16),
        ],
        scratch_shapes=[
            pltpu.VMEM((2 * LANES, 2 * E), BF16),
            pltpu.VMEM((2 * STATE, E), F32),
            pltpu.VMEM((8, LANES), F32),
        ],
        compiler_params=params(),
        cost_estimate=cost(4e9, 12 << 20),
        name="block_states",
    )(act, dtraw, hp)


def intra_kernel(act_ref, u_ref, vt_ref, y_ref):
    sq = (STRETCH, STRETCH)
    i, j = iota(sq, 0), iota(sq, 1)
    after, at = i > j, i >= j
    bm = act_ref[:, E : E + LANES]
    cm = act_ref[:, E + LANES :]
    gf = dot_nt(cm[:, :STATE], bm[:, :STATE])
    gr = dot_nt(cm[:, STATE:], bm[:, STATE:])
    gram = jnp.where(after, gf, jnp.where(at, 0.0, gr))
    left = iota((STRETCH, LANES), 1) < HDIM
    for p in range(PAIRS):
        cols = slice(p * LANES, (p + 1) * LANES)
        mats = []
        for h in (2 * p, 2 * p + 1):
            r = HEADS + h
            row = jnp.where(at, u_ref[:, h : h + 1], u_ref[:, r : r + 1])
            col = jnp.where(after, vt_ref[0, h : h + 1, :], vt_ref[0, r : r + 1, :])
            mats.append((jnp.exp2(row + col) * gram).astype(BF16))
        y = dot(jnp.concatenate(mats, axis=0), act_ref[:, cols])
        y_ref[:, cols] = jnp.where(left, y[:STRETCH], y[STRETCH:])


def intra(act, u, vt):
    length = act.shape[0]
    return pl.pallas_call(
        intra_kernel,
        grid=(length // STRETCH,),
        in_specs=[
            pl.BlockSpec((STRETCH, CHANNELS), lambda b: (b, 0)),
            pl.BlockSpec((STRETCH, LANES), lambda b: (b, 0)),
            pl.BlockSpec((1, LANES, STRETCH), lambda b: (b, 0, 0)),
        ],
        out_specs=pl.BlockSpec((STRETCH, E), lambda b: (b, 0)),
        out_shape=jax.ShapeDtypeStruct((length, E), F32),
        compiler_params=params(),
        cost_estimate=cost(8e9, 12 << 20),
        name="intra",
    )(act, u, vt)


def from_others(me, got_ref, upward):
    n = got_ref.shape[0] + 1
    side = lambda d: (d < me) if upward else (d > me)
    total = jnp.zeros((STATE, E), F32)
    for q in range(1, n):
        d = jnp.bitwise_xor(me, q)
        log = jnp.zeros((1, E), F32)
        for k in range(1, n):
            if k != q:
                e = jnp.bitwise_xor(me, k)
                between = ((d < e) & (e < me)) if upward else ((me < e) & (e < d))
                row = got_ref[k - 1, STATE : STATE + 1, :].astype(F32)
                log = log + jnp.where(between, row, 0.0)
        term = jnp.exp2(log) * got_ref[q - 1, :STATE, :].astype(F32)
        total = total + jnp.where(side(d), term, 0.0)
    return total


def gate_kernel(
    me_ref, y_ref, act_ref, z_ref, dg_ref, eu_ref, s_ref, got_ref, tot_ref, rows_ref,
    gated_ref, dz_ref, dy_ref, ent_ref, p_ref, pay_ref, sums_ref,
    exp_ref, dev_ref, cum_ref, yv_ref, ef_ref, er_ref,
):
    b = pl.program_id(0)
    nb = pl.num_programs(0)

    @pl.when(b == 0)
    def _():
        fill_expand(exp_ref)
        dev_ref[...] = jnp.zeros_like(dev_ref)
        cum_ref[...] = jnp.zeros_like(cum_ref)
        sums_ref[...] = jnp.zeros_like(sums_ref)
        me = me_ref[0]
        state = from_others(me, got_ref, True)
        for c in range(s_ref.shape[0]):
            ent_ref[c, :STATE] = state.astype(BF16)
            dec, _ = spread_rows(jnp.exp2(tot_ref[c]), exp_ref)
            state = dec[0:1] * state + s_ref[c, :STATE].astype(F32)
        state = from_others(me, got_ref, False)
        for c in reversed(range(s_ref.shape[0])):
            ent_ref[c, STATE:] = state.astype(BF16)
            _, dec = spread_rows(jnp.exp2(tot_ref[c]), exp_ref)
            state = dec[0:1] * state + s_ref[c, STATE:].astype(F32)

    cm = act_ref[:, E + LANES :]
    e2 = two_parts(eu_ref[...])
    square = jnp.zeros((STRETCH, LANES), F32)
    cross = jnp.zeros((STRETCH, LANES), F32)
    for p in range(PAIRS):
        cols = slice(p * LANES, (p + 1) * LANES)
        ef = spread(e2, exp_ref, p)
        er = spread(e2, exp_ref, PAIRS + p)
        ef_ref[:, cols] = ef
        er_ref[:, cols] = er
        mixed = y_ref[:, cols] + ef * dot(cm[:, :STATE], ent_ref[b, :STATE, cols])
        mixed = mixed + er * dot(cm[:, STATE:], ent_ref[b, STATE:, cols])
        mixed = mixed.astype(BF16).astype(F32)
        yv = mixed + rows_ref[0:1, cols] * act_ref[:, cols].astype(F32)
        yv_ref[:, cols] = yv
        z = z_ref[:, cols].astype(F32)
        yg = yv * (z * jax.nn.sigmoid(z))
        square = square + yg * yg
        cross = cross + rows_ref[1:2, cols] * dg_ref[:, cols].astype(F32) * yg
    inv = lax.rsqrt(jnp.sum(square, axis=1, keepdims=True) / E + EPSILON)
    back = inv * inv * inv * (jnp.sum(cross, axis=1, keepdims=True) / E)

    total8 = tot_ref[b]
    _, dec_r = spread_rows(jnp.exp2(total8), exp_ref)
    pre_f, _ = spread_rows(jnp.exp2(cum_ref[...]), exp_ref)
    ct = cm.T
    for p in range(PAIRS):
        cols = slice(p * LANES, (p + 1) * LANES)
        z = z_ref[:, cols].astype(F32)
        sig = jax.nn.sigmoid(z)
        ga = z * sig
        yv = yv_ref[:, cols]
        yg = yv * ga
        normed = yg * inv
        dg = dg_ref[:, cols].astype(F32)
        gated_ref[:, cols] = (normed * rows_ref[1:2, cols]).astype(BF16)
        dyg = inv * (rows_ref[1:2, cols] * dg) - yg * back
        dy = dyg * ga
        dz_ref[:, cols] = (dyg * yv * sig * (1.0 + z * (1.0 - sig))).astype(BF16)
        low = dy.astype(BF16)
        dy_ref[:, cols] = low
        fold = lambda t: jnp.sum(t.reshape(STRETCH // 8, 8, LANES), axis=0)
        sums_ref[0:8, cols] = sums_ref[0:8, cols] + fold(dg * normed)
        sums_ref[8:16, cols] = sums_ref[8:16, cols] + fold(dy * act_ref[:, cols].astype(F32))
        low = low.astype(F32)
        pf = dot(ct[:STATE], (ef_ref[:, cols] * low).astype(BF16))
        pr = dot(ct[STATE:], (er_ref[:, cols] * low).astype(BF16))
        p_ref[0, :STATE, cols] = pf.astype(BF16)
        p_ref[0, STATE:, cols] = pr.astype(BF16)
        dev_ref[:STATE, cols] = dev_ref[:STATE, cols] + pre_f[0:1, cols] * pf
        dev_ref[STATE:, cols] = dec_r[0:1, cols] * dev_ref[STATE:, cols] + pr
    cum_ref[...] = cum_ref[...] + total8

    @pl.when(b == nb - 1)
    def _():
        write_payload(pay_ref, dev_ref, cum_ref, exp_ref)


def gate(me, y, act, z, dg, eu, s, got, tot, rows):
    length = act.shape[0]
    nb = length // STRETCH
    line = pl.BlockSpec((STRETCH, E), lambda b: (b, 0))
    return pl.pallas_call(
        gate_kernel,
        grid=(nb,),
        in_specs=[
            pl.BlockSpec(memory_space=pltpu.SMEM),
            line,
            pl.BlockSpec((STRETCH, CHANNELS), lambda b: (b, 0)),
            line,
            line,
            pl.BlockSpec((STRETCH, LANES), lambda b: (b, 0)),
            whole(s.shape),
            whole(got.shape),
            whole(tot.shape),
            whole((8, E)),
        ],
        out_specs=[
            line,
            line,
            line,
            whole(s.shape),
            pl.BlockSpec((1, 2 * STATE, E), lambda b: (b, 0, 0)),
            whole((2, PAY, E)),
            whole((16, E)),
        ],
        out_shape=[
            jax.ShapeDtypeStruct((length, E), BF16),
            jax.ShapeDtypeStruct((length, E), BF16),
            jax.ShapeDtypeStruct((length, E), BF16),
            jax.ShapeDtypeStruct(s.shape, BF16),
            jax.ShapeDtypeStruct(s.shape, BF16),
            jax.ShapeDtypeStruct((2, PAY, E), BF16),
            jax.ShapeDtypeStruct((16, E), F32),
        ],
        scratch_shapes=[
            pltpu.VMEM((2 * LANES, 2 * E), BF16),
            pltpu.VMEM((2 * STATE, E), F32),
            pltpu.VMEM((8, LANES), F32),
            pltpu.VMEM((STRETCH, E), F32),
            pltpu.VMEM((STRETCH, E), F32),
            pltpu.VMEM((STRETCH, E), F32),
        ],
        compiler_params=params(),
        cost_estimate=cost(8e9, 32 << 20),
        name="gate",
    )(me, y, act, z, dg, eu, s, got, tot, rows)


def mixer_back_kernel(
    me_ref, act_ref, dy_ref, v_ref, ut_ref, eu_ref, wv_ref, ent_ref, p_ref, got_ref, tot_ref, dtraw_ref, hp_ref,
    dx_ref, dmap_ref, ddt_ref, sums_ref,
    exp_ref, head_ref, out_ref, mask_ref, cs_ref, dmt_ref,
):
    b = pl.program_id(0)
    sq = (STRETCH, STRETCH)
    j, i = iota(sq, 0), iota(sq, 1)
    after, at = i > j, i >= j

    @pl.when(b == 0)
    def _():
        fill_expand(exp_ref)
        sums_ref[...] = jnp.zeros_like(sums_ref)
        cs_ref[...] = jnp.zeros_like(cs_ref)
        mask_ref[...] = jnp.where(after, 1.0, 0.0).astype(BF16)
        for c in range(PAIRS):
            row = iota((2 * LANES, LANES), 0)
            lane = iota((2 * LANES, LANES), 1)
            which = jnp.where(row >= LANES, HEADS, 0) + 2 * c
            which = which + jnp.where(jnp.bitwise_and(row, LANES - 1) >= HDIM, 1, 0)
            head_ref[c] = jnp.where(lane == which, 1.0, 0.0).astype(BF16)
        me = me_ref[0]
        state = from_others(me, got_ref, False)
        for c in reversed(range(p_ref.shape[0])):
            out_ref[c, :STATE] = state.astype(BF16)
            dec, _ = spread_rows(jnp.exp2(tot_ref[c]), exp_ref)
            state = dec[0:1] * state + p_ref[c, :STATE].astype(F32)
        state = from_others(me, got_ref, True)
        for c in range(p_ref.shape[0]):
            out_ref[c, STATE:] = state.astype(BF16)
            _, dec = spread_rows(jnp.exp2(tot_ref[c]), exp_ref)
            state = dec[0:1] * state + p_ref[c, STATE:].astype(F32)

    bm = act_ref[:, E : E + LANES]
    cm = act_ref[:, E + LANES :]
    bf, br, cf, cr = bm[:, :STATE], bm[:, STATE:], cm[:, :STATE], cm[:, STATE:]
    gram = jnp.where(after, dot_nt(bf, cf), jnp.where(at, 0.0, dot_nt(br, cr)))
    e2 = two_parts(eu_ref[...])
    w2 = two_parts(wv_ref[...])
    left = iota((STRETCH, LANES), 1) < HDIM
    ones = jnp.full((8, STRETCH), 1.0, BF16)
    mask = mask_ref[...]
    dmt_ref[...] = jnp.zeros_like(dmt_ref)
    dgram = jnp.zeros(sq, F32)
    col_r = jnp.zeros((STRETCH, LANES), F32)
    col_q = jnp.zeros((STRETCH, LANES), F32)
    carry = jnp.zeros((8, LANES), F32)
    for p in range(PAIRS):
        cols = slice(p * LANES, (p + 1) * LANES)
        xb = act_ref[:, cols]
        dyb = dy_ref[:, cols]
        x = xb.astype(F32)
        dy = dyb.astype(F32)
        x0 = jnp.where(left, x, 0.0).astype(BF16)
        x1 = jnp.where(left, 0.0, x).astype(BF16)
        dm = dot_nt(jnp.concatenate([x0, x1], axis=0), dyb)
        mats = []
        for k, h in enumerate((2 * p, 2 * p + 1)):
            r = HEADS + h
            row = jnp.where(after, v_ref[:, h : h + 1], v_ref[:, r : r + 1])
            col = jnp.where(at, ut_ref[0, h : h + 1, :], ut_ref[0, r : r + 1, :])
            decay = jnp.exp2(row + col)
            mats.append((decay * gram).astype(BF16))
            da = dm[k * STRETCH : (k + 1) * STRETCH] * decay
            dgram = dgram + da
            t = (da * gram).astype(BF16)
            tf = t * mask
            cs = dot(ones, jnp.concatenate([t, tf], axis=1))
            rs = dot_nt(ones, jnp.concatenate([t, tf], axis=0))
            cs_ref[h : h + 1, :] = cs[0:1]
            cs_ref[64 + h : 65 + h, :] = rs[0:1]
        dx2 = dot(jnp.concatenate(mats, axis=0), dyb)
        dx = jnp.where(left, dx2[:STRETCH], dx2[STRETCH:])

        wf = spread(w2, exp_ref, p)
        wr = spread(w2, exp_ref, PAIRS + p)
        ef = spread(e2, exp_ref, p)
        er = spread(e2, exp_ref, PAIRS + p)
        pf, pr = out_ref[b, :STATE, cols], out_ref[b, STATE:, cols]
        sf, sr = ent_ref[0, :STATE, cols], ent_ref[0, STATE:, cols]
        vf = wf * dot(bf, pf)
        vr = wr * dot(br, pr)
        dx_ref[:, cols] = (dx + vf + vr).astype(BF16)
        dyf = ef * dy
        dyr = er * dy
        heads = head_ref[p]
        col_r = col_r + dot(jnp.concatenate([vf * x, vr * x], axis=1).astype(BF16), heads)
        qf = dyf * dot(cf, sf)
        qr = dyr * dot(cr, sr)
        col_q = col_q + dot(jnp.concatenate([qf, qr], axis=1).astype(BF16), heads)
        xf = (wf * x).astype(BF16)
        xr = (wr * x).astype(BF16)
        dmt_ref[:STATE] = dmt_ref[:STATE] + dot_nt(pf, xf)
        dmt_ref[STATE : 2 * STATE] = dmt_ref[STATE : 2 * STATE] + dot_nt(pr, xr)
        dmt_ref[2 * STATE : 3 * STATE] = dmt_ref[2 * STATE : 3 * STATE] + dot_nt(sf, dyf.astype(BF16))
        dmt_ref[3 * STATE :] = dmt_ref[3 * STATE :] + dot_nt(sr, dyr.astype(BF16))
        fold = lambda t: jnp.sum(t.reshape(STATE // 8, 8, LANES), axis=0)
        pair = jnp.concatenate(
            [fold(pf.astype(F32) * sf.astype(F32)), fold(pr.astype(F32) * sr.astype(F32))], axis=1
        )
        carry = carry + dot(pair.astype(BF16), heads)

    gfwd = jnp.where(after, dgram, 0.0).astype(BF16)
    grev = jnp.where(at, 0.0, dgram).astype(BF16)
    bt, ct = bm.T, cm.T
    db_f = dmt_ref[:STATE] + dot_nt(ct[:STATE], gfwd)
    db_r = dmt_ref[STATE : 2 * STATE] + dot_nt(ct[STATE:], grev)
    dc_f = dmt_ref[2 * STATE : 3 * STATE] + dot(bt[:STATE], gfwd)
    dc_r = dmt_ref[3 * STATE :] + dot(bt[STATE:], grev)
    dmap_ref[:, :LANES] = jnp.concatenate([db_f, db_r], axis=0).T
    dmap_ref[:, LANES:] = jnp.concatenate([dc_f, dc_r], axis=0).T

    both = cs_ref[...]
    tot, fwd = both[:, :LANES], both[:, LANES:]
    rev = tot - fwd
    pad = jnp.zeros((LANES - 2 * HEADS, LANES), F32)
    cs = jnp.concatenate([fwd[:HEADS], rev[:HEADS], pad], axis=0).T
    rs = jnp.concatenate([fwd[64 : 64 + HEADS], rev[64 : 64 + HEADS], pad], axis=0).T
    lane = iota((STRETCH, LANES), 1)
    forward = lane < HEADS
    later = jnp.where(after, 1.0, 0.0)
    earlier = jnp.where(at, 0.0, 1.0)
    later_at = jnp.where(at, 1.0, 0.0)
    earlier_at = jnp.where(after, 0.0, 1.0)
    exact = functools.partial(jnp.dot, precision=lax.Precision.HIGHEST, preferred_element_type=F32)
    gain = cs + col_q
    dlg_f = exact(later, gain) - exact(later_at, rs) + exact(earlier, col_r)
    dlg_r = exact(earlier, gain) - exact(earlier_at, rs) + exact(later, col_r)
    dlg = jnp.where(forward, dlg_f, dlg_r)
    dlg = dlg + jnp.exp2(tot_ref[b])[0:1] * jnp.sum(carry, axis=0, keepdims=True)
    pre, dt, lg = step_sizes(dtraw_ref[...], hp_ref)
    dtb = dt.astype(BF16).astype(F32)
    ok = (dtb > 0.0) & (lane < 2 * HEADS)
    ddt = jnp.where(ok, (rs + col_r) / jnp.where(ok, dtb, 1.0), 0.0)
    ddt = ddt.astype(BF16).astype(F32)
    dlg = jnp.where(lane < 2 * HEADS, dlg, 0.0).astype(BF16).astype(F32)
    draw = (ddt + dlg * hp_ref[1:2, :]) * jax.nn.sigmoid(pre)
    ddt_ref[...] = draw.astype(BF16)
    fold = lambda t: jnp.sum(t.reshape(STRETCH // 8, 8, LANES), axis=0)
    sums_ref[0:8] = sums_ref[0:8] + fold(draw)
    sums_ref[8:16] = sums_ref[8:16] + fold(dlg * lg)


def mixer_back(me, act, dy, v, ut, eu, wv, ent, p, got, tot, dtraw, hp):
    length = act.shape[0]
    nb = length // STRETCH
    sq = pl.BlockSpec((STRETCH, LANES), lambda b: (b, 0))
    line = pl.BlockSpec((STRETCH, E), lambda b: (b, 0))
    cube = pl.BlockSpec((1, LANES, STRETCH), lambda b: (b, 0, 0))
    return pl.pallas_call(
        mixer_back_kernel,
        grid=(nb,),
        in_specs=[
            pl.BlockSpec(memory_space=pltpu.SMEM),
            pl.BlockSpec((STRETCH, CHANNELS), lambda b: (b, 0)),
            line,
            sq,
            cube,
            sq,
            sq,
            pl.BlockSpec((1, 2 * STATE, E), lambda b: (b, 0, 0)),
            whole(p.shape),
            whole(got.shape),
            whole(tot.shape),
            sq,
            whole((8, LANES)),
        ],
        out_specs=[
            line,
            pl.BlockSpec((STRETCH, 2 * LANES), lambda b: (b, 0)),
            sq,
            whole((16, LANES)),
        ],
        out_shape=[
            jax.ShapeDtypeStruct((length, E), BF16),
            jax.ShapeDtypeStruct((length, 2 * LANES), F32),
            jax.ShapeDtypeStruct((length, LANES), BF16),
            jax.ShapeDtypeStruct((16, LANES), F32),
        ],
        scratch_shapes=[
            pltpu.VMEM((2 * LANES, 2 * E), BF16),
            pltpu.VMEM((PAIRS, 2 * LANES, LANES), BF16),
            pltpu.VMEM(p.shape, BF16),
            pltpu.VMEM((STRETCH, STRETCH), BF16),
            pltpu.VMEM((LANES, 2 * LANES), F32),
            pltpu.VMEM((4 * STATE, STRETCH), F32),
        ],
        compiler_params=params(),
        cost_estimate=cost(16e9, 20 << 20),
        name="mixer_back",
    )(me, act, dy, v, ut, eu, wv, ent, p, got, tot, dtraw, hp)


def conv_back_kernel(
    dx_ref, dy_ref, dmap_ref, slope_ref, conv_ref, taps_ref, skip_ref, dconv_ref, sums_ref, dact_ref, dpad_ref, pad_ref
):
    j = pl.program_id(0)
    length = slope_ref.shape[0]

    @pl.when(j < PAIRS)
    def _():
        dact_ref[...] = dx_ref[...].astype(F32) + skip_ref[0:1, :] * dy_ref[...].astype(F32)

    @pl.when(j >= PAIRS)
    def _():
        dact_ref[...] = dmap_ref[...]

    margin = 2 * EDGE
    dpad_ref[0:margin] = jnp.zeros((margin, LANES), F32)
    dpad_ref[margin + length :] = jnp.zeros((margin, LANES), F32)
    dpad_ref[margin : margin + length] = dact_ref[...] * slope_ref[...].astype(F32)
    pad_ref[EDGE : EDGE + length] = conv_ref[:length].astype(F32)
    pad_ref[0:EDGE] = conv_ref[length : length + EDGE].astype(F32)
    pad_ref[EDGE + length :] = conv_ref[length + EDGE :].astype(F32)
    half = TAPS // 2

    def spread_back(first, rows):
        out = jnp.zeros((rows, LANES), F32)
        for k in range(TAPS):
            start = margin + first - k + half
            out = out + taps_ref[k : k + 1, :] * dpad_ref[start : start + rows]
        return out.astype(BF16)

    step = 128
    sums = [jnp.zeros((8, LANES), F32) for _ in range(TAPS + 1)]
    for c in range(length // step):
        first = c * step
        dconv_ref[first : first + step] = spread_back(first, step)
        fold = lambda t: jnp.sum(t.reshape(step // 8, 8, LANES), axis=0)
        dpre = dpad_ref[margin + first : margin + first + step]
        for k in range(TAPS):
            start = first + k + EDGE - half
            sums[k] = sums[k] + fold(dpre * pad_ref[start : start + step])
        sums[TAPS] = sums[TAPS] + fold(dpre)
    edges = jnp.concatenate([spread_back(-EDGE, EDGE), spread_back(length, EDGE)], axis=0)
    dconv_ref[length:] = edges
    sums_ref[...] = jnp.concatenate([jnp.sum(t, axis=0, keepdims=True) for t in sums], axis=0)


def conv_back(dx, dy, dmap, slope, conv, taps, skip):
    ext = conv.shape[0]
    length = ext - 2 * EDGE
    early = lambda j: (0, jnp.minimum(j, PAIRS - 1))
    late = lambda j: (0, jnp.maximum(j - PAIRS, 0))
    col = lambda j: (0, j)
    return pl.pallas_call(
        conv_back_kernel,
        grid=(CHANNELS // LANES,),
        in_specs=[
            pl.BlockSpec((length, LANES), early),
            pl.BlockSpec((length, LANES), early),
            pl.BlockSpec((length, LANES), late),
            pl.BlockSpec((length, LANES), col),
            pl.BlockSpec((ext, LANES), col),
            pl.BlockSpec((8, LANES), col),
            pl.BlockSpec((8, LANES), early),
        ],
        out_specs=[pl.BlockSpec((ext, LANES), col), pl.BlockSpec((8, LANES), col)],
        out_shape=[
            jax.ShapeDtypeStruct((ext, CHANNELS), BF16),
            jax.ShapeDtypeStruct((8, CHANNELS), F32),
        ],
        scratch_shapes=[
            pltpu.VMEM((length, LANES), F32),
            pltpu.VMEM((length + 4 * EDGE, LANES), F32),
            pltpu.VMEM((ext, LANES), F32),
        ],
        compiler_params=params(),
        cost_estimate=cost(2e9, 20 << 20),
        name="conv_back",
    )(dx, dy, dmap, slope, conv, taps, skip)


def send_states(payload, to_later):
    n, me = lax.axis_size("seq"), lax.axis_index("seq")
    got = []
    for q in range(1, n):
        later = (me ^ q) > me
        first = later if to_later else ~later
        got.append(swap(jnp.where(first, payload[0], payload[1]), "seq", q))
    return jnp.stack(got)


def per_device(
    layer_in, norm_gain, in_weight, conv_weight, conv_bias, head_params, out_gain, out_weight, out_cotangent
):
    ns, nw = lax.axis_size("seq"), lax.axis_size("wt")
    ndev = ns * nw
    seq_me = lax.axis_index("seq").astype(jnp.int32)
    me = seq_me * nw + lax.axis_index("wt").astype(jnp.int32)
    me_arr, seq_arr = me.reshape(1), seq_me.reshape(1)
    tokens = layer_in[0]
    cotangent = out_cotangent[0]
    length, d = tokens.shape
    share = in_weight.shape[0]
    cshare = conv_bias.shape[0]
    gshare = out_gain.shape[0]
    spare = WIDE - (in_weight.shape[1] - E)

    small = jnp.concatenate([conv_weight.reshape(-1), conv_bias, out_gain, norm_gain])
    small = jnp.pad(small, (0, share * spare - small.shape[0])).reshape(share, spare)
    first = jnp.concatenate([in_weight[:, E:], small], axis=1)
    rest_z, rest_o = in_weight[:, :E], out_weight
    a1 = gather_z(first)
    a1, rest_z, rest_o = lax.optimization_barrier((a1, rest_z, rest_o))
    z1, o1 = gather_z(rest_z), gather_z(rest_o)
    a2 = gather_seq(a1)
    a2, z1, o1 = lax.optimization_barrier((a2, z1, o1))
    z2, o2 = gather_seq(z1), gather_seq(o1)
    w_first = gather_core(a2).reshape(d, WIDE)
    w_z = gather_core(z2).reshape(d, E)
    w_out = reorder(me_arr, gather_core(o2).reshape(ndev, gshare, d)).reshape(E, d)

    forward = [(i, i + 1) for i in range(ns - 1)]
    backward = [(i + 1, i) for i in range(ns - 1)]
    before = lax.ppermute(tokens[length - EDGE :], "seq", forward)
    behind = lax.ppermute(tokens[:EDGE], "seq", backward)
    ext = jnp.concatenate([tokens, before, behind], axis=0)
    blocks = jnp.arange(d, dtype=jnp.int32) // share
    natural = (blocks ^ me) * share + jnp.arange(d, dtype=jnp.int32) % share
    perm = (jnp.arange(d, dtype=jnp.int32)[:, None] == natural[None, :]).astype(BF16)
    u_x = dot(ext, perm)
    inv_in = lax.rsqrt(jnp.mean(jnp.square(ext.astype(F32)), axis=1, keepdims=True) + EPSILON)

    extras = w_first[:, WIDE - spare :].reshape(ndev, share * spare)
    n_small = (TAPS + 1) * cshare + gshare + share
    order = (jnp.arange(ndev, dtype=jnp.int32)[:, None] ^ me) == jnp.arange(ndev, dtype=jnp.int32)[None, :]
    nat = dot(order.astype(BF16), extras[:, :n_small])
    taps = jnp.transpose(nat[:, : TAPS * cshare].reshape(ndev, TAPS, cshare), (1, 0, 2)).reshape(TAPS, CHANNELS)
    bias = nat[:, TAPS * cshare : (TAPS + 1) * cshare].reshape(1, CHANNELS)
    taps = jnp.concatenate([taps, bias], axis=0)
    gain_out = nat[:, (TAPS + 1) * cshare : (TAPS + 1) * cshare + gshare].reshape(1, E)
    gain_x = extras[:, n_small - share : n_small].reshape(1, d).astype(F32)

    normed = (u_x * inv_in * gain_x).astype(BF16)
    conv, act, slope, dtraw = conv_forward(normed, w_first, taps)

    twice = jnp.concatenate([head_params, head_params], axis=1)
    rates = jnp.stack([twice[0], -jnp.exp(twice[1])])
    hp = jnp.pad(rates, ((0, 6), (0, LANES - 2 * HEADS)))
    u, v, ut, vt, eu, wv, tot, s, pay = block_states(act, dtraw, hp)
    got = send_states(pay, True)
    y = intra(act, u, vt)
    own = normed[:length]
    z = dot(own, w_z).astype(BF16)
    dgated = dot_nt(cotangent, w_out).astype(BF16)
    skip = jnp.repeat(head_params[2], HDIM)[None]
    rows = jnp.concatenate([skip, gain_out, jnp.zeros((6, E), F32)], axis=0)
    gated, dz, dy, ent, p, pay, sums = gate(seq_arr, y, act, z, dgated, eu, s, got, tot, rows)
    got = send_states(pay, False)

    layer_out = (tokens.astype(F32) + dot(gated, w_out)).astype(BF16)[None]
    g_out = lax.dot_general(gated, cotangent, TN, preferred_element_type=F32).astype(BF16)
    g_z = lax.dot_general(own, dz, TN, preferred_element_type=F32).astype(BF16)
    dn_z = dot_nt(dz, w_z)
    lead = (ns, nw // 2, 2)
    g_out = reorder(me_arr, g_out.reshape(ndev, gshare, d)).reshape(*lead, gshare, d)
    grad_out = scatter_sum(g_out)
    grad_z = scatter_sum(g_z.reshape(*lead, share, E))

    dx, dmap, ddt, hsums = mixer_back(seq_arr, act, dy, v, ut, eu, wv, ent, p, got, tot, dtraw, hp)
    dconv, csums = conv_back(dx, dy, dmap, slope, conv, taps, rows)

    hrow = jnp.sum(hsums.reshape(2, 8, LANES), axis=1)[:, : 2 * HEADS].reshape(2, 2, HEADS).sum(axis=1)
    skip_grad = jnp.sum(sums[8:].reshape(8, HEADS, HDIM), axis=(0, 2))
    head_grad = sum_everywhere(jnp.concatenate([hrow, skip_grad[None]], axis=0))

    g_c = lax.dot_general(normed, dconv, TN, preferred_element_type=F32)
    g_dt = lax.dot_general(own, ddt, TN, preferred_element_type=F32)
    dn_c = dot_nt(dconv, w_first[:, :CHANNELS])
    dn_dt = dot_nt(ddt[:, : 2 * HEADS], w_first[:, CHANNELS : CHANNELS + 2 * HEADS])
    mine = dn_z + dn_dt
    dn = dn_c + jnp.concatenate([mine, jnp.zeros((2 * EDGE, d), F32)], axis=0)
    gain_grad = jnp.sum(dn * u_x * inv_in, axis=0)
    og_grad = jnp.sum(sums[:8], axis=0)

    vectors = jnp.concatenate(
        [
            jnp.transpose(csums[:TAPS].reshape(TAPS, ndev, cshare), (1, 0, 2)).reshape(ndev, TAPS * cshare),
            csums[TAPS].reshape(ndev, cshare),
            og_grad.reshape(ndev, gshare),
        ],
        axis=1,
    )
    vectors = jnp.dot(order.astype(F32), vectors, precision=lax.Precision.HIGHEST)
    vectors = jnp.concatenate([vectors, gain_grad.reshape(ndev, share)], axis=1)
    vectors = jnp.pad(vectors, ((0, 0), (0, share * spare - n_small))).reshape(d, spare)
    g_first = jnp.concatenate([g_c, g_dt[:, : 2 * HEADS], vectors], axis=1)
    grad_first = scatter_sum(g_first.reshape(*lead, share, WIDE))

    dn_hi = dn.astype(BF16)
    dn_lo = (dn - dn_hi.astype(F32)).astype(BF16)
    dn = dot_nt(dn_hi, perm) + dot_nt(dn_lo, perm)
    prev_edge = lax.ppermute(dn[length : length + EDGE], "seq", backward)
    next_edge = lax.ppermute(dn[length + EDGE :], "seq", forward)
    middle = jnp.zeros((length - 2 * EDGE, d), F32)
    dn = dn[:length] + jnp.concatenate([next_edge, middle, prev_edge], axis=0)
    u, inv = tokens.astype(F32), inv_in[:length]
    scaled = nat[:, n_small - share :].reshape(1, d) * dn
    in_grad = cotangent.astype(F32) + inv * scaled
    in_grad = in_grad - u * inv**3 * jnp.mean(scaled * u, axis=1, keepdims=True)

    vec = grad_first[:, WIDE - spare :].reshape(-1)
    c0, c1, c2 = TAPS * cshare, (TAPS + 1) * cshare, (TAPS + 1) * cshare + gshare
    return (
        layer_out,
        in_grad[None],
        vec[c2 : c2 + share],
        jnp.concatenate([grad_z, grad_first[:, : WIDE - spare]], axis=1),
        vec[:c0].reshape(TAPS, cshare),
        vec[c0:c1],
        head_grad,
        vec[c1:c2],
        grad_out,
    )


def solution(mesh):
    rows = P(("seq", "wt"))
    table = P(("seq", "wt"), None)
    tokens = P("wt", "seq", None)
    taps = P(None, ("seq", "wt"))
    return jax.shard_map(
        per_device,
        mesh=mesh,
        in_specs=(tokens, rows, table, taps, rows, P(), rows, table, tokens),
        out_specs=(tokens, tokens, rows, table, taps, rows, P(), rows, table),
        check_vma=False,
    )
```

```python
import functools

import jax
import jax.numpy as jnp
from jax import lax
from jax.experimental import pallas as pl
from jax.experimental.pallas import tpu as pltpu
from jax.sharding import PartitionSpec as P

HEADS = 24
HDIM = 64
STATE = 64
STRETCH = 128
TAPS = 7
E = 1536
CHANNELS = 1792
PAIRS = HEADS // 2
LANES = 128
WIDE = 1920
EDGE = 8
EPSILON = 1e-05
LOG2E = 1.4426950408889634

F32 = jnp.float32
BF16 = jnp.bfloat16
NT = (((1,), (1,)), ((), ()))
TN = (((0,), (0,)), ((), ()))


def dot(a, b):
    return jnp.dot(a, b, preferred_element_type=F32)


def dot_nt(a, b):
    return lax.dot_general(a, b, NT, preferred_element_type=F32)


def params(limit=56):
    return pltpu.CompilerParams(vmem_limit_bytes=limit << 20)


def cost(flops, moved, trans=0):
    return pl.CostEstimate(flops=int(flops), bytes_accessed=int(moved), transcendentals=int(trans))


def whole(shape):
    return pl.BlockSpec(shape, lambda *_: (0,) * len(shape))


def swap(x, axis, q):
    n = lax.axis_size(axis)
    return lax.ppermute(x, axis, [(i, i ^ q) for i in range(n)])


def gather_z(x):
    return [x] + [swap(x, "wt", 2 * q) for q in range(1, lax.axis_size("wt") // 2)]


def gather_seq(x):
    return [x] + [swap(x, "seq", q) for q in range(1, lax.axis_size("seq"))]


def block_order(ns, nw):
    return [s * nw + 2 * z + c for c in range(2) for s in range(ns) for z in range(nw // 2)]


def low(t):
    return t.astype(BF16)


def up(t):
    return t.astype(F32)


def scatter_core(kept, got):
    return [low(up(kept[q]) + up(got[q])) for q in range(kept.shape[0])]


def scatter_seq(a, *first):
    got = [after(swap(a[q], "seq", q), *first) for q in range(1, len(a))]
    total = lambda z: sum((up(t[z]) for t in got), up(a[0][z]))
    return [low(total(z)) for z in range(a[0].shape[0])]


def scatter_z(b, *first):
    got = [after(swap(b[q], "wt", 2 * q), *first) for q in range(1, len(b))]
    return sum((up(t) for t in got), up(b[0]))


def tree_sum(parts):
    while len(parts) > 1:
        parts = [parts[i] + parts[i + 1] for i in range(0, len(parts), 2)]
    return parts[0]


def sum_everywhere(x):
    ns, nw = lax.axis_size("seq"), lax.axis_size("wt")
    x = tree_sum([x] + [swap(x, "seq", q) for q in range(1, ns)])
    x = tree_sum([x] + [swap(x, "wt", 2 * q) for q in range(1, nw // 2)])
    return x + swap(x, "wt", 1)


def after(x, *others):
    return lax.optimization_barrier((x, *others))[0]


def unpack_kernel(order, me_ref, a_ref, b_ref, z_ref, o_ref):
    half = a_ref.shape[2]
    count = a_ref.shape[0] // 4
    for p, offset in enumerate(order):
        x_ref, k = (a_ref, 4 * p) if p < count else (b_ref, 4 * (p - count))
        z_ref[p, :, :half] = x_ref[k]
        z_ref[p, :, half:] = x_ref[k + 1]
        target = 2 * jnp.bitwise_xor(me_ref[0], offset)
        o_ref[target] = x_ref[k + 2]
        o_ref[target + 1] = x_ref[k + 3]


def unpack(order, me, a, b):
    n, share, half = a.shape
    shapes = [(n // 2, share, 2 * half), (n, share, half)]
    return pl.pallas_call(
        functools.partial(unpack_kernel, order),
        grid=(1,),
        out_shape=[jax.ShapeDtypeStruct(s, a.dtype) for s in shapes],
        in_specs=[pl.BlockSpec(memory_space=pltpu.SMEM), whole(a.shape), whole(b.shape)],
        out_specs=[whole(s) for s in shapes],
        compiler_params=params(),
        cost_estimate=cost(0, 8 * a.size),
        name="unpack",
    )(me, a, b)


def pack_kernel(order, me_ref, z_ref, o_ref, a_ref, b_ref):
    half = a_ref.shape[2]
    count = a_ref.shape[0] // 4
    for p, offset in enumerate(order):
        x_ref, k = (a_ref, 4 * p) if p < count else (b_ref, 4 * (p - count))
        x_ref[k] = z_ref[p, :, :half]
        x_ref[k + 1] = z_ref[p, :, half:]
        source = 2 * jnp.bitwise_xor(me_ref[0], offset)
        x_ref[k + 2] = o_ref[source]
        x_ref[k + 3] = o_ref[source + 1]


def pack(order, me, z, o):
    n, share, wide = z.shape
    shape = (2 * n, share, wide // 2)
    return pl.pallas_call(
        functools.partial(pack_kernel, order),
        grid=(1,),
        out_shape=[jax.ShapeDtypeStruct(shape, z.dtype)] * 2,
        in_specs=[pl.BlockSpec(memory_space=pltpu.SMEM), whole(z.shape), whole(o.shape)],
        out_specs=[whole(shape)] * 2,
        compiler_params=params(),
        cost_estimate=cost(0, 8 * z.size),
        name="pack",
    )(me, z, o)


def conv_kernel(nx_ref, wa_ref, wb_ref, taps_ref, conv_ref, act_ref, slope_ref, dt_ref, pad_ref):
    j = pl.program_id(0)
    length = act_ref.shape[0]
    half = wa_ref.shape[0]
    r = dot(nx_ref[:, :half], wa_ref[...]) + dot(nx_ref[:, half:], wb_ref[...])

    @pl.when(j == CHANNELS // LANES)
    def _():
        dt_ref[...] = r[:length]

    @pl.when(j < CHANNELS // LANES)
    def _():
        low = r.astype(BF16)
        conv_ref[...] = low
        f = low.astype(F32)
        pad_ref[EDGE : EDGE + length] = f[:length]
        pad_ref[0:EDGE] = f[length : length + EDGE]
        pad_ref[EDGE + length :] = f[length + EDGE :]
        step = 128
        for c in range(length // step):
            pre = jnp.broadcast_to(taps_ref[TAPS : TAPS + 1, :], (step, LANES))
            for k in range(TAPS):
                start = c * step + k + EDGE - TAPS // 2
                pre = pre + taps_ref[k : k + 1, :] * pad_ref[start : start + step]
            sig = jax.nn.sigmoid(pre)
            rows = slice(c * step, (c + 1) * step)
            act_ref[rows] = (pre * sig).astype(BF16)
            slope_ref[rows] = (sig * (1.0 + pre * (1.0 - sig))).astype(BF16)


def conv_forward(normed, wa, wb, taps):
    ext, d = normed.shape
    length = ext - 2 * EDGE
    blocks = CHANNELS // LANES
    last = blocks - 1
    col = lambda j: (0, jnp.minimum(j, last))
    return pl.pallas_call(
        conv_kernel,
        grid=(blocks + 1,),
        in_specs=[
            whole((ext, d)),
            pl.BlockSpec((d // 2, LANES), lambda j: (0, j)),
            pl.BlockSpec((d // 2, LANES), lambda j: (0, j)),
            pl.BlockSpec((8, LANES), col),
        ],
        out_specs=[
            pl.BlockSpec((ext, LANES), col),
            pl.BlockSpec((length, LANES), col),
            pl.BlockSpec((length, LANES), col),
            whole((length, LANES)),
        ],
        out_shape=[
            jax.ShapeDtypeStruct((ext, CHANNELS), BF16),
            jax.ShapeDtypeStruct((length, CHANNELS), BF16),
            jax.ShapeDtypeStruct((length, CHANNELS), BF16),
            jax.ShapeDtypeStruct((length, LANES), F32),
        ],
        scratch_shapes=[pltpu.VMEM((ext, LANES), F32)],
        compiler_params=params(),
        cost_estimate=cost(2 * ext * d * WIDE, 16 << 20),
        name="conv_forward",
    )(normed, wa, wb, taps)


def iota(shape, dim):
    return lax.broadcasted_iota(jnp.int32, shape, dim)


def fill_expand(exp_ref):
    for c in range(2 * E // LANES):
        row = jnp.bitwise_and(iota((2 * LANES, LANES), 0), LANES - 1)
        lane = iota((2 * LANES, LANES), 1)
        head = 2 * c + jnp.where(lane >= HDIM, 1, 0)
        exp_ref[:, c * LANES : (c + 1) * LANES] = jnp.where(row == head, 1.0, 0.0).astype(BF16)


def two_parts(x):
    hi = x.astype(BF16)
    lo = (x - hi.astype(F32)).astype(BF16)
    return jnp.concatenate([hi, lo], axis=1)


def spread(parts, exp_ref, chunk):
    return dot(parts, exp_ref[:, chunk * LANES : (chunk + 1) * LANES])


def spread_rows(row, exp_ref):
    both = dot(two_parts(row), exp_ref[...])
    return both[:, :E], both[:, E:]


def step_sizes(dtraw, hp_ref):
    lane = iota(dtraw.shape, 1)
    pre = jnp.where(lane < 2 * HEADS, dtraw + hp_ref[0:1, :], 0.0)
    dt = jnp.maximum(pre, 0.0) + jnp.log1p(jnp.exp(-jnp.abs(pre)))
    return pre, dt, hp_ref[1:2, :] * dt


def states_kernel(
    act_ref, dtraw_ref, hp_ref, u_ref, v_ref, ut_ref, vt_ref, eu_ref, wv_ref, tot_ref, s_ref, pay_ref,
    exp_ref, dev_ref, cum_ref,
):
    b = pl.program_id(0)
    nb = pl.num_programs(0)

    @pl.when(b == 0)
    def _():
        fill_expand(exp_ref)
        dev_ref[...] = jnp.zeros_like(dev_ref)
        cum_ref[...] = jnp.zeros_like(cum_ref)

    sq = (STRETCH, LANES)
    lane = iota(sq, 1)
    forward = lane < HEADS
    _, dt, lg = step_sizes(dtraw_ref[...], hp_ref)
    dtb = dt.astype(BF16).astype(F32)
    lgb = lg.astype(BF16)
    upto = jnp.where(iota(sq, 0) >= iota(sq, 1), 1.0, 0.0).astype(BF16)
    run = dot(upto, lgb)
    before = run - lgb.astype(F32)
    total = run[STRETCH - 1 : STRETCH, :] * LOG2E
    logdt = jnp.where(dtb > 0.0, jnp.log(jnp.where(dtb > 0.0, dtb, 1.0)) * LOG2E, -1e30)
    u = jnp.where(forward, before, -run) * LOG2E
    v = jnp.where(forward, -run, before) * LOG2E + logdt
    u_ref[...] = u
    v_ref[...] = v
    ut_ref[0] = u.T
    vt_ref[0] = v.T
    eu = jnp.exp2(u + jnp.where(forward, 0.0, total))
    wv = jnp.exp2(v + jnp.where(forward, total, 0.0))
    eu_ref[...] = eu
    wv_ref[...] = wv
    total8 = jnp.broadcast_to(total, (8, LANES))
    tot_ref[0] = total8

    bt = act_ref[:, E : E + LANES].T
    w2 = two_parts(wv)
    dec_f, _ = spread_rows(jnp.exp2(total8), exp_ref)
    _, pre_r = spread_rows(jnp.exp2(cum_ref[...]), exp_ref)
    for p in range(PAIRS):
        cols = slice(p * LANES, (p + 1) * LANES)
        x = act_ref[:, cols].astype(F32)
        zf = (x * spread(w2, exp_ref, p)).astype(BF16)
        zr = (x * spread(w2, exp_ref, PAIRS + p)).astype(BF16)
        sf = dot(bt[:STATE], zf)
        sr = dot(bt[STATE:], zr)
        s_ref[0, :STATE, cols] = sf.astype(BF16)
        s_ref[0, STATE:, cols] = sr.astype(BF16)
        dev_ref[:STATE, cols] = dec_f[0:1, cols] * dev_ref[:STATE, cols] + sf
        dev_ref[STATE:, cols] = dev_ref[STATE:, cols] + pre_r[0:1, cols] * sr
    cum_ref[...] = cum_ref[...] + total8

    @pl.when(b == nb - 1)
    def _():
        write_payload(pay_ref, dev_ref, cum_ref, exp_ref)


def write_payload(pay_ref, dev_ref, cum_ref, exp_ref):
    cum_f, cum_r = spread_rows(cum_ref[...], exp_ref)
    pay_ref[0, :STATE] = dev_ref[:STATE].astype(BF16)
    pay_ref[1, :STATE] = dev_ref[STATE:].astype(BF16)
    pay_ref[0, STATE:] = jnp.concatenate([cum_f, cum_f], axis=0).astype(BF16)
    pay_ref[1, STATE:] = jnp.concatenate([cum_r, cum_r], axis=0).astype(BF16)


PAY = STATE + 16


def block_states(act, dtraw, hp):
    length = act.shape[0]
    nb = length // STRETCH
    sq = pl.BlockSpec((STRETCH, LANES), lambda b: (b, 0))
    cube = pl.BlockSpec((1, STRETCH, LANES), lambda b: (b, 0, 0))
    flat = jax.ShapeDtypeStruct((length, LANES), F32)
    deep = jax.ShapeDtypeStruct((nb, LANES, STRETCH), F32)
    return pl.pallas_call(
        states_kernel,
        grid=(nb,),
        in_specs=[pl.BlockSpec((STRETCH, CHANNELS), lambda b: (b, 0)), sq, whole((8, LANES))],
        out_specs=[
            sq, sq, cube, cube, sq, sq,
            pl.BlockSpec((1, 8, LANES), lambda b: (b, 0, 0)),
            pl.BlockSpec((1, 2 * STATE, E), lambda b: (b, 0, 0)),
            whole((2, PAY, E)),
        ],
        out_shape=[
            flat, flat, deep, deep, flat, flat,
            jax.ShapeDtypeStruct((nb, 8, LANES), F32),
            jax.ShapeDtypeStruct((nb, 2 * STATE, E), BF16),
            jax.ShapeDtypeStruct((2, PAY, E), BF16),
        ],
        scratch_shapes=[
            pltpu.VMEM((2 * LANES, 2 * E), BF16),
            pltpu.VMEM((2 * STATE, E), F32),
            pltpu.VMEM((8, LANES), F32),
        ],
        compiler_params=params(),
        cost_estimate=cost(4e9, 12 << 20),
        name="block_states",
    )(act, dtraw, hp)


def intra_kernel(act_ref, u_ref, vt_ref, y_ref):
    sq = (STRETCH, STRETCH)
    i, j = iota(sq, 0), iota(sq, 1)
    after, at = i > j, i >= j
    bm = act_ref[:, E : E + LANES]
    cm = act_ref[:, E + LANES :]
    gf = dot_nt(cm[:, :STATE], bm[:, :STATE])
    gr = dot_nt(cm[:, STATE:], bm[:, STATE:])
    gram = jnp.where(after, gf, jnp.where(at, 0.0, gr))
    left = iota((STRETCH, LANES), 1) < HDIM
    for p in range(PAIRS):
        cols = slice(p * LANES, (p + 1) * LANES)
        mats = []
        for h in (2 * p, 2 * p + 1):
            r = HEADS + h
            row = jnp.where(at, u_ref[:, h : h + 1], u_ref[:, r : r + 1])
            col = jnp.where(after, vt_ref[0, h : h + 1, :], vt_ref[0, r : r + 1, :])
            mats.append((jnp.exp2(row + col) * gram).astype(BF16))
        y = dot(jnp.concatenate(mats, axis=0), act_ref[:, cols])
        y_ref[:, cols] = jnp.where(left, y[:STRETCH], y[STRETCH:])


def intra(act, u, vt):
    length = act.shape[0]
    return pl.pallas_call(
        intra_kernel,
        grid=(length // STRETCH,),
        in_specs=[
            pl.BlockSpec((STRETCH, CHANNELS), lambda b: (b, 0)),
            pl.BlockSpec((STRETCH, LANES), lambda b: (b, 0)),
            pl.BlockSpec((1, LANES, STRETCH), lambda b: (b, 0, 0)),
        ],
        out_specs=pl.BlockSpec((STRETCH, E), lambda b: (b, 0)),
        out_shape=jax.ShapeDtypeStruct((length, E), F32),
        compiler_params=params(),
        cost_estimate=cost(8e9, 12 << 20),
        name="intra",
    )(act, u, vt)


def from_others(me, got_ref, upward):
    n = got_ref.shape[0] + 1
    side = lambda d: (d < me) if upward else (d > me)
    total = jnp.zeros((STATE, E), F32)
    for q in range(1, n):
        d = jnp.bitwise_xor(me, q)
        log = jnp.zeros((1, E), F32)
        for k in range(1, n):
            if k != q:
                e = jnp.bitwise_xor(me, k)
                between = ((d < e) & (e < me)) if upward else ((me < e) & (e < d))
                row = got_ref[k - 1, STATE : STATE + 1, :].astype(F32)
                log = log + jnp.where(between, row, 0.0)
        term = jnp.exp2(log) * got_ref[q - 1, :STATE, :].astype(F32)
        total = total + jnp.where(side(d), term, 0.0)
    return total


def gate_kernel(
    me_ref, y_ref, act_ref, z_ref, dg_ref, eu_ref, s_ref, got_ref, tot_ref, rows_ref,
    gated_ref, dz_ref, dy_ref, ent_ref, p_ref, pay_ref, skip_ref,
    exp_ref, dev_ref, cum_ref, yv_ref, ef_ref, er_ref, sums_ref,
):
    b = pl.program_id(0)
    nb = pl.num_programs(0)

    @pl.when(b == 0)
    def _():
        fill_expand(exp_ref)
        dev_ref[...] = jnp.zeros_like(dev_ref)
        cum_ref[...] = jnp.zeros_like(cum_ref)
        sums_ref[...] = jnp.zeros_like(sums_ref)
        me = me_ref[0]
        state = from_others(me, got_ref, True)
        for c in range(s_ref.shape[0]):
            ent_ref[c, :STATE] = state.astype(BF16)
            dec, _ = spread_rows(jnp.exp2(tot_ref[c]), exp_ref)
            state = dec[0:1] * state + s_ref[c, :STATE].astype(F32)
        state = from_others(me, got_ref, False)
        for c in reversed(range(s_ref.shape[0])):
            ent_ref[c, STATE:] = state.astype(BF16)
            _, dec = spread_rows(jnp.exp2(tot_ref[c]), exp_ref)
            state = dec[0:1] * state + s_ref[c, STATE:].astype(F32)

    cm = act_ref[:, E + LANES :]
    e2 = two_parts(eu_ref[...])
    square = jnp.zeros((STRETCH, LANES), F32)
    cross = jnp.zeros((STRETCH, LANES), F32)
    for p in range(PAIRS):
        cols = slice(p * LANES, (p + 1) * LANES)
        ef = spread(e2, exp_ref, p)
        er = spread(e2, exp_ref, PAIRS + p)
        ef_ref[:, cols] = ef
        er_ref[:, cols] = er
        mixed = y_ref[:, cols] + ef * dot(cm[:, :STATE], ent_ref[b, :STATE, cols])
        mixed = mixed + er * dot(cm[:, STATE:], ent_ref[b, STATE:, cols])
        mixed = mixed.astype(BF16).astype(F32)
        yv = mixed + rows_ref[0:1, cols] * act_ref[:, cols].astype(F32)
        yv_ref[:, cols] = yv
        z = z_ref[:, cols].astype(F32)
        yg = yv * (z * jax.nn.sigmoid(z))
        square = square + yg * yg
        cross = cross + rows_ref[1:2, cols] * dg_ref[:, cols].astype(F32) * yg
    inv = lax.rsqrt(jnp.sum(square, axis=1, keepdims=True) / E + EPSILON)
    back = inv * inv * inv * (jnp.sum(cross, axis=1, keepdims=True) / E)

    total8 = tot_ref[b]
    _, dec_r = spread_rows(jnp.exp2(total8), exp_ref)
    pre_f, _ = spread_rows(jnp.exp2(cum_ref[...]), exp_ref)
    ct = cm.T
    for p in range(PAIRS):
        cols = slice(p * LANES, (p + 1) * LANES)
        z = z_ref[:, cols].astype(F32)
        sig = jax.nn.sigmoid(z)
        ga = z * sig
        yv = yv_ref[:, cols]
        yg = yv * ga
        normed = yg * inv
        dg = dg_ref[:, cols].astype(F32)
        gated_ref[:, cols] = (normed * rows_ref[1:2, cols]).astype(BF16)
        dyg = inv * (rows_ref[1:2, cols] * dg) - yg * back
        dy = dyg * ga
        dz_ref[:, cols] = (dyg * yv * sig * (1.0 + z * (1.0 - sig))).astype(BF16)
        low = dy.astype(BF16)
        dy_ref[:, cols] = low
        fold = lambda t: jnp.sum(t.reshape(STRETCH // 8, 8, LANES), axis=0)
        sums_ref[:, cols] = sums_ref[:, cols] + fold(dy * act_ref[:, cols].astype(F32))
        low = low.astype(F32)
        pf = dot(ct[:STATE], (ef_ref[:, cols] * low).astype(BF16))
        pr = dot(ct[STATE:], (er_ref[:, cols] * low).astype(BF16))
        p_ref[0, :STATE, cols] = pf.astype(BF16)
        p_ref[0, STATE:, cols] = pr.astype(BF16)
        dev_ref[:STATE, cols] = dev_ref[:STATE, cols] + pre_f[0:1, cols] * pf
        dev_ref[STATE:, cols] = dec_r[0:1, cols] * dev_ref[STATE:, cols] + pr
    cum_ref[...] = cum_ref[...] + total8

    @pl.when(b == nb - 1)
    def _():
        write_payload(pay_ref, dev_ref, cum_ref, exp_ref)
        per_head = exp_ref[:LANES, :E].astype(F32)
        skip_ref[...] = lax.dot_general(
            sums_ref[...], per_head, NT, precision=lax.Precision.HIGHEST, preferred_element_type=F32
        )


def gate(me, y, act, z, dg, eu, s, got, tot, rows):
    length = act.shape[0]
    nb = length // STRETCH
    line = pl.BlockSpec((STRETCH, E), lambda b: (b, 0))
    return pl.pallas_call(
        gate_kernel,
        grid=(nb,),
        in_specs=[
            pl.BlockSpec(memory_space=pltpu.SMEM),
            line,
            pl.BlockSpec((STRETCH, CHANNELS), lambda b: (b, 0)),
            line,
            line,
            pl.BlockSpec((STRETCH, LANES), lambda b: (b, 0)),
            whole(s.shape),
            whole(got.shape),
            whole(tot.shape),
            whole((8, E)),
        ],
        out_specs=[
            line,
            line,
            line,
            whole(s.shape),
            pl.BlockSpec((1, 2 * STATE, E), lambda b: (b, 0, 0)),
            whole((2, PAY, E)),
            whole((8, LANES)),
        ],
        out_shape=[
            jax.ShapeDtypeStruct((length, E), BF16),
            jax.ShapeDtypeStruct((length, E), BF16),
            jax.ShapeDtypeStruct((length, E), BF16),
            jax.ShapeDtypeStruct(s.shape, BF16),
            jax.ShapeDtypeStruct(s.shape, BF16),
            jax.ShapeDtypeStruct((2, PAY, E), BF16),
            jax.ShapeDtypeStruct((8, LANES), F32),
        ],
        scratch_shapes=[
            pltpu.VMEM((2 * LANES, 2 * E), BF16),
            pltpu.VMEM((2 * STATE, E), F32),
            pltpu.VMEM((8, LANES), F32),
            pltpu.VMEM((STRETCH, E), F32),
            pltpu.VMEM((STRETCH, E), F32),
            pltpu.VMEM((STRETCH, E), F32),
            pltpu.VMEM((8, E), F32),
        ],
        compiler_params=params(),
        cost_estimate=cost(8e9, 32 << 20),
        name="gate",
    )(me, y, act, z, dg, eu, s, got, tot, rows)


def mixer_back_kernel(
    me_ref, act_ref, dy_ref, v_ref, ut_ref, eu_ref, wv_ref, ent_ref, p_ref, got_ref, tot_ref, dtraw_ref, hp_ref,
    dx_ref, dmap_ref, ddt_ref, sums_ref,
    exp_ref, head_ref, out_ref, mask_ref, cs_ref, dmt_ref,
):
    b = pl.program_id(0)
    sq = (STRETCH, STRETCH)
    j, i = iota(sq, 0), iota(sq, 1)
    after, at = i > j, i >= j

    @pl.when(b == 0)
    def _():
        fill_expand(exp_ref)
        sums_ref[...] = jnp.zeros_like(sums_ref)
        cs_ref[...] = jnp.zeros_like(cs_ref)
        mask_ref[...] = jnp.where(after, 1.0, 0.0).astype(BF16)
        for c in range(PAIRS):
            row = iota((2 * LANES, LANES), 0)
            lane = iota((2 * LANES, LANES), 1)
            which = jnp.where(row >= LANES, HEADS, 0) + 2 * c
            which = which + jnp.where(jnp.bitwise_and(row, LANES - 1) >= HDIM, 1, 0)
            head_ref[c] = jnp.where(lane == which, 1.0, 0.0).astype(BF16)
        me = me_ref[0]
        state = from_others(me, got_ref, False)
        for c in reversed(range(p_ref.shape[0])):
            out_ref[c, :STATE] = state.astype(BF16)
            dec, _ = spread_rows(jnp.exp2(tot_ref[c]), exp_ref)
            state = dec[0:1] * state + p_ref[c, :STATE].astype(F32)
        state = from_others(me, got_ref, True)
        for c in range(p_ref.shape[0]):
            out_ref[c, STATE:] = state.astype(BF16)
            _, dec = spread_rows(jnp.exp2(tot_ref[c]), exp_ref)
            state = dec[0:1] * state + p_ref[c, STATE:].astype(F32)

    bm = act_ref[:, E : E + LANES]
    cm = act_ref[:, E + LANES :]
    bf, br, cf, cr = bm[:, :STATE], bm[:, STATE:], cm[:, :STATE], cm[:, STATE:]
    gram = jnp.where(after, dot_nt(bf, cf), jnp.where(at, 0.0, dot_nt(br, cr)))
    e2 = two_parts(eu_ref[...])
    w2 = two_parts(wv_ref[...])
    left = iota((STRETCH, LANES), 1) < HDIM
    ones = jnp.full((8, STRETCH), 1.0, BF16)
    mask = mask_ref[...]
    dmt_ref[...] = jnp.zeros_like(dmt_ref)
    dgram = jnp.zeros(sq, F32)
    col_r = jnp.zeros((STRETCH, LANES), F32)
    col_q = jnp.zeros((STRETCH, LANES), F32)
    carry = jnp.zeros((8, LANES), F32)
    for p in range(PAIRS):
        cols = slice(p * LANES, (p + 1) * LANES)
        xb = act_ref[:, cols]
        dyb = dy_ref[:, cols]
        x = xb.astype(F32)
        dy = dyb.astype(F32)
        x0 = jnp.where(left, x, 0.0).astype(BF16)
        x1 = jnp.where(left, 0.0, x).astype(BF16)
        dm = dot_nt(jnp.concatenate([x0, x1], axis=0), dyb)
        mats = []
        for k, h in enumerate((2 * p, 2 * p + 1)):
            r = HEADS + h
            row = jnp.where(after, v_ref[:, h : h + 1], v_ref[:, r : r + 1])
            col = jnp.where(at, ut_ref[0, h : h + 1, :], ut_ref[0, r : r + 1, :])
            decay = jnp.exp2(row + col)
            mats.append((decay * gram).astype(BF16))
            da = dm[k * STRETCH : (k + 1) * STRETCH] * decay
            dgram = dgram + da
            t = (da * gram).astype(BF16)
            tf = t * mask
            cs = dot(ones, jnp.concatenate([t, tf], axis=1))
            rs = dot_nt(ones, jnp.concatenate([t, tf], axis=0))
            cs_ref[h : h + 1, :] = cs[0:1]
            cs_ref[64 + h : 65 + h, :] = rs[0:1]
        dx2 = dot(jnp.concatenate(mats, axis=0), dyb)
        dx = jnp.where(left, dx2[:STRETCH], dx2[STRETCH:])

        wf = spread(w2, exp_ref, p)
        wr = spread(w2, exp_ref, PAIRS + p)
        ef = spread(e2, exp_ref, p)
        er = spread(e2, exp_ref, PAIRS + p)
        pf, pr = out_ref[b, :STATE, cols], out_ref[b, STATE:, cols]
        sf, sr = ent_ref[0, :STATE, cols], ent_ref[0, STATE:, cols]
        vf = wf * dot(bf, pf)
        vr = wr * dot(br, pr)
        dx_ref[:, cols] = (dx + vf + vr).astype(BF16)
        dyf = ef * dy
        dyr = er * dy
        heads = head_ref[p]
        col_r = col_r + dot(jnp.concatenate([vf * x, vr * x], axis=1).astype(BF16), heads)
        qf = dyf * dot(cf, sf)
        qr = dyr * dot(cr, sr)
        col_q = col_q + dot(jnp.concatenate([qf, qr], axis=1).astype(BF16), heads)
        xf = (wf * x).astype(BF16)
        xr = (wr * x).astype(BF16)
        dmt_ref[:STATE] = dmt_ref[:STATE] + dot_nt(pf, xf)
        dmt_ref[STATE : 2 * STATE] = dmt_ref[STATE : 2 * STATE] + dot_nt(pr, xr)
        dmt_ref[2 * STATE : 3 * STATE] = dmt_ref[2 * STATE : 3 * STATE] + dot_nt(sf, dyf.astype(BF16))
        dmt_ref[3 * STATE :] = dmt_ref[3 * STATE :] + dot_nt(sr, dyr.astype(BF16))
        fold = lambda t: jnp.sum(t.reshape(STATE // 8, 8, LANES), axis=0)
        pair = jnp.concatenate(
            [fold(pf.astype(F32) * sf.astype(F32)), fold(pr.astype(F32) * sr.astype(F32))], axis=1
        )
        carry = carry + dot(pair.astype(BF16), heads)

    gfwd = jnp.where(after, dgram, 0.0).astype(BF16)
    grev = jnp.where(at, 0.0, dgram).astype(BF16)
    bt, ct = bm.T, cm.T
    db_f = dmt_ref[:STATE] + dot_nt(ct[:STATE], gfwd)
    db_r = dmt_ref[STATE : 2 * STATE] + dot_nt(ct[STATE:], grev)
    dc_f = dmt_ref[2 * STATE : 3 * STATE] + dot(bt[:STATE], gfwd)
    dc_r = dmt_ref[3 * STATE :] + dot(bt[STATE:], grev)
    dmap_ref[:, :LANES] = jnp.concatenate([db_f, db_r], axis=0).T
    dmap_ref[:, LANES:] = jnp.concatenate([dc_f, dc_r], axis=0).T

    both = cs_ref[...]
    tot, fwd = both[:, :LANES], both[:, LANES:]
    rev = tot - fwd
    pad = jnp.zeros((LANES - 2 * HEADS, LANES), F32)
    cs = jnp.concatenate([fwd[:HEADS], rev[:HEADS], pad], axis=0).T
    rs = jnp.concatenate([fwd[64 : 64 + HEADS], rev[64 : 64 + HEADS], pad], axis=0).T
    lane = iota((STRETCH, LANES), 1)
    forward = lane < HEADS
    later = jnp.where(after, 1.0, 0.0)
    earlier = jnp.where(at, 0.0, 1.0)
    later_at = jnp.where(at, 1.0, 0.0)
    earlier_at = jnp.where(after, 0.0, 1.0)
    exact = functools.partial(jnp.dot, precision=lax.Precision.HIGHEST, preferred_element_type=F32)
    gain = cs + col_q
    dlg_f = exact(later, gain) - exact(later_at, rs) + exact(earlier, col_r)
    dlg_r = exact(earlier, gain) - exact(earlier_at, rs) + exact(later, col_r)
    dlg = jnp.where(forward, dlg_f, dlg_r)
    dlg = dlg + jnp.exp2(tot_ref[b])[0:1] * jnp.sum(carry, axis=0, keepdims=True)
    pre, dt, lg = step_sizes(dtraw_ref[...], hp_ref)
    dtb = dt.astype(BF16).astype(F32)
    ok = (dtb > 0.0) & (lane < 2 * HEADS)
    ddt = jnp.where(ok, (rs + col_r) / jnp.where(ok, dtb, 1.0), 0.0)
    ddt = ddt.astype(BF16).astype(F32)
    dlg = jnp.where(lane < 2 * HEADS, dlg, 0.0).astype(BF16).astype(F32)
    draw = (ddt + dlg * hp_ref[1:2, :]) * jax.nn.sigmoid(pre)
    ddt_ref[...] = draw.astype(BF16)
    fold = lambda t: jnp.sum(t.reshape(STRETCH // 8, 8, LANES), axis=0)
    sums_ref[0:8] = sums_ref[0:8] + fold(draw)
    sums_ref[8:16] = sums_ref[8:16] + fold(dlg * lg)


def mixer_back(me, act, dy, v, ut, eu, wv, ent, p, got, tot, dtraw, hp):
    length = act.shape[0]
    nb = length // STRETCH
    sq = pl.BlockSpec((STRETCH, LANES), lambda b: (b, 0))
    line = pl.BlockSpec((STRETCH, E), lambda b: (b, 0))
    cube = pl.BlockSpec((1, LANES, STRETCH), lambda b: (b, 0, 0))
    return pl.pallas_call(
        mixer_back_kernel,
        grid=(nb,),
        in_specs=[
            pl.BlockSpec(memory_space=pltpu.SMEM),
            pl.BlockSpec((STRETCH, CHANNELS), lambda b: (b, 0)),
            line,
            sq,
            cube,
            sq,
            sq,
            pl.BlockSpec((1, 2 * STATE, E), lambda b: (b, 0, 0)),
            whole(p.shape),
            whole(got.shape),
            whole(tot.shape),
            sq,
            whole((8, LANES)),
        ],
        out_specs=[
            line,
            pl.BlockSpec((STRETCH, 2 * LANES), lambda b: (b, 0)),
            sq,
            whole((16, LANES)),
        ],
        out_shape=[
            jax.ShapeDtypeStruct((length, E), BF16),
            jax.ShapeDtypeStruct((length, 2 * LANES), F32),
            jax.ShapeDtypeStruct((length, LANES), BF16),
            jax.ShapeDtypeStruct((16, LANES), F32),
        ],
        scratch_shapes=[
            pltpu.VMEM((2 * LANES, 2 * E), BF16),
            pltpu.VMEM((PAIRS, 2 * LANES, LANES), BF16),
            pltpu.VMEM(p.shape, BF16),
            pltpu.VMEM((STRETCH, STRETCH), BF16),
            pltpu.VMEM((LANES, 2 * LANES), F32),
            pltpu.VMEM((4 * STATE, STRETCH), F32),
        ],
        compiler_params=params(),
        cost_estimate=cost(16e9, 20 << 20),
        name="mixer_back",
    )(me, act, dy, v, ut, eu, wv, ent, p, got, tot, dtraw, hp)


def conv_back_kernel(
    dx_ref, dy_ref, dmap_ref, slope_ref, conv_ref, taps_ref, skip_ref, ddt_ref, hsum_ref, ssum_ref,
    dconv_ref, sums_ref, dact_ref, dpad_ref, pad_ref,
):
    j = pl.program_id(0)
    length = slope_ref.shape[0]

    @pl.when(j == CHANNELS // LANES)
    def _():
        dconv_ref[:length] = ddt_ref[...]
        dconv_ref[length:] = jnp.zeros((2 * EDGE, LANES), BF16)
        parts = [hsum_ref[:8], hsum_ref[8:], ssum_ref[...]]
        parts = [jnp.sum(t, axis=0, keepdims=True) for t in parts]
        sums_ref[...] = jnp.concatenate(parts + [jnp.zeros((5, LANES), F32)], axis=0)

    @pl.when(j < CHANNELS // LANES)
    def _():
        conv_back_block(
            j, length, dx_ref, dy_ref, dmap_ref, slope_ref, conv_ref, taps_ref, skip_ref, dconv_ref, sums_ref,
            dact_ref, dpad_ref, pad_ref,
        )


def conv_back_block(
    j, length, dx_ref, dy_ref, dmap_ref, slope_ref, conv_ref, taps_ref, skip_ref, dconv_ref, sums_ref,
    dact_ref, dpad_ref, pad_ref,
):

    @pl.when(j < PAIRS)
    def _():
        dact_ref[...] = dx_ref[...].astype(F32) + skip_ref[0:1, :] * dy_ref[...].astype(F32)

    @pl.when(j >= PAIRS)
    def _():
        dact_ref[...] = dmap_ref[...]

    margin = 2 * EDGE
    dpad_ref[0:margin] = jnp.zeros((margin, LANES), F32)
    dpad_ref[margin + length :] = jnp.zeros((margin, LANES), F32)
    dpad_ref[margin : margin + length] = dact_ref[...] * slope_ref[...].astype(F32)
    pad_ref[EDGE : EDGE + length] = conv_ref[:length].astype(F32)
    pad_ref[0:EDGE] = conv_ref[length : length + EDGE].astype(F32)
    pad_ref[EDGE + length :] = conv_ref[length + EDGE :].astype(F32)
    half = TAPS // 2

    def spread_back(first, rows):
        out = jnp.zeros((rows, LANES), F32)
        for k in range(TAPS):
            start = margin + first - k + half
            out = out + taps_ref[k : k + 1, :] * dpad_ref[start : start + rows]
        return out.astype(BF16)

    step = 128
    sums = [jnp.zeros((8, LANES), F32) for _ in range(TAPS + 1)]
    for c in range(length // step):
        first = c * step
        dconv_ref[first : first + step] = spread_back(first, step)
        fold = lambda t: jnp.sum(t.reshape(step // 8, 8, LANES), axis=0)
        dpre = dpad_ref[margin + first : margin + first + step]
        for k in range(TAPS):
            start = first + k + EDGE - half
            sums[k] = sums[k] + fold(dpre * pad_ref[start : start + step])
        sums[TAPS] = sums[TAPS] + fold(dpre)
    edges = jnp.concatenate([spread_back(-EDGE, EDGE), spread_back(length, EDGE)], axis=0)
    dconv_ref[length:] = edges
    sums_ref[...] = jnp.concatenate([jnp.sum(t, axis=0, keepdims=True) for t in sums], axis=0)


def conv_back(dx, dy, dmap, slope, conv, taps, skip, ddt, hsums, ssums):
    ext = conv.shape[0]
    length = ext - 2 * EDGE
    early = lambda j: (0, jnp.minimum(j, PAIRS - 1))
    late = lambda j: (0, jnp.clip(j - PAIRS, 0, 1))
    col = lambda j: (0, jnp.minimum(j, CHANNELS // LANES - 1))
    return pl.pallas_call(
        conv_back_kernel,
        grid=(WIDE // LANES,),
        in_specs=[
            pl.BlockSpec((length, LANES), early),
            pl.BlockSpec((length, LANES), early),
            pl.BlockSpec((length, LANES), late),
            pl.BlockSpec((length, LANES), col),
            pl.BlockSpec((ext, LANES), col),
            pl.BlockSpec((8, LANES), col),
            pl.BlockSpec((8, LANES), early),
            whole((length, LANES)),
            whole((16, LANES)),
            whole((8, LANES)),
        ],
        out_specs=[pl.BlockSpec((ext, LANES), lambda j: (0, j)), pl.BlockSpec((8, LANES), lambda j: (0, j))],
        out_shape=[
            jax.ShapeDtypeStruct((ext, WIDE), BF16),
            jax.ShapeDtypeStruct((8, WIDE), F32),
        ],
        scratch_shapes=[
            pltpu.VMEM((length, LANES), F32),
            pltpu.VMEM((length + 4 * EDGE, LANES), F32),
            pltpu.VMEM((ext, LANES), F32),
        ],
        compiler_params=params(),
        cost_estimate=cost(2e9, 20 << 20),
        name="conv_back",
    )(dx, dy, dmap, slope, conv, taps, skip, ddt, hsums, ssums)


def send_states(payload, to_later):
    n, me = lax.axis_size("seq"), lax.axis_index("seq")
    sent, got = [], []
    for q in range(1, n):
        later = (me ^ q) > me
        first = later if to_later else ~later
        sent.append(jnp.where(first, payload[0], payload[1]))
        got.append(swap(sent[-1], "seq", q))
    return sent, jnp.stack(got)


def per_device(
    layer_in, norm_gain, in_weight, conv_weight, conv_bias, head_params, out_gain, out_weight, out_cotangent
):
    ns, nw = lax.axis_size("seq"), lax.axis_size("wt")
    ndev = ns * nw
    seq_me = lax.axis_index("seq").astype(jnp.int32)
    me = seq_me * nw + lax.axis_index("wt").astype(jnp.int32)
    me_arr, seq_arr = me.reshape(1), seq_me.reshape(1)
    tokens = layer_in[0]
    cotangent = out_cotangent[0]
    length, d = tokens.shape
    share = in_weight.shape[0]
    cshare = conv_bias.shape[0]
    gshare = out_gain.shape[0]
    spare = WIDE - (in_weight.shape[1] - E)

    forward = [(i, i + 1) for i in range(ns - 1)]
    backward = [(i + 1, i) for i in range(ns - 1)]
    before = lax.ppermute(tokens[length - EDGE :], "seq", forward)
    behind = lax.ppermute(tokens[:EDGE], "seq", backward)
    ext = jnp.concatenate([tokens, before, behind], axis=0)

    small = jnp.concatenate([conv_weight.reshape(-1), conv_bias, out_gain, norm_gain])
    n_small = small.shape[0]
    small = jnp.pad(small, (0, 8 * LANES - n_small)).reshape(8, LANES)
    first = jnp.pad(in_weight[:, E:], ((0, 0), (0, spare)))
    half = E // 2
    rest = jnp.concatenate(
        [in_weight[None, :, :half], in_weight[None, :, half:E], out_weight.reshape(2, share, d)], axis=0
    )
    a1 = jnp.stack(gather_z(first))
    b1 = gather_z(after(rest, a1))
    s1 = jnp.stack(gather_z(small))
    a2 = jnp.stack(gather_seq(after(a1, before, behind, s1)))
    s2 = jnp.stack(gather_seq(s1))
    b1 = jnp.stack(b1)
    b2 = gather_seq(after(b1, a2))
    wa, wb = a2.reshape(d // 2, WIDE), swap(after(a2, b1), "wt", 1).reshape(d // 2, WIDE)

    blocks = jnp.arange(d, dtype=jnp.int32) // share
    offsets = block_order(ns, nw)
    offset_of = jnp.array(offsets, jnp.int32)
    natural = (offset_of[blocks] ^ me) * share + jnp.arange(d, dtype=jnp.int32) % share
    perm = (jnp.arange(d, dtype=jnp.int32)[:, None] == natural[None, :]).astype(BF16)
    u_x = dot(ext, perm)
    inv_in = lax.rsqrt(jnp.mean(jnp.square(ext.astype(F32)), axis=1, keepdims=True) + EPSILON)

    extras = jnp.stack([s2, swap(s2, "wt", 1)]).reshape(ndev, 8 * LANES)
    order = jnp.arange(ndev, dtype=jnp.int32)[:, None] == (offset_of[None, :] ^ me)
    nat = dot(order.astype(BF16), extras[:, :n_small])
    taps = jnp.transpose(nat[:, : TAPS * cshare].reshape(ndev, TAPS, cshare), (1, 0, 2)).reshape(TAPS, CHANNELS)
    bias = nat[:, TAPS * cshare : (TAPS + 1) * cshare].reshape(1, CHANNELS)
    taps = jnp.concatenate([taps, bias], axis=0)
    gain_out = nat[:, (TAPS + 1) * cshare : (TAPS + 1) * cshare + gshare].reshape(1, E)
    gain_x = extras[:, n_small - share : n_small].reshape(1, d).astype(F32)

    normed = (u_x * inv_in * gain_x).astype(BF16)
    conv, act, slope, dtraw = conv_forward(normed, wa, wb, taps)

    twice = jnp.concatenate([head_params, head_params], axis=1)
    rates = jnp.stack([twice[0], -jnp.exp(twice[1])])
    hp = jnp.pad(rates, ((0, 6), (0, LANES - 2 * HEADS)))
    b2 = jnp.stack([after(t, dtraw) for t in b2]).reshape(2 * ndev, share, half)
    b3 = swap(b2, "wt", 1)
    u, v, ut, vt, eu, wv, tot, s, pay = block_states(act, dtraw, hp)
    sent, got = send_states(pay, True)
    w_z, w_out = unpack(offsets, me_arr, b2, after(b3, *sent))
    w_z, w_out = w_z.reshape(d, E), w_out.reshape(E, d)
    own = normed[:length]
    z = dot(own, w_z).astype(BF16)
    dgated = dot_nt(cotangent, w_out).astype(BF16)
    y = intra(act, u, vt)
    skip = jnp.repeat(head_params[2], HDIM)[None]
    rows = jnp.concatenate([skip, gain_out, jnp.zeros((6, E), F32)], axis=0)
    gated, dz, dy, ent, p, pay, ssums = gate(seq_arr, y, act, z, dgated, eu, s, got, tot, rows)
    sent, got = send_states(pay, False)

    gated_then = after(gated, *sent)
    g_out = lax.dot_general(gated_then, cotangent, TN, preferred_element_type=F32).astype(BF16)
    g_z = lax.dot_general(own, after(dz, *sent), TN, preferred_element_type=F32).astype(BF16)
    g_z = after(g_z, got)
    kept, moved = pack(offsets, me_arr, g_z.reshape(ndev, share, E), g_out.reshape(2 * ndev, share, d))
    moved = swap(moved, "wt", 1)
    dx, dmap, ddt, hsums = mixer_back(
        seq_arr, act, after(dy, kept), v, ut, eu, wv, ent, p, got, tot, dtraw, hp
    )
    split = lambda t: t.reshape(ns, nw // 2, 4, share, half)
    r1 = scatter_core(split(kept), split(after(moved, dx)))
    dconv, csums = conv_back(after(dx, *r1), dy, dmap, slope, conv, taps, rows, ddt, hsums, ssums)

    r2 = scatter_seq(r1)
    g_c = lax.dot_general(normed, dconv, TN, preferred_element_type=F32).astype(BF16)
    g_c = g_c.reshape(2, ns, nw // 2, share, WIDE)
    sent = after(g_c[1], *r2)
    f1 = scatter_core(g_c[0], swap(sent, "wt", 1))
    w_first = jnp.concatenate([wa, wb])
    dn = dot_nt(after(dconv, sent), w_first)
    f2 = scatter_seq(f1)
    dn_z = dot_nt(after(dz, *f1), w_z)
    layer_out = (tokens.astype(F32) + dot(after(gated, *f1), w_out)).astype(BF16)[None]
    dn = dn + jnp.concatenate([dn_z, jnp.zeros((2 * EDGE, d), F32)], axis=0)
    grad_first = scatter_z(f2)
    r3 = scatter_z(r2, *f2)
    csums = sum_everywhere(after(csums, *f1))

    dn = after(dn, *f2)
    dn_hi = dn.astype(BF16)
    dn_lo = (dn - dn_hi.astype(F32)).astype(BF16)
    dn = dot_nt(dn_hi, perm) + dot_nt(dn_lo, perm)
    prev_edge = lax.ppermute(dn[length : length + EDGE], "seq", backward)
    next_edge = lax.ppermute(dn[length + EDGE :], "seq", forward)
    middle = jnp.zeros((length - 2 * EDGE, d), F32)
    dn = dn[:length] + jnp.concatenate([next_edge, middle, prev_edge], axis=0)
    u, inv = tokens.astype(F32), inv_in[:length]
    scaled = nat[:, n_small - share :].reshape(1, d) * dn
    in_grad = cotangent.astype(F32) + inv * scaled
    in_grad = in_grad - u * inv**3 * jnp.mean(scaled * u, axis=1, keepdims=True)

    grad_z = jnp.concatenate([r3[0], r3[1]], axis=1)
    grad_out = r3[2:].reshape(gshare, d)
    vec = lax.dynamic_slice(csums, (0, me * cshare), (8, cshare))
    pair = csums[:3, CHANNELS : CHANNELS + 2 * HEADS]
    head_grad = pair[:, :HEADS] + pair[:, HEADS:]
    grad_in = jnp.concatenate([grad_z, grad_first[:, : WIDE - spare]], axis=1)
    gain_grad = jnp.sum(in_weight.astype(F32) * grad_in, axis=1) / norm_gain.astype(F32)
    out_gain_grad = jnp.sum(out_weight.astype(F32) * grad_out, axis=1) / out_gain.astype(F32)
    return (
        layer_out,
        in_grad[None],
        gain_grad,
        grad_in,
        vec[:TAPS],
        vec[TAPS],
        head_grad,
        out_gain_grad,
        grad_out,
    )


def solution(mesh):
    rows = P(("seq", "wt"))
    table = P(("seq", "wt"), None)
    tokens = P("wt", "seq", None)
    taps = P(None, ("seq", "wt"))
    return jax.shard_map(
        per_device,
        mesh=mesh,
        in_specs=(tokens, rows, table, taps, rows, P(), rows, table, tokens),
        out_specs=(tokens, tokens, rows, table, taps, rows, P(), rows, table),
        check_vma=False,
    )
```

```python
import functools

import jax
import jax.numpy as jnp
from jax import lax
from jax.experimental import pallas as pl
from jax.experimental.pallas import tpu as pltpu
from jax.sharding import PartitionSpec as P

HEADS = 24
HDIM = 64
STATE = 64
STRETCH = 128
TAPS = 7
E = 1536
CHANNELS = 1792
PAIRS = HEADS // 2
LANES = 128
WIDE = 1920
EDGE = 8
EPSILON = 1e-05
LOG2E = 1.4426950408889634

F32 = jnp.float32
BF16 = jnp.bfloat16
NT = (((1,), (1,)), ((), ()))
TN = (((0,), (0,)), ((), ()))


def dot(a, b):
    return jnp.dot(a, b, preferred_element_type=F32)


def dot_nt(a, b):
    return lax.dot_general(a, b, NT, preferred_element_type=F32)


def params(limit=56):
    return pltpu.CompilerParams(vmem_limit_bytes=limit << 20)


def cost(flops, moved, trans=0):
    return pl.CostEstimate(flops=int(flops), bytes_accessed=int(moved), transcendentals=int(trans))


def whole(shape):
    return pl.BlockSpec(shape, lambda *_: (0,) * len(shape), pipeline_mode=pl.Buffered(1))


def swap(x, axis, q):
    n = lax.axis_size(axis)
    return lax.ppermute(x, axis, [(i, i ^ q) for i in range(n)])


def gather_z(x):
    return [x] + [swap(x, "wt", 2 * q) for q in range(1, lax.axis_size("wt") // 2)]


def gather_seq(x):
    return [x] + [swap(x, "seq", q) for q in range(1, lax.axis_size("seq"))]


def block_order(ns, nw):
    return [s * nw + 2 * z + c for c in range(2) for s in range(ns) for z in range(nw // 2)]


def low(t):
    return t.astype(BF16)


def up(t):
    return t.astype(F32)


def scatter_core(kept, got):
    return [low(up(kept[q]) + up(got[q])) for q in range(kept.shape[0])]


def scatter_seq(a, got=None):
    if got is None:
        got = [swap(a[q], "seq", q) for q in range(1, len(a))]
    total = lambda z: sum((up(t[z]) for t in got), up(a[0][z]))
    return [low(total(z)) for z in range(a[0].shape[0])]


def scatter_z(b, *first):
    got = [after(swap(b[q], "wt", 2 * q), *first) for q in range(1, len(b))]
    return sum((up(t) for t in got), up(b[0]))


def tree_sum(parts):
    while len(parts) > 1:
        parts = [parts[i] + parts[i + 1] for i in range(0, len(parts), 2)]
    return parts[0]


def sum_everywhere(x, first, second, third):
    ns, nw = lax.axis_size("seq"), lax.axis_size("wt")
    x = after(x, first)
    x = tree_sum([x] + [swap(x, "seq", q) for q in range(1, ns)])
    x = after(x, second)
    x = tree_sum([x] + [swap(x, "wt", 2 * q) for q in range(1, nw // 2)])
    x = after(x, third)
    return x + swap(x, "wt", 1)


def after(x, *others):
    return lax.optimization_barrier((x, *others))[0]


def unpack_kernel(order, me_ref, a_ref, b_ref, z_ref, o_ref):
    half = a_ref.shape[2]
    count = a_ref.shape[0] // 4
    for p, offset in enumerate(order):
        x_ref, k = (a_ref, 4 * p) if p < count else (b_ref, 4 * (p - count))
        z_ref[p, :, :half] = x_ref[k]
        z_ref[p, :, half:] = x_ref[k + 1]
        target = 2 * jnp.bitwise_xor(me_ref[0], offset)
        o_ref[target] = x_ref[k + 2]
        o_ref[target + 1] = x_ref[k + 3]


def unpack(order, me, a, b):
    n, share, half = a.shape
    shapes = [(n // 2, share, 2 * half), (n, share, half)]
    return pl.pallas_call(
        functools.partial(unpack_kernel, order),
        grid=(1,),
        out_shape=[jax.ShapeDtypeStruct(s, a.dtype) for s in shapes],
        in_specs=[pl.BlockSpec(memory_space=pltpu.SMEM), whole(a.shape), whole(b.shape)],
        out_specs=[whole(s) for s in shapes],
        compiler_params=params(12),
        cost_estimate=cost(0, 8 * a.size),
        name="unpack",
    )(me, a, b)


def pack_kernel(order, me_ref, z_ref, o_ref, a_ref, b_ref):
    half = a_ref.shape[2]
    count = a_ref.shape[0] // 4
    for p, offset in enumerate(order):
        x_ref, k = (a_ref, 4 * p) if p < count else (b_ref, 4 * (p - count))
        x_ref[k] = z_ref[p, :, :half]
        x_ref[k + 1] = z_ref[p, :, half:]
        source = 2 * jnp.bitwise_xor(me_ref[0], offset)
        x_ref[k + 2] = o_ref[source]
        x_ref[k + 3] = o_ref[source + 1]


def pack(order, me, z, o):
    n, share, wide = z.shape
    shape = (2 * n, share, wide // 2)
    return pl.pallas_call(
        functools.partial(pack_kernel, order),
        grid=(1,),
        out_shape=[jax.ShapeDtypeStruct(shape, z.dtype)] * 2,
        in_specs=[pl.BlockSpec(memory_space=pltpu.SMEM), whole(z.shape), whole(o.shape)],
        out_specs=[whole(shape)] * 2,
        compiler_params=params(12),
        cost_estimate=cost(0, 8 * z.size),
        name="pack",
    )(me, z, o)


BLOCK = 256


SHIFTS = [k for k in range(TAPS) if k != TAPS // 2]
MARGIN = 16
WINDOW = STRETCH + 2 * MARGIN


def fill_shifts(shift_ref, sign):
    for n, k in enumerate(SHIFTS):
        picked = iota((STRETCH, WINDOW), 0) + (MARGIN + sign * (k - TAPS // 2))
        same = iota((STRETCH, WINDOW), 1) == picked
        shift_ref[n * STRETCH : (n + 1) * STRETCH, :] = jnp.where(same, 1.0, 0.0).astype(BF16)


def shifted_rows(shift_ref, pad_ref, first):
    rows = dot(shift_ref[...], pad_ref[first : first + WINDOW, :])
    out = {k: rows[n * STRETCH : (n + 1) * STRETCH] for n, k in enumerate(SHIFTS)}
    out[TAPS // 2] = pad_ref[first + MARGIN : first + MARGIN + STRETCH, :].astype(F32)
    return out


def conv_kernel(
    nx_ref, wa_ref, wb_ref, da_ref, db_ref, taps_ref, conv_ref, act_ref, slope_ref, dt_ref, pad_ref, shift_ref
):
    length = act_ref.shape[0]

    @pl.when(pl.program_id(0) == 0)
    def _():
        fill_shifts(shift_ref, 1)
        pad_ref[...] = jnp.zeros_like(pad_ref)

    w = jnp.concatenate([wa_ref[...], wb_ref[...]], axis=0)
    zeros = jnp.zeros((EDGE, BLOCK), BF16)
    r = dot(nx_ref[length:], w).astype(BF16)
    conv_ref[length:] = r
    pad_ref[:MARGIN] = jnp.concatenate([zeros, r[:EDGE]], axis=0)
    pad_ref[MARGIN + length :] = jnp.concatenate([r[EDGE:], zeros], axis=0)
    count = length // STRETCH
    for c in range(count + 1):
        if c < count:
            rows = slice(c * STRETCH, (c + 1) * STRETCH)
            r = dot(nx_ref[rows], w).astype(BF16)
            conv_ref[rows] = r
            pad_ref[MARGIN + rows.start : MARGIN + rows.stop] = r
        if c > 0:
            first = (c - 1) * STRETCH
            pre = jnp.broadcast_to(taps_ref[TAPS : TAPS + 1, :], (STRETCH, BLOCK))
            for k, x in shifted_rows(shift_ref, pad_ref, first).items():
                pre = pre + taps_ref[k : k + 1, :] * x
            sig = jax.nn.sigmoid(pre)
            act = pre * sig
            rows = slice(first, first + STRETCH)
            act_ref[rows] = act.astype(BF16)
            slope_ref[rows] = (sig + act * (1.0 - sig)).astype(BF16)

    @pl.when(pl.program_id(0) == pl.num_programs(0) - 1)
    def _():
        w = jnp.concatenate([da_ref[...], db_ref[...]], axis=0)
        dt_ref[...] = dot(nx_ref[:length], w)


def conv_forward(normed, wa, wb, taps):
    ext, d = normed.shape
    length = ext - 2 * EDGE
    col = lambda j: (0, j)
    steps = pl.BlockSpec((d // 2, LANES), lambda j: (0, CHANNELS // LANES))
    return pl.pallas_call(
        conv_kernel,
        grid=(CHANNELS // BLOCK,),
        in_specs=[
            whole((ext, d)),
            pl.BlockSpec((d // 2, BLOCK), col),
            pl.BlockSpec((d // 2, BLOCK), col),
            steps,
            steps,
            pl.BlockSpec((8, BLOCK), col),
        ],
        out_specs=[
            pl.BlockSpec((ext, BLOCK), col),
            pl.BlockSpec((length, BLOCK), col),
            pl.BlockSpec((length, BLOCK), col),
            whole((length, LANES)),
        ],
        out_shape=[
            jax.ShapeDtypeStruct((ext, CHANNELS), BF16),
            jax.ShapeDtypeStruct((length, CHANNELS), BF16),
            jax.ShapeDtypeStruct((length, CHANNELS), BF16),
            jax.ShapeDtypeStruct((length, LANES), F32),
        ],
        scratch_shapes=[
            pltpu.VMEM((length + 2 * MARGIN, BLOCK), BF16),
            pltpu.VMEM((len(SHIFTS) * STRETCH, WINDOW), BF16),
        ],
        compiler_params=params(14),
        cost_estimate=cost(2 * ext * d * WIDE, 16 << 20),
        name="conv_forward",
    )(normed, wa, wb, wa, wb, taps)


def iota(shape, dim):
    return lax.broadcasted_iota(jnp.int32, shape, dim)


def fill_expand(exp_ref):
    for c in range(2 * E // LANES):
        row = jnp.bitwise_and(iota((2 * LANES, LANES), 0), LANES - 1)
        head = 2 * c + jnp.where(iota((2 * LANES, LANES), 1) >= HDIM, 1, 0)
        exp_ref[:, c * LANES : (c + 1) * LANES] = jnp.where(row == head, 1.0, 0.0).astype(BF16)


def fill_heads(heads_ref):
    for c in range(4 * PAIRS):
        head = 2 * (c % PAIRS) + (HEADS if c >= 2 * PAIRS else 0)
        head = head + jnp.where(iota((LANES, LANES), 0) >= HDIM, 1, 0)
        same = iota((LANES, LANES), 1) == head
        heads_ref[c * LANES : (c + 1) * LANES, :] = jnp.where(same, 1.0, 0.0).astype(BF16)


def two_parts(x):
    hi = x.astype(BF16)
    lo = (x - hi.astype(F32)).astype(BF16)
    return jnp.concatenate([hi, lo], axis=1)


CHUNKS = [slice(c * 2 * LANES, (c + 1) * 2 * LANES) for c in range(E // (2 * LANES))]
PAIR_COLS = [slice(p * LANES, (p + 1) * LANES) for p in range(PAIRS)]


def shifted(cols):
    return slice(cols.start + E, cols.stop + E)


def pair_rows(row, p, first):
    h = first + 2 * p
    left = iota((8, LANES), 1) < HDIM
    return jnp.where(left, row[:, h : h + 1], row[:, h + 1 : h + 2])


def scan_states(out_ref, state_ref, tot_ref, add_ref, first, backward):
    rows = slice(0, STATE) if first == 0 else slice(STATE, 2 * STATE)
    order = range(add_ref.shape[0])
    for c in reversed(order) if backward else order:
        dec = jnp.exp2(tot_ref[c])
        for p, cols in enumerate(PAIR_COLS):
            state = state_ref[:, cols]
            out_ref[c, rows, cols] = state.astype(BF16)
            state_ref[:, cols] = pair_rows(dec, p, first)[0:1] * state + add_ref[c, rows, cols].astype(F32)


def step_sizes(dtraw, hp_ref):
    lane = iota(dtraw.shape, 1)
    pre = jnp.where(lane < 2 * HEADS, dtraw + hp_ref[0:1, :], 0.0)
    dt = jnp.maximum(pre, 0.0) + jnp.log1p(jnp.exp(-jnp.abs(pre)))
    return pre, dt, hp_ref[1:2, :] * dt


def states_kernel(
    act_ref, dtraw_ref, hp_ref, u_ref, v_ref, ut_ref, vt_ref, eu_ref, wv_ref, tot_ref, s_ref, pay_ref,
    exp_ref, dev_ref, cum_ref, z_ref,
):
    b = pl.program_id(0)
    nb = pl.num_programs(0)

    @pl.when(b == 0)
    def _():
        fill_expand(exp_ref)
        dev_ref[...] = jnp.zeros_like(dev_ref)
        cum_ref[...] = jnp.zeros_like(cum_ref)

    sq = (STRETCH, LANES)
    lane = iota(sq, 1)
    forward = lane < HEADS
    _, dt, lg = step_sizes(dtraw_ref[...], hp_ref)
    dtb = dt.astype(BF16).astype(F32)
    lgb = lg.astype(BF16)
    upto = jnp.where(iota(sq, 0) >= iota(sq, 1), 1.0, 0.0).astype(BF16)
    run = dot(upto, lgb)
    before = run - lgb.astype(F32)
    total = run[STRETCH - 1 : STRETCH, :] * LOG2E
    logdt = jnp.where(dtb > 0.0, jnp.log(jnp.where(dtb > 0.0, dtb, 1.0)) * LOG2E, -1e30)
    u = jnp.where(forward, before, -run) * LOG2E
    v = jnp.where(forward, -run, before) * LOG2E + logdt
    u_ref[...] = u
    v_ref[...] = v
    ut_ref[0] = u.T
    vt_ref[0] = v.T
    eu = jnp.exp2(u + jnp.where(forward, 0.0, total))
    wv = jnp.exp2(v + jnp.where(forward, total, 0.0))
    eu_ref[...] = eu
    wv_ref[...] = wv
    total8 = jnp.broadcast_to(total, (8, LANES))
    tot_ref[0] = total8

    bt = act_ref[:, E : E + LANES].T
    w2 = two_parts(wv)
    for cols in CHUNKS:
        x = act_ref[:, cols].astype(F32)
        z_ref[:, cols] = (x * dot(w2, exp_ref[:, cols])).astype(BF16)
        z_ref[:, shifted(cols)] = (x * dot(w2, exp_ref[:, shifted(cols)])).astype(BF16)
    dec = jnp.exp2(total8)
    pre = jnp.exp2(cum_ref[...])
    for c, cols in enumerate(CHUNKS):
        sf = dot(bt[:STATE], z_ref[:, cols])
        sr = dot(bt[STATE:], z_ref[:, shifted(cols)])
        s_ref[0, :STATE, cols] = sf.astype(BF16)
        s_ref[0, STATE:, cols] = sr.astype(BF16)
        dec_f = jnp.concatenate([pair_rows(dec, 2 * c, 0), pair_rows(dec, 2 * c + 1, 0)], axis=1)
        pre_r = jnp.concatenate([pair_rows(pre, 2 * c, HEADS), pair_rows(pre, 2 * c + 1, HEADS)], axis=1)
        dev_ref[:STATE, cols] = dec_f[0:1] * dev_ref[:STATE, cols] + sf
        dev_ref[STATE:, cols] = dev_ref[STATE:, cols] + pre_r[0:1] * sr
    cum_ref[...] = cum_ref[...] + total8

    @pl.when(b == nb - 1)
    def _():
        write_payload(pay_ref, dev_ref, cum_ref)


def write_payload(pay_ref, dev_ref, cum_ref):
    cum = cum_ref[...]
    pay_ref[0, :STATE] = dev_ref[:STATE].astype(BF16)
    pay_ref[1, :STATE] = dev_ref[STATE:].astype(BF16)
    for k in range(2):
        for p, cols in enumerate(PAIR_COLS):
            row = pair_rows(cum, p, k * HEADS)
            pay_ref[k, STATE:, cols] = jnp.concatenate([row, row], axis=0).astype(BF16)


PAY = STATE + 16


def block_states(act, dtraw, hp):
    length = act.shape[0]
    nb = length // STRETCH
    sq = pl.BlockSpec((STRETCH, LANES), lambda b: (b, 0))
    cube = pl.BlockSpec((1, STRETCH, LANES), lambda b: (b, 0, 0))
    flat = jax.ShapeDtypeStruct((length, LANES), F32)
    deep = jax.ShapeDtypeStruct((nb, LANES, STRETCH), F32)
    return pl.pallas_call(
        states_kernel,
        grid=(nb,),
        in_specs=[pl.BlockSpec((STRETCH, CHANNELS), lambda b: (b, 0)), sq, whole((8, LANES))],
        out_specs=[
            sq, sq, cube, cube, sq, sq,
            pl.BlockSpec((1, 8, LANES), lambda b: (b, 0, 0)),
            pl.BlockSpec((1, 2 * STATE, E), lambda b: (b, 0, 0)),
            whole((2, PAY, E)),
        ],
        out_shape=[
            flat, flat, deep, deep, flat, flat,
            jax.ShapeDtypeStruct((nb, 8, LANES), F32),
            jax.ShapeDtypeStruct((nb, 2 * STATE, E), BF16),
            jax.ShapeDtypeStruct((2, PAY, E), BF16),
        ],
        scratch_shapes=[
            pltpu.VMEM((2 * LANES, 2 * E), BF16),
            pltpu.VMEM((2 * STATE, E), F32),
            pltpu.VMEM((8, LANES), F32),
            pltpu.VMEM((STRETCH, 2 * E), BF16),
        ],
        compiler_params=params(12),
        cost_estimate=cost(4e9, 12 << 20),
        name="block_states",
    )(act, dtraw, hp)


def from_others(me, got_ref, upward):
    n = got_ref.shape[0] + 1
    side = lambda d: (d < me) if upward else (d > me)
    total = jnp.zeros((STATE, E), F32)
    for q in range(1, n):
        d = jnp.bitwise_xor(me, q)
        log = jnp.zeros((1, E), F32)
        for k in range(1, n):
            if k != q:
                e = jnp.bitwise_xor(me, k)
                between = ((d < e) & (e < me)) if upward else ((me < e) & (e < d))
                row = got_ref[k - 1, STATE : STATE + 1, :].astype(F32)
                log = log + jnp.where(between, row, 0.0)
        term = jnp.exp2(log) * got_ref[q - 1, :STATE, :].astype(F32)
        total = total + jnp.where(side(d), term, 0.0)
    return total


MAPS = slice(E, E + LANES), slice(E + LANES, E + 2 * LANES)


def split_store(ref, cols, value):
    hi = value.astype(BF16)
    ref[:, cols] = hi
    ref[:, shifted(cols)] = (value - hi.astype(F32)).astype(BF16)


def gate_kernel(
    me_ref, act_ref, z_ref, dg_ref, u_ref, vt_ref, eu_ref, s_ref, got_ref, tot_ref, rows_ref,
    gated_ref, dz_ref, dy_ref, yz_ref, gain_ref, ent_ref, p_ref, pay_ref, skip_ref,
    exp_ref, heads_ref, dev_ref, cum_ref, e_ref, y_ref, yv_ref, prod_ref, sums_ref, state_ref,
):
    b = pl.program_id(0)
    nb = pl.num_programs(0)

    @pl.when(b == 0)
    def _():
        fill_expand(exp_ref)
        fill_heads(heads_ref)
        dev_ref[...] = jnp.zeros_like(dev_ref)
        cum_ref[...] = jnp.zeros_like(cum_ref)
        sums_ref[...] = jnp.zeros_like(sums_ref)
        me = me_ref[0]
        state_ref[...] = from_others(me, got_ref, True)
        scan_states(ent_ref, state_ref, tot_ref, s_ref, 0, False)
        state_ref[...] = from_others(me, got_ref, False)
        scan_states(ent_ref, state_ref, tot_ref, s_ref, HEADS, True)

    sq = (STRETCH, STRETCH)
    i, j = iota(sq, 0), iota(sq, 1)
    after_j, at = i > j, i >= j
    lower = jnp.where(after_j, 1.0, 0.0).astype(BF16)
    upper = jnp.where(at, 0.0, 1.0).astype(BF16)
    bm, cm = act_ref[:, MAPS[0]], act_ref[:, MAPS[1]]
    cf, cr = cm[:, :STATE], cm[:, STATE:]
    gram = jnp.where(after_j, dot_nt(cf, bm[:, :STATE]), jnp.where(at, 0.0, dot_nt(cr, bm[:, STATE:])))
    left = iota((STRETCH, LANES), 1) < HDIM

    e2 = two_parts(eu_ref[...])
    for cols in CHUNKS:
        for c, state in ((cf, ent_ref[b, :STATE, cols]), (cr, ent_ref[b, STATE:, cols])):
            at_cols = cols if c is cf else shifted(cols)
            e = dot(e2, exp_ref[:, at_cols])
            e_ref[:, at_cols] = e
            y_ref[:, at_cols] = e * dot(c, state)

    square = jnp.zeros((STRETCH, LANES), F32)
    cross = jnp.zeros((STRETCH, LANES), F32)
    for p, cols in enumerate(PAIR_COLS):
        mats = []
        for h in (2 * p, 2 * p + 1):
            r = HEADS + h
            row = jnp.where(at, u_ref[:, h : h + 1], u_ref[:, r : r + 1])
            col = jnp.where(after_j, vt_ref[0, h : h + 1, :], vt_ref[0, r : r + 1, :])
            mats.append((jnp.exp2(row + col) * gram).astype(BF16))
        mats = [m * lower for m in mats] + [m * upper for m in mats]
        y = dot(jnp.concatenate(mats, axis=0), act_ref[:, cols])
        yf = y_ref[:, cols] + jnp.where(left, y[:STRETCH], y[STRETCH : 2 * STRETCH])
        yr = y_ref[:, shifted(cols)] + jnp.where(left, y[2 * STRETCH : 3 * STRETCH], y[3 * STRETCH :])
        y_ref[:, cols] = yf
        y_ref[:, shifted(cols)] = yr
        mixed = (yf + yr).astype(BF16).astype(F32)
        yv = mixed + rows_ref[0:1, cols] * act_ref[:, cols].astype(F32)
        yv_ref[:, cols] = yv
        z = z_ref[:, cols].astype(F32)
        yg = yv * (z * jax.nn.sigmoid(z))
        square = square + yg * yg
        cross = cross + rows_ref[1:2, cols] * dg_ref[:, cols].astype(F32) * yg
    inv = lax.rsqrt(jnp.sum(square, axis=1, keepdims=True) / E + EPSILON)
    back = inv * inv * inv * (jnp.sum(cross, axis=1, keepdims=True) / E)

    for p, cols in enumerate(PAIR_COLS):
        z = z_ref[:, cols].astype(F32)
        sig = jax.nn.sigmoid(z)
        ga = z * sig
        yv = yv_ref[:, cols]
        yg = yv * ga
        gain = rows_ref[1:2, cols]
        gated_ref[:, cols] = (yg * inv * gain).astype(BF16)
        dyg = inv * (gain * dg_ref[:, cols].astype(F32)) - yg * back
        dy = dyg * ga
        dz_ref[:, cols] = (dyg * yv * (sig + ga * (1.0 - sig))).astype(BF16)
        low_dy = dy.astype(BF16)
        dy_ref[:, cols] = low_dy
        fold = lambda t: jnp.sum(t.reshape(STRETCH // 8, 8, LANES), axis=0)
        sums_ref[:, cols] = sums_ref[:, cols] + fold(dy * act_ref[:, cols].astype(F32))
        dy = low_dy.astype(F32)
        yz_ref[:, cols] = (e_ref[:, cols] * dy).astype(BF16)
        yz_ref[:, shifted(cols)] = (e_ref[:, shifted(cols)] * dy).astype(BF16)
        split_store(prod_ref, cols, y_ref[:, cols] * dy)
        split_store(prod_ref, slice(cols.start + 2 * E, cols.stop + 2 * E), y_ref[:, shifted(cols)] * dy)
    gain_ref[...] = dot(prod_ref[...], heads_ref[...])

    total8 = tot_ref[b]
    dec = jnp.exp2(total8)
    pre = jnp.exp2(cum_ref[...])
    ct = cm.T
    for c, cols in enumerate(CHUNKS):
        pf = dot(ct[:STATE], yz_ref[:, cols])
        pr = dot(ct[STATE:], yz_ref[:, shifted(cols)])
        p_ref[0, :STATE, cols] = pf.astype(BF16)
        p_ref[0, STATE:, cols] = pr.astype(BF16)
        pre_f = jnp.concatenate([pair_rows(pre, 2 * c, 0), pair_rows(pre, 2 * c + 1, 0)], axis=1)
        dec_r = jnp.concatenate([pair_rows(dec, 2 * c, HEADS), pair_rows(dec, 2 * c + 1, HEADS)], axis=1)
        dev_ref[:STATE, cols] = dev_ref[:STATE, cols] + pre_f[0:1] * pf
        dev_ref[STATE:, cols] = dec_r[0:1] * dev_ref[STATE:, cols] + pr
    cum_ref[...] = cum_ref[...] + total8

    @pl.when(b == nb - 1)
    def _():
        write_payload(pay_ref, dev_ref, cum_ref)
        skip_ref[...] = lax.dot_general(
            sums_ref[...], exp_ref[:LANES, :E].astype(F32), NT,
            precision=lax.Precision.HIGHEST, preferred_element_type=F32,
        )


def gate(me, act, z, dg, u, vt, eu, s, got, tot, rows):
    length = act.shape[0]
    nb = length // STRETCH
    line = pl.BlockSpec((STRETCH, E), lambda b: (b, 0))
    sq = pl.BlockSpec((STRETCH, LANES), lambda b: (b, 0))
    low_line = jax.ShapeDtypeStruct((length, E), BF16)
    return pl.pallas_call(
        gate_kernel,
        grid=(nb,),
        in_specs=[
            pl.BlockSpec(memory_space=pltpu.SMEM),
            pl.BlockSpec((STRETCH, CHANNELS), lambda b: (b, 0)),
            line,
            line,
            sq,
            pl.BlockSpec((1, LANES, STRETCH), lambda b: (b, 0, 0)),
            sq,
            whole(s.shape),
            whole(got.shape),
            whole(tot.shape),
            whole((8, E)),
        ],
        out_specs=[
            line,
            line,
            line,
            pl.BlockSpec((STRETCH, 2 * E), lambda b: (b, 0)),
            sq,
            whole(s.shape),
            pl.BlockSpec((1, 2 * STATE, E), lambda b: (b, 0, 0)),
            whole((2, PAY, E)),
            whole((8, LANES)),
        ],
        out_shape=[
            low_line,
            low_line,
            low_line,
            jax.ShapeDtypeStruct((length, 2 * E), BF16),
            jax.ShapeDtypeStruct((length, LANES), F32),
            jax.ShapeDtypeStruct(s.shape, BF16),
            jax.ShapeDtypeStruct(s.shape, BF16),
            jax.ShapeDtypeStruct((2, PAY, E), BF16),
            jax.ShapeDtypeStruct((8, LANES), F32),
        ],
        scratch_shapes=[
            pltpu.VMEM((2 * LANES, 2 * E), BF16),
            pltpu.VMEM((4 * E, LANES), BF16),
            pltpu.VMEM((2 * STATE, E), F32),
            pltpu.VMEM((8, LANES), F32),
            pltpu.VMEM((STRETCH, 2 * E), F32),
            pltpu.VMEM((STRETCH, 2 * E), F32),
            pltpu.VMEM((STRETCH, E), F32),
            pltpu.VMEM((STRETCH, 4 * E), BF16),
            pltpu.VMEM((8, E), F32),
            pltpu.VMEM((STATE, E), F32),
        ],
        compiler_params=params(30),
        cost_estimate=cost(16e9, 32 << 20),
        name="gate",
    )(me, act, z, dg, u, vt, eu, s, got, tot, rows)


def mixer_back_kernel(
    me_ref, act_ref, dy_ref, yz_ref, v_ref, ut_ref, wv_ref, gain_ref, ent_ref, p_ref, got_ref, tot_ref,
    dtraw_ref, hp_ref,
    dx_ref, dmap_ref, ddt_ref, sums_ref,
    exp_ref, heads_ref, out_ref, v_in_ref, xz_ref, prod_ref, state_ref, row_ref,
):
    b = pl.program_id(0)
    sq = (STRETCH, STRETCH)
    j, i = iota(sq, 0), iota(sq, 1)
    after_j, at = i > j, i >= j

    @pl.when(b == 0)
    def _():
        fill_expand(exp_ref)
        fill_heads(heads_ref)
        sums_ref[...] = jnp.zeros_like(sums_ref)
        row_ref[...] = jnp.zeros_like(row_ref)
        me = me_ref[0]
        state_ref[...] = from_others(me, got_ref, False)
        scan_states(out_ref, state_ref, tot_ref, p_ref, 0, True)
        state_ref[...] = from_others(me, got_ref, True)
        scan_states(out_ref, state_ref, tot_ref, p_ref, HEADS, False)

    bm, cm = act_ref[:, MAPS[0]], act_ref[:, MAPS[1]]
    bf, br, cf, cr = bm[:, :STATE], bm[:, STATE:], cm[:, :STATE], cm[:, STATE:]
    gram = jnp.where(after_j, dot_nt(bf, cf), jnp.where(at, 0.0, dot_nt(br, cr)))
    lower = jnp.where(after_j, 1.0, 0.0).astype(BF16)
    upper = jnp.where(at, 0.0, 1.0).astype(BF16)
    left = iota((STRETCH, LANES), 1) < HDIM

    w2 = two_parts(wv_ref[...])
    for cols in CHUNKS:
        x = act_ref[:, cols].astype(F32)
        for k, m, state in ((0, bf, out_ref[b, :STATE, cols]), (1, br, out_ref[b, STATE:, cols])):
            at_cols = cols if k == 0 else shifted(cols)
            w = dot(w2, exp_ref[:, at_cols])
            v_in = w * dot(m, state)
            v_in_ref[:, at_cols] = v_in
            xz_ref[:, at_cols] = (w * x).astype(BF16)
            row_ref[k : k + 1, cols] = jnp.sum(v_in * x, axis=0, keepdims=True)
    p_out, s_in = out_ref[b], ent_ref[0]
    db_f = dot_nt(xz_ref[:, :E], p_out[:STATE])
    db_r = dot_nt(xz_ref[:, E:], p_out[STATE:])
    dc_f = dot_nt(yz_ref[:, :E], s_in[:STATE])
    dc_r = dot_nt(yz_ref[:, E:], s_in[STATE:])

    dgram = jnp.zeros(sq, F32)
    for p, cols in enumerate(PAIR_COLS):
        x = act_ref[:, cols].astype(F32)
        dyb = dy_ref[:, cols]
        x2 = jnp.concatenate([jnp.where(left, x, 0.0), jnp.where(left, 0.0, x)], axis=0).astype(BF16)
        dm = dot_nt(x2, dyb)
        mats = []
        for k, h in enumerate((2 * p, 2 * p + 1)):
            r = HEADS + h
            row = jnp.where(after_j, v_ref[:, h : h + 1], v_ref[:, r : r + 1])
            col = jnp.where(at, ut_ref[0, h : h + 1, :], ut_ref[0, r : r + 1, :])
            decay = jnp.exp2(row + col)
            mats.append((decay * gram).astype(BF16))
            dgram = dgram + dm[k * STRETCH : (k + 1) * STRETCH] * decay
        mats = [m * lower for m in mats] + [m * upper for m in mats]
        d4 = dot(jnp.concatenate(mats, axis=0), dyb)
        vf = v_in_ref[:, cols] + jnp.where(left, d4[:STRETCH], d4[STRETCH : 2 * STRETCH])
        vr = v_in_ref[:, shifted(cols)] + jnp.where(left, d4[2 * STRETCH : 3 * STRETCH], d4[3 * STRETCH :])
        dx_ref[:, cols] = (vf + vr).astype(BF16)
        split_store(prod_ref, cols, vf * x)
        split_store(prod_ref, slice(cols.start + 2 * E, cols.stop + 2 * E), vr * x)
    dlog = dot(prod_ref[...], heads_ref[...])

    gfwd = jnp.where(after_j, dgram, 0.0).astype(BF16)
    grev = jnp.where(at, 0.0, dgram).astype(BF16)
    gfwd_t = gfwd.T
    grev_t = grev.T
    dmap_ref[:, :LANES] = jnp.concatenate([db_f + dot(gfwd, cf), db_r + dot(grev, cr)], axis=1)
    dmap_ref[:, LANES:] = jnp.concatenate([dc_f + dot(gfwd_t, bf), dc_r + dot(grev_t, br)], axis=1)

    pe = p_out.astype(F32) * s_in.astype(F32)
    col_sum = lambda t: jnp.sum(t, axis=0, keepdims=True)
    row_ref[2:3, :] = col_sum(pe[:STATE])
    row_ref[3:4, :] = col_sum(pe[STATE:])
    sums = row_ref[...]
    hi = sums.astype(BF16)
    lo = (sums - hi.astype(F32)).astype(BF16)
    f_heads, r_heads = heads_ref[:E], heads_ref[2 * E : 3 * E]
    on_f = dot(hi, f_heads) + dot(lo, f_heads)
    on_r = dot(hi, r_heads) + dot(lo, r_heads)
    through = jnp.exp2(tot_ref[b])[0:1] * (on_f[2:3] + on_r[3:4]) + on_f[0:1] + on_r[1:2]
    lane = iota((STRETCH, LANES), 1)
    forward = lane < HEADS
    gain = gain_ref[...]
    both = jnp.concatenate([gain, dlog], axis=1)
    top = both.astype(BF16)
    rest = both - top.astype(F32)
    mid = rest.astype(BF16)
    end = (rest - mid.astype(F32)).astype(BF16)
    later = dot(lower, top) + dot(lower, mid) + dot(lower, end)
    later_gain, later_dlog = later[:, :LANES], later[:, LANES:]
    dlg = jnp.where(
        forward,
        later_gain - later_dlog - dlog,
        (col_sum(gain) - later_gain - gain) - (col_sum(dlog) - later_dlog),
    )
    dlg = dlg + through
    pre, dt, lg = step_sizes(dtraw_ref[...], hp_ref)
    dtb = dt.astype(BF16).astype(F32)
    ok = (dtb > 0.0) & (lane < 2 * HEADS)
    ddt = jnp.where(ok, dlog / jnp.where(ok, dtb, 1.0), 0.0)
    ddt = ddt.astype(BF16).astype(F32)
    dlg = jnp.where(lane < 2 * HEADS, dlg, 0.0).astype(BF16).astype(F32)
    draw = (ddt + dlg * hp_ref[1:2, :]) * jax.nn.sigmoid(pre)
    ddt_ref[...] = draw.astype(BF16)
    fold = lambda t: jnp.sum(t.reshape(STRETCH // 8, 8, LANES), axis=0)
    sums_ref[0:8] = sums_ref[0:8] + fold(draw)
    sums_ref[8:16] = sums_ref[8:16] + fold(dlg * lg)


def mixer_back(me, act, dy, yz, v, ut, wv, gain, ent, p, got, tot, dtraw, hp):
    length = act.shape[0]
    nb = length // STRETCH
    sq = pl.BlockSpec((STRETCH, LANES), lambda b: (b, 0))
    line = pl.BlockSpec((STRETCH, E), lambda b: (b, 0))
    states = pl.BlockSpec((1, 2 * STATE, E), lambda b: (b, 0, 0))
    return pl.pallas_call(
        mixer_back_kernel,
        grid=(nb,),
        in_specs=[
            pl.BlockSpec(memory_space=pltpu.SMEM),
            pl.BlockSpec((STRETCH, CHANNELS), lambda b: (b, 0)),
            line,
            pl.BlockSpec((STRETCH, 2 * E), lambda b: (b, 0)),
            sq,
            pl.BlockSpec((1, LANES, STRETCH), lambda b: (b, 0, 0)),
            sq,
            sq,
            states,
            whole(p.shape),
            whole(got.shape),
            whole(tot.shape),
            sq,
            whole((8, LANES)),
        ],
        out_specs=[
            line,
            pl.BlockSpec((STRETCH, 2 * LANES), lambda b: (b, 0)),
            sq,
            whole((16, LANES)),
        ],
        out_shape=[
            jax.ShapeDtypeStruct((length, E), BF16),
            jax.ShapeDtypeStruct((length, 2 * LANES), F32),
            jax.ShapeDtypeStruct((length, LANES), BF16),
            jax.ShapeDtypeStruct((16, LANES), F32),
        ],
        scratch_shapes=[
            pltpu.VMEM((2 * LANES, 2 * E), BF16),
            pltpu.VMEM((4 * E, LANES), BF16),
            pltpu.VMEM(p.shape, BF16),
            pltpu.VMEM((STRETCH, 2 * E), F32),
            pltpu.VMEM((STRETCH, 2 * E), BF16),
            pltpu.VMEM((STRETCH, 4 * E), BF16),
            pltpu.VMEM((STATE, E), F32),
            pltpu.VMEM((8, E), F32),
        ],
        compiler_params=params(26),
        cost_estimate=cost(16e9, 20 << 20),
        name="mixer_back",
    )(me, act, dy, yz, v, ut, wv, gain, ent, p, got, tot, dtraw, hp)


def conv_back_block(length, dact_ref, slope_ref, conv_ref, taps_ref, dconv_ref, sums_ref, dpad_ref, edge_ref, shift_ref):
    half = TAPS // 2
    fold = lambda t: jnp.sum(t.reshape(t.shape[0] // 8, 8, BLOCK), axis=0)
    sums = [jnp.zeros((8, BLOCK), F32) for _ in range(TAPS + 1)]
    zeros = jnp.zeros((MARGIN, BLOCK), BF16)
    dpad_ref[:MARGIN] = zeros
    dpad_ref[MARGIN + length :] = zeros
    for c in range(length // STRETCH):
        rows = slice(c * STRETCH, (c + 1) * STRETCH)
        dpre = dact_ref[rows] * slope_ref[rows].astype(F32)
        sums[TAPS] = sums[TAPS] + fold(dpre)
        dpad_ref[MARGIN + rows.start : MARGIN + rows.stop] = dpre.astype(BF16)
    for c in range(length // STRETCH):
        rows = slice(c * STRETCH, (c + 1) * STRETCH)
        x = conv_ref[rows].astype(F32)
        out = jnp.zeros((STRETCH, BLOCK), F32)
        for k, moved in shifted_rows(shift_ref, dpad_ref, rows.start).items():
            out = out + taps_ref[k : k + 1, :] * moved
            sums[k] = sums[k] + fold(x * moved)
        dconv_ref[rows] = out.astype(BF16)
    edge_ref[: 2 * MARGIN] = dpad_ref[: 2 * MARGIN].astype(F32)
    edge_ref[2 * MARGIN :] = dpad_ref[length:].astype(F32)
    edges = []
    for where, base in ((0, MARGIN - EDGE), (1, 3 * MARGIN)):
        first = length + where * EDGE
        x = conv_ref[length:].astype(F32)[where * EDGE : (where + 1) * EDGE]
        out = jnp.zeros((EDGE, BLOCK), F32)
        for k in range(TAPS):
            moved = edge_ref[base - k + half : base - k + half + EDGE]
            out = out + taps_ref[k : k + 1, :] * moved
            sums[k] = sums[k] + x * moved
        edges.append(out)
    dconv_ref[length:] = jnp.concatenate(edges, axis=0).astype(BF16)
    sums_ref[...] = jnp.concatenate([jnp.sum(t, axis=0, keepdims=True) for t in sums], axis=0)


def conv_back_kernel(
    dx_ref, dy_ref, dmap_ref, slope_ref, conv_ref, taps_ref, skip_ref, ddt_ref, hsum_ref, ssum_ref,
    dconv_ref, sums_ref, dact_ref, dpad_ref, edge_ref, shift_ref,
):
    j = pl.program_id(0)
    maps = E // BLOCK
    length = slope_ref.shape[0]

    @pl.when(j == 0)
    def _():
        fill_shifts(shift_ref, -1)

    @pl.when(j < maps)
    def _():
        dact_ref[...] = dx_ref[...].astype(F32) + skip_ref[0:1, :] * dy_ref[...].astype(F32)

    @pl.when(j == maps)
    def _():
        dact_ref[...] = dmap_ref[...]

    @pl.when(j <= maps)
    def _():
        conv_back_block(
            length, dact_ref, slope_ref, conv_ref, taps_ref, dconv_ref, sums_ref, dpad_ref, edge_ref, shift_ref
        )

    @pl.when(j > maps)
    def _():
        dconv_ref[:length, :LANES] = ddt_ref[...]
        dconv_ref[length:, :LANES] = jnp.zeros((2 * EDGE, LANES), BF16)
        parts = [hsum_ref[:8], hsum_ref[8:], ssum_ref[...]]
        parts = [jnp.sum(t, axis=0, keepdims=True) for t in parts]
        sums_ref[:, :LANES] = jnp.concatenate(parts + [jnp.zeros((5, LANES), F32)], axis=0)


def conv_back(dx, dy, dmap, slope, conv, taps, skip, ddt, hsums, ssums):
    ext = conv.shape[0]
    length = ext - 2 * EDGE
    early = lambda j: (0, jnp.minimum(j, E // BLOCK - 1))
    inner = lambda j: (0, jnp.minimum(j, CHANNELS // BLOCK - 1))
    col = lambda j: (0, j)
    return pl.pallas_call(
        conv_back_kernel,
        grid=(CHANNELS // BLOCK + 1,),
        in_specs=[
            pl.BlockSpec((length, BLOCK), early),
            pl.BlockSpec((length, BLOCK), early),
            whole((length, 2 * LANES)),
            pl.BlockSpec((length, BLOCK), inner),
            pl.BlockSpec((ext, BLOCK), inner),
            pl.BlockSpec((8, BLOCK), inner),
            pl.BlockSpec((8, BLOCK), early),
            whole((length, LANES)),
            whole((16, LANES)),
            whole((8, LANES)),
        ],
        out_specs=[pl.BlockSpec((ext, BLOCK), col), pl.BlockSpec((8, BLOCK), col)],
        out_shape=[
            jax.ShapeDtypeStruct((ext, WIDE), BF16),
            jax.ShapeDtypeStruct((8, WIDE), F32),
        ],
        scratch_shapes=[
            pltpu.VMEM((length, BLOCK), F32),
            pltpu.VMEM((length + 2 * MARGIN, BLOCK), BF16),
            pltpu.VMEM((4 * MARGIN, BLOCK), F32),
            pltpu.VMEM((len(SHIFTS) * STRETCH, WINDOW), BF16),
        ],
        compiler_params=params(14),
        cost_estimate=cost(2e9, 20 << 20),
        name="conv_back",
    )(dx, dy, dmap, slope, conv, taps, skip, ddt, hsums, ssums)


def send_states(payload, to_later):
    n, me = lax.axis_size("seq"), lax.axis_index("seq")
    sent, got = [], []
    for q in range(1, n):
        later = (me ^ q) > me
        first = later if to_later else ~later
        sent.append(jnp.where(first, payload[0], payload[1]))
        got.append(swap(sent[-1], "seq", q))
    return sent, got


def per_device(
    layer_in, norm_gain, in_weight, conv_weight, conv_bias, head_params, out_gain, out_weight, out_cotangent
):
    ns, nw = lax.axis_size("seq"), lax.axis_size("wt")
    ndev = ns * nw
    seq_me = lax.axis_index("seq").astype(jnp.int32)
    me = seq_me * nw + lax.axis_index("wt").astype(jnp.int32)
    me_arr, seq_arr = me.reshape(1), seq_me.reshape(1)
    tokens = layer_in[0]
    cotangent = out_cotangent[0]
    length, d = tokens.shape
    share = in_weight.shape[0]
    cshare = conv_bias.shape[0]
    gshare = out_gain.shape[0]
    spare = WIDE - (in_weight.shape[1] - E)

    forward = [(i, i + 1) for i in range(ns - 1)]
    backward = [(i + 1, i) for i in range(ns - 1)]
    before = lax.ppermute(tokens[length - EDGE :], "seq", forward)
    behind = lax.ppermute(tokens[:EDGE], "seq", backward)
    ext = jnp.concatenate([tokens, before, behind], axis=0)

    small = jnp.concatenate([conv_weight.reshape(-1), conv_bias, out_gain, norm_gain])
    n_small = small.shape[0]
    small = jnp.pad(small, (0, 8 * LANES - n_small)).reshape(8, LANES)
    first = jnp.pad(in_weight[:, E:], ((0, 0), (0, spare)))
    half = E // 2
    rest = jnp.concatenate(
        [in_weight[None, :, :half], in_weight[None, :, half:E], out_weight.reshape(2, share, d)], axis=0
    )
    a1 = jnp.stack(gather_z(first))
    b1 = gather_z(after(rest, a1))
    s1 = jnp.stack(gather_z(small))
    a2 = jnp.stack(gather_seq(after(a1, before, behind, s1)))
    s2 = jnp.stack(gather_seq(s1))
    b1 = jnp.stack(b1)
    b2 = gather_seq(after(b1, a2))
    wa, wb = a2.reshape(d // 2, WIDE), swap(after(a2, b1), "wt", 1).reshape(d // 2, WIDE)

    blocks = jnp.arange(d, dtype=jnp.int32) // share
    offsets = block_order(ns, nw)
    offset_of = jnp.array(offsets, jnp.int32)
    natural = (offset_of[blocks] ^ me) * share + jnp.arange(d, dtype=jnp.int32) % share
    perm = (jnp.arange(d, dtype=jnp.int32)[:, None] == natural[None, :]).astype(BF16)
    u_x = dot(ext, perm)
    inv_in = lax.rsqrt(jnp.mean(jnp.square(ext.astype(F32)), axis=1, keepdims=True) + EPSILON)

    extras = jnp.stack([s2, swap(s2, "wt", 1)]).reshape(ndev, 8 * LANES)
    order = jnp.arange(ndev, dtype=jnp.int32)[:, None] == (offset_of[None, :] ^ me)
    nat = dot(order.astype(BF16), extras[:, :n_small])
    taps = jnp.transpose(nat[:, : TAPS * cshare].reshape(ndev, TAPS, cshare), (1, 0, 2)).reshape(TAPS, CHANNELS)
    bias = nat[:, TAPS * cshare : (TAPS + 1) * cshare].reshape(1, CHANNELS)
    taps = jnp.concatenate([taps, bias], axis=0)
    gain_out = nat[:, (TAPS + 1) * cshare : (TAPS + 1) * cshare + gshare].reshape(1, E)
    gain_x = extras[:, n_small - share : n_small].reshape(1, d).astype(F32)

    normed = (u_x * inv_in * gain_x).astype(BF16)
    conv, act, slope, dtraw = conv_forward(normed, wa, wb, taps)

    twice = jnp.concatenate([head_params, head_params], axis=1)
    rates = jnp.stack([twice[0], -jnp.exp(twice[1])])
    hp = jnp.pad(rates, ((0, 6), (0, LANES - 2 * HEADS)))
    b2 = jnp.stack([after(t, dtraw) for t in b2]).reshape(2 * ndev, share, half)
    b3 = swap(b2, "wt", 1)
    u, v, ut, vt, eu, wv, tot, s, pay = block_states(act, dtraw, hp)
    sent, got = send_states(pay, True)
    w_z, w_out = unpack(offsets, me_arr, b2, after(b3, *sent))
    w_z, w_out = w_z.reshape(d, E), w_out.reshape(E, d)
    own = normed[:length]
    z = dot(own, w_z).astype(BF16)
    dgated = dot_nt(cotangent, w_out).astype(BF16)
    skip = jnp.repeat(head_params[2], HDIM)[None]
    rows = jnp.concatenate([skip, gain_out, jnp.zeros((6, E), F32)], axis=0)
    got = jnp.stack([after(t, z, dgated) for t in got])
    gated, dz, dy, yz, gain, ent, p, pay, ssums = gate(seq_arr, act, z, dgated, u, vt, eu, s, got, tot, rows)
    sent, got = send_states(pay, False)

    gated_then, dz_then = after(gated, *sent), after(dz, *sent)
    g_out = lax.dot_general(gated_then, cotangent, TN, preferred_element_type=F32).astype(BF16)
    g_z = lax.dot_general(own, dz_then, TN, preferred_element_type=F32).astype(BF16)
    dn_z = dot_nt(dz_then, w_z)
    layer_out = (tokens.astype(F32) + dot(gated_then, w_out)).astype(BF16)[None]
    got = jnp.stack([after(t, g_out, g_z, dn_z, layer_out) for t in got])
    kept, moved = pack(offsets, me_arr, g_z.reshape(ndev, share, E), g_out.reshape(2 * ndev, share, d))
    moved = swap(moved, "wt", 1)
    dx, dmap, ddt, hsums = mixer_back(
        seq_arr, act, after(dy, kept), yz, v, ut, wv, gain, ent, p, got, tot, dtraw, hp
    )
    split = lambda t: t.reshape(ns, nw // 2, 4, share, half)
    r1 = scatter_core(split(kept), split(after(moved, dx)))
    dconv, csums = conv_back(after(dx, *r1), dy, dmap, slope, conv, taps, rows, ddt, hsums, ssums)

    g_c = lax.dot_general(normed, dconv, TN, preferred_element_type=F32).astype(BF16)
    g_c = g_c.reshape(2, ns, nw // 2, share, WIDE)
    r2 = scatter_seq(r1)
    sent = after(g_c[1], *r2)
    f1 = scatter_core(g_c[0], swap(sent, "wt", 1))
    w_first = jnp.concatenate([wa, wb])
    dn = dot_nt(after(dconv, sent), w_first)
    f_got = [swap(f1[q], "seq", q) for q in range(1, ns)]
    f2 = scatter_seq(f1, f_got)
    dn = dn + jnp.concatenate([dn_z, jnp.zeros((2 * EDGE, d), F32)], axis=0)
    grad_first = scatter_z(f2)
    r3 = scatter_z(r2, *f2)
    csums = sum_everywhere(csums, f_got[0], f_got[(ns - 1) // 2], f_got[-1])

    dn = after(dn, *f2)
    dn_hi = dn.astype(BF16)
    dn_lo = (dn - dn_hi.astype(F32)).astype(BF16)
    dn = dot_nt(dn_hi, perm) + dot_nt(dn_lo, perm)
    prev_edge = lax.ppermute(dn[length : length + EDGE], "seq", backward)
    next_edge = lax.ppermute(dn[length + EDGE :], "seq", forward)
    middle = jnp.zeros((length - 2 * EDGE, d), F32)
    dn = dn[:length] + jnp.concatenate([next_edge, middle, prev_edge], axis=0)
    u, inv = tokens.astype(F32), inv_in[:length]
    scaled = nat[:, n_small - share :].reshape(1, d) * dn
    in_grad = cotangent.astype(F32) + inv * scaled
    in_grad = in_grad - u * inv**3 * jnp.mean(scaled * u, axis=1, keepdims=True)

    grad_z = jnp.concatenate([r3[0], r3[1]], axis=1)
    grad_out = r3[2:].reshape(gshare, d)
    vec = lax.dynamic_slice(csums, (0, me * cshare), (8, cshare))
    pair = csums[:3, CHANNELS : CHANNELS + 2 * HEADS]
    head_grad = pair[:, :HEADS] + pair[:, HEADS:]
    grad_in = jnp.concatenate([grad_z, grad_first[:, : WIDE - spare]], axis=1)
    gain_grad = jnp.sum(in_weight.astype(F32) * grad_in, axis=1) / norm_gain.astype(F32)
    out_gain_grad = jnp.sum(out_weight.astype(F32) * grad_out, axis=1) / out_gain.astype(F32)
    return (
        layer_out,
        in_grad[None],
        gain_grad,
        grad_in,
        vec[:TAPS],
        vec[TAPS],
        head_grad,
        out_gain_grad,
        grad_out,
    )


def solution(mesh):
    rows = P(("seq", "wt"))
    table = P(("seq", "wt"), None)
    tokens = P("wt", "seq", None)
    taps = P(None, ("seq", "wt"))
    return jax.shard_map(
        per_device,
        mesh=mesh,
        in_specs=(tokens, rows, table, taps, rows, P(), rows, table, tokens),
        out_specs=(tokens, tokens, rows, table, taps, rows, P(), rows, table),
        check_vma=False,
    )
```

```python
import functools

import jax
import jax.numpy as jnp
from jax import lax
from jax.experimental import pallas as pl
from jax.experimental.pallas import tpu as pltpu
from jax.sharding import PartitionSpec as P

HEADS = 24
HDIM = 64
STATE = 64
STRETCH = 128
TAPS = 7
E = 1536
CHANNELS = 1792
PAIRS = HEADS // 2
LANES = 128
WIDE = 1920
EDGE = 8
EPSILON = 1e-05
LOG2E = 1.4426950408889634

F32 = jnp.float32
BF16 = jnp.bfloat16
NT = (((1,), (1,)), ((), ()))
TN = (((0,), (0,)), ((), ()))


def dot(a, b):
    return jnp.dot(a, b, preferred_element_type=F32)


def dot_nt(a, b):
    return lax.dot_general(a, b, NT, preferred_element_type=F32)


def params(limit=56):
    return pltpu.CompilerParams(vmem_limit_bytes=limit << 20)


def cost(flops, moved, trans=0):
    return pl.CostEstimate(flops=int(flops), bytes_accessed=int(moved), transcendentals=int(trans))


def whole(shape):
    return pl.BlockSpec(shape, lambda *_: (0,) * len(shape), pipeline_mode=pl.Buffered(1))


def swap(x, axis, q):
    n = lax.axis_size(axis)
    return lax.ppermute(x, axis, [(i, i ^ q) for i in range(n)])


def gather_z(x):
    return [x] + [swap(x, "wt", 2 * q) for q in range(1, lax.axis_size("wt") // 2)]


def gather_seq(x):
    return [x] + [swap(x, "seq", q) for q in range(1, lax.axis_size("seq"))]


def block_order(ns, nw):
    return [s * nw + 2 * z + c for c in range(2) for s in range(ns) for z in range(nw // 2)]


def low(t):
    return t.astype(BF16)


def up(t):
    return t.astype(F32)


def scatter_core(kept, got):
    return [low(up(kept[q]) + up(got[q])) for q in range(kept.shape[0])]


def scatter_seq(a, got=None):
    if got is None:
        got = [swap(a[q], "seq", q) for q in range(1, len(a))]
    total = lambda z: sum((up(t[z]) for t in got), up(a[0][z]))
    return [low(total(z)) for z in range(a[0].shape[0])]


def scatter_z(b, got=None):
    if got is None:
        got = [swap(b[q], "wt", 2 * q) for q in range(1, len(b))]
    return sum((up(t) for t in got), up(b[0]))


def tree_sum(parts):
    while len(parts) > 1:
        parts = [parts[i] + parts[i + 1] for i in range(0, len(parts), 2)]
    return parts[0]


def sum_everywhere(x, first, middle, last):
    ns, nw = lax.axis_size("seq"), lax.axis_size("wt")
    x = after(x, *first)
    x = tree_sum([x] + [after(swap(x, "wt", 2 * q), *middle) for q in range(1, nw // 2)])
    x = x + swap(x, "wt", 1)
    x = after(x, *last)
    return tree_sum([x] + [swap(x, "seq", q) for q in range(1, ns)])


def after(x, *others):
    return lax.optimization_barrier((x, *others))[0]


def unpack_kernel(order, me_ref, a_ref, b_ref, z_ref, o_ref):
    half = a_ref.shape[2]
    count = a_ref.shape[0] // 4
    for p, offset in enumerate(order):
        x_ref, k = (a_ref, 4 * p) if p < count else (b_ref, 4 * (p - count))
        z_ref[p, :, :half] = x_ref[k]
        z_ref[p, :, half:] = x_ref[k + 1]
        target = 2 * jnp.bitwise_xor(me_ref[0], offset)
        o_ref[target] = x_ref[k + 2]
        o_ref[target + 1] = x_ref[k + 3]


def unpack(order, me, a, b):
    n, share, half = a.shape
    shapes = [(n // 2, share, 2 * half), (n, share, half)]
    return pl.pallas_call(
        functools.partial(unpack_kernel, order),
        grid=(1,),
        out_shape=[jax.ShapeDtypeStruct(s, a.dtype) for s in shapes],
        in_specs=[pl.BlockSpec(memory_space=pltpu.SMEM), whole(a.shape), whole(b.shape)],
        out_specs=[whole(s) for s in shapes],
        compiler_params=params(12),
        cost_estimate=cost(0, 8 * a.size),
        name="unpack",
    )(me, a, b)


def pack_kernel(order, me_ref, z_ref, o_ref, a_ref, b_ref):
    half = a_ref.shape[2]
    count = a_ref.shape[0] // 4
    for p, offset in enumerate(order):
        x_ref, k = (a_ref, 4 * p) if p < count else (b_ref, 4 * (p - count))
        x_ref[k] = z_ref[p, :, :half]
        x_ref[k + 1] = z_ref[p, :, half:]
        source = 2 * jnp.bitwise_xor(me_ref[0], offset)
        x_ref[k + 2] = o_ref[source]
        x_ref[k + 3] = o_ref[source + 1]


def pack(order, me, z, o):
    n, share, wide = z.shape
    shape = (2 * n, share, wide // 2)
    return pl.pallas_call(
        functools.partial(pack_kernel, order),
        grid=(1,),
        out_shape=[jax.ShapeDtypeStruct(shape, z.dtype)] * 2,
        in_specs=[pl.BlockSpec(memory_space=pltpu.SMEM), whole(z.shape), whole(o.shape)],
        out_specs=[whole(shape)] * 2,
        compiler_params=params(12),
        cost_estimate=cost(0, 8 * z.size),
        name="pack",
    )(me, z, o)


BLOCK = 256


SHIFTS = [k for k in range(TAPS) if k != TAPS // 2]
MARGIN = 16
WINDOW = STRETCH + 2 * MARGIN


def fill_shifts(shift_ref, sign):
    for n, k in enumerate(SHIFTS):
        picked = iota((STRETCH, WINDOW), 0) + (MARGIN + sign * (k - TAPS // 2))
        same = iota((STRETCH, WINDOW), 1) == picked
        shift_ref[n * STRETCH : (n + 1) * STRETCH, :] = jnp.where(same, 1.0, 0.0).astype(BF16)


def shifted_rows(shift_ref, pad_ref, first):
    rows = dot(shift_ref[...], pad_ref[first : first + WINDOW, :])
    out = {k: rows[n * STRETCH : (n + 1) * STRETCH] for n, k in enumerate(SHIFTS)}
    out[TAPS // 2] = pad_ref[first + MARGIN : first + MARGIN + STRETCH, :].astype(F32)
    return out


def conv_kernel(
    nx_ref, wa_ref, wb_ref, da_ref, db_ref, taps_ref, conv_ref, act_ref, slope_ref, dt_ref, pad_ref, shift_ref
):
    length = act_ref.shape[0]

    @pl.when(pl.program_id(0) == 0)
    def _():
        fill_shifts(shift_ref, 1)
        pad_ref[...] = jnp.zeros_like(pad_ref)

    w = jnp.concatenate([wa_ref[...], wb_ref[...]], axis=0)
    zeros = jnp.zeros((EDGE, BLOCK), BF16)
    r = dot(nx_ref[length:], w).astype(BF16)
    conv_ref[length:] = r
    pad_ref[:MARGIN] = jnp.concatenate([zeros, r[:EDGE]], axis=0)
    pad_ref[MARGIN + length :] = jnp.concatenate([r[EDGE:], zeros], axis=0)
    count = length // STRETCH
    for c in range(count + 1):
        if c < count:
            rows = slice(c * STRETCH, (c + 1) * STRETCH)
            r = dot(nx_ref[rows], w).astype(BF16)
            conv_ref[rows] = r
            pad_ref[MARGIN + rows.start : MARGIN + rows.stop] = r
        if c > 0:
            first = (c - 1) * STRETCH
            pre = jnp.broadcast_to(taps_ref[TAPS : TAPS + 1, :], (STRETCH, BLOCK))
            for k, x in shifted_rows(shift_ref, pad_ref, first).items():
                pre = pre + taps_ref[k : k + 1, :] * x
            sig = jax.nn.sigmoid(pre)
            act = pre * sig
            rows = slice(first, first + STRETCH)
            act_ref[rows] = act.astype(BF16)
            slope_ref[rows] = (sig + act * (1.0 - sig)).astype(BF16)

    @pl.when(pl.program_id(0) == pl.num_programs(0) - 1)
    def _():
        w = jnp.concatenate([da_ref[...], db_ref[...]], axis=0)
        dt_ref[...] = dot(nx_ref[:length], w)


def conv_forward(normed, wa, wb, taps):
    ext, d = normed.shape
    length = ext - 2 * EDGE
    col = lambda j: (0, j)
    steps = pl.BlockSpec((d // 2, LANES), lambda j: (0, CHANNELS // LANES))
    return pl.pallas_call(
        conv_kernel,
        grid=(CHANNELS // BLOCK,),
        in_specs=[
            whole((ext, d)),
            pl.BlockSpec((d // 2, BLOCK), col),
            pl.BlockSpec((d // 2, BLOCK), col),
            steps,
            steps,
            pl.BlockSpec((8, BLOCK), col),
        ],
        out_specs=[
            pl.BlockSpec((ext, BLOCK), col),
            pl.BlockSpec((length, BLOCK), col),
            pl.BlockSpec((length, BLOCK), col),
            whole((length, LANES)),
        ],
        out_shape=[
            hbm((ext, CHANNELS), BF16),
            hbm((length, CHANNELS), BF16),
            hbm((length, CHANNELS), BF16),
            jax.ShapeDtypeStruct((length, LANES), F32),
        ],
        scratch_shapes=[
            pltpu.VMEM((length + 2 * MARGIN, BLOCK), BF16),
            pltpu.VMEM((len(SHIFTS) * STRETCH, WINDOW), BF16),
        ],
        compiler_params=params(14),
        cost_estimate=cost(2 * ext * d * WIDE, 16 << 20),
        name="conv_forward",
    )(normed, wa, wb, wa, wb, taps)


def hbm(shape, kind):
    return pltpu.HBM(shape, kind)


def in_hbm(x):
    return pltpu.with_memory_space_constraint(x, pltpu.HBM)


def iota(shape, dim):
    return lax.broadcasted_iota(jnp.int32, shape, dim)


def fill_expand(exp_ref):
    for c in range(2 * E // LANES):
        row = jnp.bitwise_and(iota((2 * LANES, LANES), 0), LANES - 1)
        head = 2 * c + jnp.where(iota((2 * LANES, LANES), 1) >= HDIM, 1, 0)
        exp_ref[:, c * LANES : (c + 1) * LANES] = jnp.where(row == head, 1.0, 0.0).astype(BF16)


def fill_heads(heads_ref):
    for c in range(2 * PAIRS):
        row = iota((LANES, LANES), 0)
        head = 2 * (c % PAIRS) + jnp.where(row >= HDIM, 1, 0)
        head = head + jnp.where(jnp.bitwise_and(row, HDIM - 1) >= HDIM // 2, HEADS, 0)
        same = iota((LANES, LANES), 1) == head
        heads_ref[c * LANES : (c + 1) * LANES, :] = jnp.where(same, 1.0, 0.0).astype(BF16)


def fold_pair(f, r, first):
    half = HDIM // 2
    return jnp.where(first, f + pltpu.roll(f, LANES - half, 1), r + pltpu.roll(r, half, 1))


def two_parts(x):
    hi = x.astype(BF16)
    lo = (x - hi.astype(F32)).astype(BF16)
    return jnp.concatenate([hi, lo], axis=1)


CHUNKS = [slice(c * 2 * LANES, (c + 1) * 2 * LANES) for c in range(E // (2 * LANES))]
PAIR_COLS = [slice(p * LANES, (p + 1) * LANES) for p in range(PAIRS)]


def shifted(cols):
    return slice(cols.start + E, cols.stop + E)


def pair_rows(row, p, first):
    h = first + 2 * p
    left = iota((8, LANES), 1) < HDIM
    return jnp.where(left, row[:, h : h + 1], row[:, h + 1 : h + 2])


def scan_states(out_ref, state_ref, tot_ref, add_ref, first, backward):
    rows = slice(0, STATE) if first == 0 else slice(STATE, 2 * STATE)
    order = range(add_ref.shape[0])
    for c in reversed(order) if backward else order:
        dec = jnp.exp2(tot_ref[c])
        for p, cols in enumerate(PAIR_COLS):
            state = state_ref[:, cols]
            out_ref[c, rows, cols] = state.astype(BF16)
            state_ref[:, cols] = pair_rows(dec, p, first)[0:1] * state + add_ref[c, rows, cols].astype(F32)


def step_sizes(dtraw, hp_ref):
    lane = iota(dtraw.shape, 1)
    pre = jnp.where(lane < 2 * HEADS, dtraw + hp_ref[0:1, :], 0.0)
    dt = jnp.maximum(pre, 0.0) + jnp.log1p(jnp.exp(-jnp.abs(pre)))
    return pre, dt, hp_ref[1:2, :] * dt


def states_kernel(
    act_ref, dtraw_ref, hp_ref, u_ref, v_ref, ut_ref, vt_ref, eu_ref, wv_ref, tot_ref, s_ref, pay_ref,
    exp_ref, dev_ref, cum_ref, z_ref,
):
    b = pl.program_id(0)
    nb = pl.num_programs(0)

    @pl.when(b == 0)
    def _():
        fill_expand(exp_ref)
        dev_ref[...] = jnp.zeros_like(dev_ref)
        cum_ref[...] = jnp.zeros_like(cum_ref)

    sq = (STRETCH, LANES)
    lane = iota(sq, 1)
    forward = lane < HEADS
    _, dt, lg = step_sizes(dtraw_ref[...], hp_ref)
    dtb = dt.astype(BF16).astype(F32)
    lgb = lg.astype(BF16)
    upto = jnp.where(iota(sq, 0) >= iota(sq, 1), 1.0, 0.0).astype(BF16)
    run = dot(upto, lgb)
    before = run - lgb.astype(F32)
    total = run[STRETCH - 1 : STRETCH, :] * LOG2E
    logdt = jnp.where(dtb > 0.0, jnp.log(jnp.where(dtb > 0.0, dtb, 1.0)) * LOG2E, -1e30)
    u = jnp.where(forward, before, -run) * LOG2E
    v = jnp.where(forward, -run, before) * LOG2E + logdt
    u_ref[...] = u
    v_ref[...] = v
    ut_ref[0] = u.T
    vt_ref[0] = v.T
    eu = jnp.exp2(u + jnp.where(forward, 0.0, total))
    wv = jnp.exp2(v + jnp.where(forward, total, 0.0))
    eu_ref[...] = eu
    wv_ref[...] = wv
    total8 = jnp.broadcast_to(total, (8, LANES))
    tot_ref[0] = total8

    bt = act_ref[:, E : E + LANES].T
    w2 = two_parts(wv)
    for cols in CHUNKS:
        x = act_ref[:, cols].astype(F32)
        z_ref[:, cols] = (x * dot(w2, exp_ref[:, cols])).astype(BF16)
        z_ref[:, shifted(cols)] = (x * dot(w2, exp_ref[:, shifted(cols)])).astype(BF16)
    dec = jnp.exp2(total8)
    pre = jnp.exp2(cum_ref[...])
    for c, cols in enumerate(CHUNKS):
        sf = dot(bt[:STATE], z_ref[:, cols])
        sr = dot(bt[STATE:], z_ref[:, shifted(cols)])
        s_ref[0, :STATE, cols] = sf.astype(BF16)
        s_ref[0, STATE:, cols] = sr.astype(BF16)
        dec_f = jnp.concatenate([pair_rows(dec, 2 * c, 0), pair_rows(dec, 2 * c + 1, 0)], axis=1)
        pre_r = jnp.concatenate([pair_rows(pre, 2 * c, HEADS), pair_rows(pre, 2 * c + 1, HEADS)], axis=1)
        dev_ref[:STATE, cols] = dec_f[0:1] * dev_ref[:STATE, cols] + sf
        dev_ref[STATE:, cols] = dev_ref[STATE:, cols] + pre_r[0:1] * sr
    cum_ref[...] = cum_ref[...] + total8

    @pl.when(b == nb - 1)
    def _():
        write_payload(pay_ref, dev_ref, cum_ref)


def write_payload(pay_ref, dev_ref, cum_ref):
    cum = cum_ref[...]
    pay_ref[0, :STATE] = dev_ref[:STATE].astype(BF16)
    pay_ref[1, :STATE] = dev_ref[STATE:].astype(BF16)
    for k in range(2):
        for p, cols in enumerate(PAIR_COLS):
            row = pair_rows(cum, p, k * HEADS)
            pay_ref[k, STATE:, cols] = jnp.concatenate([row, row], axis=0).astype(BF16)


PAY = STATE + 16


def block_states(act, dtraw, hp):
    length = act.shape[0]
    nb = length // STRETCH
    sq = pl.BlockSpec((STRETCH, LANES), lambda b: (b, 0))
    cube = pl.BlockSpec((1, STRETCH, LANES), lambda b: (b, 0, 0))
    flat = jax.ShapeDtypeStruct((length, LANES), F32)
    deep = jax.ShapeDtypeStruct((nb, LANES, STRETCH), F32)
    return pl.pallas_call(
        states_kernel,
        grid=(nb,),
        in_specs=[pl.BlockSpec((STRETCH, CHANNELS), lambda b: (b, 0)), sq, whole((8, LANES))],
        out_specs=[
            sq, sq, cube, cube, sq, sq,
            pl.BlockSpec((1, 8, LANES), lambda b: (b, 0, 0)),
            pl.BlockSpec((1, 2 * STATE, E), lambda b: (b, 0, 0)),
            whole((2, PAY, E)),
        ],
        out_shape=[
            flat, flat, deep, deep, flat, flat,
            jax.ShapeDtypeStruct((nb, 8, LANES), F32),
            jax.ShapeDtypeStruct((nb, 2 * STATE, E), BF16),
            jax.ShapeDtypeStruct((2, PAY, E), BF16),
        ],
        scratch_shapes=[
            pltpu.VMEM((2 * LANES, 2 * E), BF16),
            pltpu.VMEM((2 * STATE, E), F32),
            pltpu.VMEM((8, LANES), F32),
            pltpu.VMEM((STRETCH, 2 * E), BF16),
        ],
        compiler_params=params(12),
        cost_estimate=cost(4e9, 12 << 20),
        name="block_states",
    )(in_hbm(act), dtraw, hp)


def from_others(me, got_ref, upward):
    n = got_ref.shape[0] + 1
    side = lambda d: (d < me) if upward else (d > me)
    total = jnp.zeros((STATE, E), F32)
    for q in range(1, n):
        d = jnp.bitwise_xor(me, q)
        log = jnp.zeros((1, E), F32)
        for k in range(1, n):
            if k != q:
                e = jnp.bitwise_xor(me, k)
                between = ((d < e) & (e < me)) if upward else ((me < e) & (e < d))
                row = got_ref[k - 1, STATE : STATE + 1, :].astype(F32)
                log = log + jnp.where(between, row, 0.0)
        term = jnp.exp2(log) * got_ref[q - 1, :STATE, :].astype(F32)
        total = total + jnp.where(side(d), term, 0.0)
    return total


MAPS = slice(E, E + LANES), slice(E + LANES, E + 2 * LANES)


def split_store(ref, rows, cols, value):
    hi = value.astype(BF16)
    ref[rows, cols] = hi
    ref[rows, shifted(cols)] = (value - hi.astype(F32)).astype(BF16)


def sigmoid(x):
    return 0.5 * jnp.tanh(0.5 * x) + 0.5


def gate_kernel(
    me_ref, act_ref, z_ref, dg_ref, u_ref, vt_ref, eu_ref, s_ref, got_ref, tot_ref, rows_ref,
    gated_ref, dz_ref, dy_ref, yz_ref, gain_ref, ent_ref, p_ref, pay_ref, skip_ref,
    exp_ref, heads_ref, dev_ref, cum_ref, e_ref, y_ref, yv_ref, sig_ref, prod_ref, sums_ref, state_ref,
):
    b = pl.program_id(0)
    nb = pl.num_programs(0)

    @pl.when(b == 0)
    def _():
        fill_expand(exp_ref)
        fill_heads(heads_ref)
        dev_ref[...] = jnp.zeros_like(dev_ref)
        cum_ref[...] = jnp.zeros_like(cum_ref)
        sums_ref[...] = jnp.zeros_like(sums_ref)
        me = me_ref[0]
        state_ref[...] = from_others(me, got_ref, True)
        scan_states(ent_ref, state_ref, tot_ref, s_ref, 0, False)
        state_ref[...] = from_others(me, got_ref, False)
        scan_states(ent_ref, state_ref, tot_ref, s_ref, HEADS, True)

    sq = (STRETCH, STRETCH)
    i, j = iota(sq, 0), iota(sq, 1)
    after_j, at = i > j, i >= j
    lower = jnp.where(after_j, 1.0, 0.0).astype(BF16)
    upper = jnp.where(at, 0.0, 1.0).astype(BF16)
    bm, cm = act_ref[:, MAPS[0]], act_ref[:, MAPS[1]]
    cf, cr = cm[:, :STATE], cm[:, STATE:]
    gram = jnp.where(after_j, dot_nt(cf, bm[:, :STATE]), jnp.where(at, 0.0, dot_nt(cr, bm[:, STATE:])))
    left = iota((STRETCH, LANES), 1) < HDIM
    first_half = jnp.bitwise_and(iota((STRETCH, LANES), 1), HDIM - 1) < HDIM // 2

    e2 = two_parts(eu_ref[...])
    for cols in CHUNKS:
        for c, state in ((cf, ent_ref[b, :STATE, cols]), (cr, ent_ref[b, STATE:, cols])):
            at_cols = cols if c is cf else shifted(cols)
            e = dot(e2, exp_ref[:, at_cols])
            e_ref[:, at_cols] = e
            y_ref[:, at_cols] = e * dot(c, state)

    square = jnp.zeros((STRETCH, LANES), F32)
    cross = jnp.zeros((STRETCH, LANES), F32)
    for p, cols in enumerate(PAIR_COLS):
        mats = []
        for h in (2 * p, 2 * p + 1):
            r = HEADS + h
            row = jnp.where(at, u_ref[:, h : h + 1], u_ref[:, r : r + 1])
            col = jnp.where(after_j, vt_ref[0, h : h + 1, :], vt_ref[0, r : r + 1, :])
            mats.append((jnp.exp2(row + col) * gram).astype(BF16))
        mats = [m * lower for m in mats] + [m * upper for m in mats]
        y = dot(jnp.concatenate(mats, axis=0), act_ref[:, cols])
        yf = y_ref[:, cols] + jnp.where(left, y[:STRETCH], y[STRETCH : 2 * STRETCH])
        yr = y_ref[:, shifted(cols)] + jnp.where(left, y[2 * STRETCH : 3 * STRETCH], y[3 * STRETCH :])
        y_ref[:, cols] = yf
        y_ref[:, shifted(cols)] = yr
        yv = yf + yr + rows_ref[0:1, cols] * act_ref[:, cols].astype(F32)
        yv_ref[:, cols] = yv
        z = z_ref[:, cols].astype(F32)
        sig = sigmoid(z)
        sig_ref[:, cols] = sig
        yg = yv * (z * sig)
        square = square + yg * yg
        cross = cross + rows_ref[1:2, cols] * dg_ref[:, cols].astype(F32) * yg
    inv = lax.rsqrt(jnp.sum(square, axis=1, keepdims=True) / E + EPSILON)
    back = inv * inv * inv * (jnp.sum(cross, axis=1, keepdims=True) / E)

    for p, cols in enumerate(PAIR_COLS):
        z = z_ref[:, cols].astype(F32)
        sig = sig_ref[:, cols]
        ga = z * sig
        yv = yv_ref[:, cols]
        yg = yv * ga
        gain = rows_ref[1:2, cols]
        gated_ref[:, cols] = (yg * inv * gain).astype(BF16)
        dyg = inv * (gain * dg_ref[:, cols].astype(F32)) - yg * back
        dy = dyg * ga
        dz_ref[:, cols] = (dyg * yv * (sig + ga * (1.0 - sig))).astype(BF16)
        low_dy = dy.astype(BF16)
        dy_ref[:, cols] = low_dy
        fold = lambda t: jnp.sum(t.reshape(STRETCH // 8, 8, LANES), axis=0)
        sums_ref[:, cols] = sums_ref[:, cols] + fold(dy * act_ref[:, cols].astype(F32))
        dy = low_dy.astype(F32)
        yz_ref[:, cols] = (e_ref[:, cols] * dy).astype(BF16)
        yz_ref[:, shifted(cols)] = (e_ref[:, shifted(cols)] * dy).astype(BF16)
        pair = fold_pair(y_ref[:, cols] * dy, y_ref[:, shifted(cols)] * dy, first_half)
        split_store(prod_ref, slice(None), cols, pair)
    gain_ref[...] = dot(prod_ref[...], heads_ref[...])

    total8 = tot_ref[b]
    dec = jnp.exp2(total8)
    pre = jnp.exp2(cum_ref[...])
    ct = cm.T
    for c, cols in enumerate(CHUNKS):
        pf = dot(ct[:STATE], yz_ref[:, cols])
        pr = dot(ct[STATE:], yz_ref[:, shifted(cols)])
        p_ref[0, :STATE, cols] = pf.astype(BF16)
        p_ref[0, STATE:, cols] = pr.astype(BF16)
        pre_f = jnp.concatenate([pair_rows(pre, 2 * c, 0), pair_rows(pre, 2 * c + 1, 0)], axis=1)
        dec_r = jnp.concatenate([pair_rows(dec, 2 * c, HEADS), pair_rows(dec, 2 * c + 1, HEADS)], axis=1)
        dev_ref[:STATE, cols] = dev_ref[:STATE, cols] + pre_f[0:1] * pf
        dev_ref[STATE:, cols] = dec_r[0:1] * dev_ref[STATE:, cols] + pr
    cum_ref[...] = cum_ref[...] + total8

    @pl.when(b == nb - 1)
    def _():
        write_payload(pay_ref, dev_ref, cum_ref)
        skip_ref[...] = lax.dot_general(
            sums_ref[...], exp_ref[:LANES, :E].astype(F32), NT,
            precision=lax.Precision.HIGHEST, preferred_element_type=F32,
        )


def gate(me, act, z, dg, u, vt, eu, s, got, tot, rows):
    length = act.shape[0]
    nb = length // STRETCH
    line = pl.BlockSpec((STRETCH, E), lambda b: (b, 0))
    sq = pl.BlockSpec((STRETCH, LANES), lambda b: (b, 0))
    low_line = jax.ShapeDtypeStruct((length, E), BF16)
    return pl.pallas_call(
        gate_kernel,
        grid=(nb,),
        in_specs=[
            pl.BlockSpec(memory_space=pltpu.SMEM),
            pl.BlockSpec((STRETCH, CHANNELS), lambda b: (b, 0)),
            line,
            line,
            sq,
            pl.BlockSpec((1, LANES, STRETCH), lambda b: (b, 0, 0)),
            sq,
            whole(s.shape),
            whole(got.shape),
            whole(tot.shape),
            whole((8, E)),
        ],
        out_specs=[
            line,
            line,
            line,
            pl.BlockSpec((STRETCH, 2 * E), lambda b: (b, 0)),
            sq,
            whole(s.shape),
            pl.BlockSpec((1, 2 * STATE, E), lambda b: (b, 0, 0)),
            whole((2, PAY, E)),
            whole((8, LANES)),
        ],
        out_shape=[
            low_line,
            low_line,
            low_line,
            jax.ShapeDtypeStruct((length, 2 * E), BF16),
            jax.ShapeDtypeStruct((length, LANES), F32),
            jax.ShapeDtypeStruct(s.shape, BF16),
            jax.ShapeDtypeStruct(s.shape, BF16),
            jax.ShapeDtypeStruct((2, PAY, E), BF16),
            jax.ShapeDtypeStruct((8, LANES), F32),
        ],
        scratch_shapes=[
            pltpu.VMEM((2 * LANES, 2 * E), BF16),
            pltpu.VMEM((2 * E, LANES), BF16),
            pltpu.VMEM((2 * STATE, E), F32),
            pltpu.VMEM((8, LANES), F32),
            pltpu.VMEM((STRETCH, 2 * E), F32),
            pltpu.VMEM((STRETCH, 2 * E), F32),
            pltpu.VMEM((STRETCH, E), F32),
            pltpu.VMEM((STRETCH, E), F32),
            pltpu.VMEM((STRETCH, 2 * E), BF16),
            pltpu.VMEM((8, E), F32),
            pltpu.VMEM((STATE, E), F32),
        ],
        compiler_params=params(30),
        cost_estimate=cost(16e9, 32 << 20),
        name="gate",
    )(me, in_hbm(act), z, dg, u, vt, eu, s, got, tot, rows)


def mixer_back_kernel(
    me_ref, act_ref, dy_ref, yz_ref, v_ref, ut_ref, wv_ref, gain_ref, ent_ref, p_ref, got_ref, tot_ref,
    dtraw_ref, hp_ref,
    dx_ref, dmap_ref, ddt_ref, sums_ref,
    exp_ref, heads_ref, out_ref, v_in_ref, xz_ref, prod_ref, state_ref, row_ref,
):
    b = pl.program_id(0)
    sq = (STRETCH, STRETCH)
    j, i = iota(sq, 0), iota(sq, 1)
    after_j, at = i > j, i >= j

    @pl.when(b == 0)
    def _():
        fill_expand(exp_ref)
        fill_heads(heads_ref)
        sums_ref[...] = jnp.zeros_like(sums_ref)
        row_ref[...] = jnp.zeros_like(row_ref)
        me = me_ref[0]
        state_ref[...] = from_others(me, got_ref, False)
        scan_states(out_ref, state_ref, tot_ref, p_ref, 0, True)
        state_ref[...] = from_others(me, got_ref, True)
        scan_states(out_ref, state_ref, tot_ref, p_ref, HEADS, False)

    bm, cm = act_ref[:, MAPS[0]], act_ref[:, MAPS[1]]
    bf, br, cf, cr = bm[:, :STATE], bm[:, STATE:], cm[:, :STATE], cm[:, STATE:]
    gram = jnp.where(after_j, dot_nt(bf, cf), jnp.where(at, 0.0, dot_nt(br, cr)))
    lower = jnp.where(after_j, 1.0, 0.0).astype(BF16)
    upper = jnp.where(at, 0.0, 1.0).astype(BF16)
    left = iota((STRETCH, LANES), 1) < HDIM
    first_half = jnp.bitwise_and(iota((STRETCH, LANES), 1), HDIM - 1) < HDIM // 2
    left_low = jnp.where(left, 1.0, 0.0).astype(BF16)
    right_low = jnp.where(left, 0.0, 1.0).astype(BF16)

    w2 = two_parts(wv_ref[...])
    for cols in CHUNKS:
        x = act_ref[:, cols].astype(F32)
        for k, m, state in ((0, bf, out_ref[b, :STATE, cols]), (1, br, out_ref[b, STATE:, cols])):
            at_cols = cols if k == 0 else shifted(cols)
            w = dot(w2, exp_ref[:, at_cols])
            v_in = w * dot(m, state)
            v_in_ref[:, at_cols] = v_in
            xz_ref[:, at_cols] = (w * x).astype(BF16)
            row_ref[k : k + 1, cols] = jnp.sum(v_in * x, axis=0, keepdims=True)
    p_out, s_in = out_ref[b], ent_ref[0]
    db_f = dot_nt(xz_ref[:, :E], p_out[:STATE])
    db_r = dot_nt(xz_ref[:, E:], p_out[STATE:])
    dc_f = dot_nt(yz_ref[:, :E], s_in[:STATE])
    dc_r = dot_nt(yz_ref[:, E:], s_in[STATE:])

    dgram = jnp.zeros(sq, F32)
    for p, cols in enumerate(PAIR_COLS):
        xb, dyb = act_ref[:, cols], dy_ref[:, cols]
        x = xb.astype(F32)
        dm = dot_nt(jnp.concatenate([xb * left_low, xb * right_low], axis=0), dyb)
        mats = []
        for k, h in enumerate((2 * p, 2 * p + 1)):
            r = HEADS + h
            row = jnp.where(after_j, v_ref[:, h : h + 1], v_ref[:, r : r + 1])
            col = jnp.where(at, ut_ref[0, h : h + 1, :], ut_ref[0, r : r + 1, :])
            decay = jnp.exp2(row + col)
            mats.append((decay * gram).astype(BF16))
            dgram = dgram + dm[k * STRETCH : (k + 1) * STRETCH] * decay
        mats = [m * lower for m in mats] + [m * upper for m in mats]
        d4 = dot(jnp.concatenate(mats, axis=0), dyb)
        vf = v_in_ref[:, cols] + jnp.where(left, d4[:STRETCH], d4[STRETCH : 2 * STRETCH])
        vr = v_in_ref[:, shifted(cols)] + jnp.where(left, d4[2 * STRETCH : 3 * STRETCH], d4[3 * STRETCH :])
        dx_ref[:, cols] = (vf + vr).astype(BF16)
        split_store(prod_ref, slice(0, STRETCH), cols, fold_pair(vf * x, vr * x, first_half))
    pe = p_out.astype(F32) * s_in.astype(F32)
    col_sum = lambda t: jnp.sum(t, axis=0, keepdims=True)
    row_ref[2:3, :] = col_sum(pe[:STATE])
    row_ref[3:4, :] = col_sum(pe[STATE:])
    for cols in PAIR_COLS:
        f = jnp.concatenate([row_ref[0:1, cols], row_ref[2:3, cols], jnp.zeros((14, LANES), F32)], axis=0)
        r = jnp.concatenate([row_ref[1:2, cols], row_ref[3:4, cols], jnp.zeros((14, LANES), F32)], axis=0)
        split_store(prod_ref, slice(STRETCH, STRETCH + 16), cols, fold_pair(f, r, first_half[:16]))
    sums = dot(prod_ref[...], heads_ref[...])
    dlog = sums[:STRETCH]
    through = sums[STRETCH : STRETCH + 1] + jnp.exp2(tot_ref[b])[0:1] * sums[STRETCH + 1 : STRETCH + 2]

    gfwd = jnp.where(after_j, dgram, 0.0).astype(BF16)
    grev = jnp.where(at, 0.0, dgram).astype(BF16)
    gfwd_t = gfwd.T
    grev_t = grev.T
    dmap_ref[:, :LANES] = jnp.concatenate([db_f + dot(gfwd, cf), db_r + dot(grev, cr)], axis=1)
    dmap_ref[:, LANES:] = jnp.concatenate([dc_f + dot(gfwd_t, bf), dc_r + dot(grev_t, br)], axis=1)

    lane = iota((STRETCH, LANES), 1)
    forward = lane < HEADS
    gain = gain_ref[...]
    both = jnp.concatenate([gain, dlog], axis=1)
    top = both.astype(BF16)
    rest = both - top.astype(F32)
    mid = rest.astype(BF16)
    end = (rest - mid.astype(F32)).astype(BF16)
    later = dot(lower, top) + dot(lower, mid) + dot(lower, end)
    later_gain, later_dlog = later[:, :LANES], later[:, LANES:]
    dlg = jnp.where(
        forward,
        later_gain - later_dlog - dlog,
        (col_sum(gain) - later_gain - gain) - (col_sum(dlog) - later_dlog),
    )
    dlg = dlg + through
    pre, dt, lg = step_sizes(dtraw_ref[...], hp_ref)
    dtb = dt.astype(BF16).astype(F32)
    ok = (dtb > 0.0) & (lane < 2 * HEADS)
    ddt = jnp.where(ok, dlog / jnp.where(ok, dtb, 1.0), 0.0)
    ddt = ddt.astype(BF16).astype(F32)
    dlg = jnp.where(lane < 2 * HEADS, dlg, 0.0).astype(BF16).astype(F32)
    draw = (ddt + dlg * hp_ref[1:2, :]) * jax.nn.sigmoid(pre)
    ddt_ref[...] = draw.astype(BF16)
    fold = lambda t: jnp.sum(t.reshape(STRETCH // 8, 8, LANES), axis=0)
    sums_ref[0:8] = sums_ref[0:8] + fold(draw)
    sums_ref[8:16] = sums_ref[8:16] + fold(dlg * lg)


def mixer_back(me, act, dy, yz, v, ut, wv, gain, ent, p, got, tot, dtraw, hp):
    length = act.shape[0]
    nb = length // STRETCH
    sq = pl.BlockSpec((STRETCH, LANES), lambda b: (b, 0))
    line = pl.BlockSpec((STRETCH, E), lambda b: (b, 0))
    states = pl.BlockSpec((1, 2 * STATE, E), lambda b: (b, 0, 0))
    return pl.pallas_call(
        mixer_back_kernel,
        grid=(nb,),
        in_specs=[
            pl.BlockSpec(memory_space=pltpu.SMEM),
            pl.BlockSpec((STRETCH, CHANNELS), lambda b: (b, 0)),
            line,
            pl.BlockSpec((STRETCH, 2 * E), lambda b: (b, 0)),
            sq,
            pl.BlockSpec((1, LANES, STRETCH), lambda b: (b, 0, 0)),
            sq,
            sq,
            states,
            whole(p.shape),
            whole(got.shape),
            whole(tot.shape),
            sq,
            whole((8, LANES)),
        ],
        out_specs=[
            line,
            pl.BlockSpec((STRETCH, 2 * LANES), lambda b: (b, 0)),
            sq,
            whole((16, LANES)),
        ],
        out_shape=[
            jax.ShapeDtypeStruct((length, E), BF16),
            jax.ShapeDtypeStruct((length, 2 * LANES), F32),
            jax.ShapeDtypeStruct((length, LANES), BF16),
            jax.ShapeDtypeStruct((16, LANES), F32),
        ],
        scratch_shapes=[
            pltpu.VMEM((2 * LANES, 2 * E), BF16),
            pltpu.VMEM((2 * E, LANES), BF16),
            pltpu.VMEM(p.shape, BF16),
            pltpu.VMEM((STRETCH, 2 * E), F32),
            pltpu.VMEM((STRETCH, 2 * E), BF16),
            pltpu.VMEM((STRETCH + 16, 2 * E), BF16),
            pltpu.VMEM((STATE, E), F32),
            pltpu.VMEM((8, E), F32),
        ],
        compiler_params=params(26),
        cost_estimate=cost(16e9, 20 << 20),
        name="mixer_back",
    )(me, in_hbm(act), dy, yz, v, ut, wv, gain, ent, p, got, tot, dtraw, hp)


def conv_back_block(length, dact_ref, slope_ref, conv_ref, taps_ref, dconv_ref, sums_ref, dpad_ref, edge_ref, shift_ref):
    half = TAPS // 2
    fold = lambda t: jnp.sum(t.reshape(t.shape[0] // 8, 8, BLOCK), axis=0)
    sums = [jnp.zeros((8, BLOCK), F32) for _ in range(TAPS + 1)]
    zeros = jnp.zeros((MARGIN, BLOCK), BF16)
    dpad_ref[:MARGIN] = zeros
    dpad_ref[MARGIN + length :] = zeros
    for c in range(length // STRETCH):
        rows = slice(c * STRETCH, (c + 1) * STRETCH)
        dpre = dact_ref[rows] * slope_ref[rows].astype(F32)
        sums[TAPS] = sums[TAPS] + fold(dpre)
        dpad_ref[MARGIN + rows.start : MARGIN + rows.stop] = dpre.astype(BF16)
    for c in range(length // STRETCH):
        rows = slice(c * STRETCH, (c + 1) * STRETCH)
        x = conv_ref[rows].astype(F32)
        out = jnp.zeros((STRETCH, BLOCK), F32)
        for k, moved in shifted_rows(shift_ref, dpad_ref, rows.start).items():
            out = out + taps_ref[k : k + 1, :] * moved
            sums[k] = sums[k] + fold(x * moved)
        dconv_ref[rows] = out.astype(BF16)
    edge_ref[: 2 * MARGIN] = dpad_ref[: 2 * MARGIN].astype(F32)
    edge_ref[2 * MARGIN :] = dpad_ref[length:].astype(F32)
    edges = []
    for where, base in ((0, MARGIN - EDGE), (1, 3 * MARGIN)):
        first = length + where * EDGE
        x = conv_ref[length:].astype(F32)[where * EDGE : (where + 1) * EDGE]
        out = jnp.zeros((EDGE, BLOCK), F32)
        for k in range(TAPS):
            moved = edge_ref[base - k + half : base - k + half + EDGE]
            out = out + taps_ref[k : k + 1, :] * moved
            sums[k] = sums[k] + x * moved
        edges.append(out)
    dconv_ref[length:] = jnp.concatenate(edges, axis=0).astype(BF16)
    sums_ref[...] = jnp.concatenate([jnp.sum(t, axis=0, keepdims=True) for t in sums], axis=0)


def conv_back_kernel(
    dx_ref, dy_ref, dmap_ref, slope_ref, conv_ref, taps_ref, skip_ref, ddt_ref, hsum_ref, ssum_ref,
    dconv_ref, sums_ref, dact_ref, dpad_ref, edge_ref, shift_ref,
):
    j = pl.program_id(0)
    maps = E // BLOCK
    length = slope_ref.shape[0]

    @pl.when(j == 0)
    def _():
        fill_shifts(shift_ref, -1)

    @pl.when(j < maps)
    def _():
        dact_ref[...] = dx_ref[...].astype(F32) + skip_ref[0:1, :] * dy_ref[...].astype(F32)

    @pl.when(j == maps)
    def _():
        dact_ref[...] = dmap_ref[...]

    @pl.when(j <= maps)
    def _():
        conv_back_block(
            length, dact_ref, slope_ref, conv_ref, taps_ref, dconv_ref, sums_ref, dpad_ref, edge_ref, shift_ref
        )

    @pl.when(j > maps)
    def _():
        dconv_ref[:length, :LANES] = ddt_ref[...]
        dconv_ref[length:, :LANES] = jnp.zeros((2 * EDGE, LANES), BF16)
        parts = [hsum_ref[:8], hsum_ref[8:], ssum_ref[...]]
        parts = [jnp.sum(t, axis=0, keepdims=True) for t in parts]
        sums_ref[:, :LANES] = jnp.concatenate(parts + [jnp.zeros((5, LANES), F32)], axis=0)


def conv_back(dx, dy, dmap, slope, conv, taps, skip, ddt, hsums, ssums):
    ext = conv.shape[0]
    length = ext - 2 * EDGE
    early = lambda j: (0, jnp.minimum(j, E // BLOCK - 1))
    inner = lambda j: (0, jnp.minimum(j, CHANNELS // BLOCK - 1))
    col = lambda j: (0, j)
    return pl.pallas_call(
        conv_back_kernel,
        grid=(CHANNELS // BLOCK + 1,),
        in_specs=[
            pl.BlockSpec((length, BLOCK), early),
            pl.BlockSpec((length, BLOCK), early),
            whole((length, 2 * LANES)),
            pl.BlockSpec((length, BLOCK), inner),
            pl.BlockSpec((ext, BLOCK), inner),
            pl.BlockSpec((8, BLOCK), inner),
            pl.BlockSpec((8, BLOCK), early),
            whole((length, LANES)),
            whole((16, LANES)),
            whole((8, LANES)),
        ],
        out_specs=[pl.BlockSpec((ext, BLOCK), col), pl.BlockSpec((8, BLOCK), col)],
        out_shape=[
            jax.ShapeDtypeStruct((ext, WIDE), BF16),
            jax.ShapeDtypeStruct((8, WIDE), F32),
        ],
        scratch_shapes=[
            pltpu.VMEM((length, BLOCK), F32),
            pltpu.VMEM((length + 2 * MARGIN, BLOCK), BF16),
            pltpu.VMEM((4 * MARGIN, BLOCK), F32),
            pltpu.VMEM((len(SHIFTS) * STRETCH, WINDOW), BF16),
        ],
        compiler_params=params(14),
        cost_estimate=cost(2e9, 20 << 20),
        name="conv_back",
    )(dx, dy, dmap, in_hbm(slope), in_hbm(conv), taps, skip, ddt, hsums, ssums)


def send_states(payload, to_later):
    n, me = lax.axis_size("seq"), lax.axis_index("seq")
    sent, got = [], []
    for q in range(1, n):
        later = (me ^ q) > me
        first = later if to_later else ~later
        sent.append(jnp.where(first, payload[0], payload[1]))
        got.append(swap(sent[-1], "seq", q))
    return sent, got


def per_device(
    layer_in, norm_gain, in_weight, conv_weight, conv_bias, head_params, out_gain, out_weight, out_cotangent
):
    ns, nw = lax.axis_size("seq"), lax.axis_size("wt")
    ndev = ns * nw
    seq_me = lax.axis_index("seq").astype(jnp.int32)
    me = seq_me * nw + lax.axis_index("wt").astype(jnp.int32)
    me_arr, seq_arr = me.reshape(1), seq_me.reshape(1)
    tokens = layer_in[0]
    cotangent = out_cotangent[0]
    length, d = tokens.shape
    share = in_weight.shape[0]
    cshare = conv_bias.shape[0]
    gshare = out_gain.shape[0]
    spare = WIDE - (in_weight.shape[1] - E)

    small = jnp.concatenate([conv_weight.reshape(-1), conv_bias, out_gain, norm_gain])
    n_small = small.shape[0]
    small = jnp.pad(small, (0, 8 * LANES - n_small)).reshape(8, LANES)
    first = jnp.pad(in_weight[:, E:], ((0, 0), (0, spare)))
    half = E // 2
    rest = jnp.concatenate(
        [in_weight[None, :, :half], in_weight[None, :, half:E], out_weight.reshape(2, share, d)], axis=0
    )
    s1 = jnp.stack(gather_z(small)).reshape(-1, LANES)
    ends = jnp.concatenate([tokens[:EDGE], tokens[length - EDGE :]], axis=0).reshape(-1, LANES)
    s1 = jnp.concatenate([s1, ends], axis=0)
    a1 = jnp.stack(gather_z(first))
    a2 = gather_seq(a1)
    b1 = jnp.stack(gather_z(rest))
    s2 = gather_seq(after(s1, a2[1]))
    a2 = jnp.stack(a2)
    wa, wb = a2.reshape(d // 2, WIDE), swap(after(a2, b1), "wt", 1).reshape(d // 2, WIDE)

    cut = s1.shape[0] - ends.shape[0]
    around = [t[cut:].reshape(2 * EDGE, d) for t in s2]
    s2 = jnp.stack([t[:cut] for t in s2])
    s3 = swap(s2, "wt", 1)
    b2 = gather_seq(after(b1, a2, s3))
    nothing = jnp.zeros((EDGE, d), BF16)
    pick = lambda rows, other: sum((jnp.where(seq_me ^ q == other, around[q][rows], nothing) for q in range(ns)), nothing)
    ext = jnp.concatenate([tokens, pick(slice(EDGE, None), seq_me - 1), pick(slice(0, EDGE), seq_me + 1)], axis=0)

    blocks = jnp.arange(d, dtype=jnp.int32) // share
    offsets = block_order(ns, nw)
    offset_of = jnp.array(offsets, jnp.int32)
    natural = (offset_of[blocks] ^ me) * share + jnp.arange(d, dtype=jnp.int32) % share
    perm = (jnp.arange(d, dtype=jnp.int32)[:, None] == natural[None, :]).astype(BF16)
    u_x = dot(ext, perm)
    inv_in = lax.rsqrt(jnp.mean(jnp.square(ext.astype(F32)), axis=1, keepdims=True) + EPSILON)

    extras = jnp.stack([s2, s3]).reshape(ndev, 8 * LANES)
    order = jnp.arange(ndev, dtype=jnp.int32)[:, None] == (offset_of[None, :] ^ me)
    nat = dot(order.astype(BF16), extras[:, :n_small])
    taps = jnp.transpose(nat[:, : TAPS * cshare].reshape(ndev, TAPS, cshare), (1, 0, 2)).reshape(TAPS, CHANNELS)
    bias = nat[:, TAPS * cshare : (TAPS + 1) * cshare].reshape(1, CHANNELS)
    taps = jnp.concatenate([taps, bias], axis=0)
    gain_out = nat[:, (TAPS + 1) * cshare : (TAPS + 1) * cshare + gshare].reshape(1, E)
    gain_x = extras[:, n_small - share : n_small].reshape(1, d).astype(F32)

    normed = (u_x * inv_in * gain_x).astype(BF16)
    conv, act, slope, dtraw = conv_forward(normed, wa, wb, taps)

    twice = jnp.concatenate([head_params, head_params], axis=1)
    rates = jnp.stack([twice[0], -jnp.exp(twice[1])])
    hp = jnp.pad(rates, ((0, 6), (0, LANES - 2 * HEADS)))
    b2 = jnp.stack([after(t, dtraw) for t in b2]).reshape(2 * ndev, share, half)
    b3 = swap(b2, "wt", 1)
    u, v, ut, vt, eu, wv, tot, s, pay = block_states(act, dtraw, hp)
    sent, got = send_states(pay, True)
    w_z, w_out = unpack(offsets, me_arr, b2, after(b3, *sent))
    w_z, w_out = w_z.reshape(d, E), w_out.reshape(E, d)
    own = normed[:length]
    z = dot(own, w_z).astype(BF16)
    dgated = dot_nt(cotangent, w_out).astype(BF16)
    skip = jnp.repeat(head_params[2], HDIM)[None]
    rows = jnp.concatenate([skip, gain_out, jnp.zeros((6, E), F32)], axis=0)
    got = jnp.stack([after(t, z, dgated) for t in got])
    gated, dz, dy, yz, gain, ent, p, pay, ssums = gate(seq_arr, act, z, dgated, u, vt, eu, s, got, tot, rows)
    sent, got = send_states(pay, False)

    gated_then, dz_then = after(gated, *sent), after(dz, *sent)
    g_out = lax.dot_general(gated_then, cotangent, TN, preferred_element_type=F32).astype(BF16)
    g_z = lax.dot_general(own, dz_then, TN, preferred_element_type=F32).astype(BF16)
    dn_z = dot_nt(dz_then, w_z)
    layer_out = (tokens.astype(F32) + dot(gated_then, w_out)).astype(BF16)[None]
    got = [after(t, g_out, g_z, dn_z, layer_out) for t in got]
    kept, moved = pack(offsets, me_arr, g_z.reshape(ndev, share, E), g_out.reshape(2 * ndev, share, d))
    moved = swap(moved, "wt", 1)
    split = lambda t: t.reshape(ns, nw // 2, 4, share, half)
    r1 = scatter_core(split(kept), split(after(moved, *got)))
    r_got = [swap(r1[q], "seq", q) for q in range(1, ns)]
    dx, dmap, ddt, hsums = mixer_back(
        seq_arr, act, after(dy, *r1), yz, v, ut, wv, gain, ent, p, jnp.stack(got), tot, dtraw, hp
    )
    r2 = scatter_seq(r1, [after(t, dx) for t in r_got])
    z_got = [swap(r2[q], "wt", 2 * q) for q in range(1, nw // 2)]
    dconv, csums = conv_back(after(dx, *r2), dy, dmap, slope, conv, taps, rows, ddt, hsums, ssums)
    r3 = scatter_z(r2, [after(t, dconv) for t in z_got])

    g_c = lax.dot_general(normed, dconv, TN, preferred_element_type=F32).astype(BF16)
    g_c = g_c.reshape(2, ns, nw // 2, share, WIDE)
    sent = after(g_c[1], r3)
    f1 = scatter_core(g_c[0], swap(sent, "wt", 1))
    w_first = jnp.concatenate([wa, wb])
    dn = dot_nt(after(dconv, *f1), w_first)
    f_got = [swap(f1[q], "seq", q) for q in range(1, ns)]
    f2 = scatter_seq(f1, f_got)
    dn = dn + jnp.concatenate([dn_z, jnp.zeros((2 * EDGE, d), F32)], axis=0)
    grad_first = scatter_z(f2)
    csums = sum_everywhere(csums, [sent], [dn], f_got[:1])

    forward = [(i, i + 1) for i in range(ns - 1)]
    backward = [(i + 1, i) for i in range(ns - 1)]
    dn_hi = dn.astype(BF16)
    dn_lo = (dn - dn_hi.astype(F32)).astype(BF16)
    dn = dot_nt(dn_hi, perm) + dot_nt(dn_lo, perm)
    edges = after(dn[length:], f_got[0])
    prev_edge = lax.ppermute(edges[:EDGE], "seq", backward)
    next_edge = lax.ppermute(edges[EDGE:], "seq", forward)
    middle = jnp.zeros((length - 2 * EDGE, d), F32)
    dn = dn[:length] + jnp.concatenate([next_edge, middle, prev_edge], axis=0)
    u, inv = tokens.astype(F32), inv_in[:length]
    scaled = nat[:, n_small - share :].reshape(1, d) * dn
    in_grad = after(cotangent, *f2).astype(F32) + inv * scaled
    in_grad = in_grad - u * inv**3 * jnp.mean(scaled * u, axis=1, keepdims=True)

    grad_z = jnp.concatenate([r3[0], r3[1]], axis=1)
    grad_out = r3[2:].reshape(gshare, d)
    vec = lax.dynamic_slice(csums, (0, me * cshare), (8, cshare))
    pair = csums[:3, CHANNELS : CHANNELS + 2 * HEADS]
    head_grad = pair[:, :HEADS] + pair[:, HEADS:]
    grad_in = jnp.concatenate([grad_z, grad_first[:, : WIDE - spare]], axis=1)
    gain_grad = jnp.sum(in_weight.astype(F32) * grad_in, axis=1) / norm_gain.astype(F32)
    out_gain_grad = jnp.sum(out_weight.astype(F32) * grad_out, axis=1) / out_gain.astype(F32)
    return (
        layer_out,
        in_grad[None],
        gain_grad,
        grad_in,
        vec[:TAPS],
        vec[TAPS],
        head_grad,
        out_gain_grad,
        grad_out,
    )


def solution(mesh):
    rows = P(("seq", "wt"))
    table = P(("seq", "wt"), None)
    tokens = P("wt", "seq", None)
    taps = P(None, ("seq", "wt"))
    return jax.shard_map(
        per_device,
        mesh=mesh,
        in_specs=(tokens, rows, table, taps, rows, P(), rows, table, tokens),
        out_specs=(tokens, tokens, rows, table, taps, rows, P(), rows, table),
        check_vma=False,
    )
```

```python
import functools

import jax
import jax.numpy as jnp
from jax import lax
from jax.experimental import pallas as pl
from jax.experimental.pallas import tpu as pltpu
from jax.sharding import PartitionSpec as P

HEADS = 24
HDIM = 64
STATE = 64
STRETCH = 128
TAPS = 7
E = 1536
CHANNELS = 1792
PAIRS = HEADS // 2
LANES = 128
WIDE = 1920
EDGE = 8
EPSILON = 1e-05
LOG2E = 1.4426950408889634

F32 = jnp.float32
BF16 = jnp.bfloat16
NT = (((1,), (1,)), ((), ()))
TN = (((0,), (0,)), ((), ()))


def dot(a, b):
    return jnp.dot(a, b, preferred_element_type=F32)


def dot_nt(a, b):
    return lax.dot_general(a, b, NT, preferred_element_type=F32)


def params(limit=56):
    return pltpu.CompilerParams(vmem_limit_bytes=limit << 20)


def cost(flops, moved, trans=0):
    return pl.CostEstimate(flops=int(flops), bytes_accessed=int(moved), transcendentals=int(trans))


def whole(shape):
    return pl.BlockSpec(shape, lambda *_: (0,) * len(shape), pipeline_mode=pl.Buffered(1))


def swap(x, axis, q):
    n = lax.axis_size(axis)
    return lax.ppermute(x, axis, [(i, i ^ q) for i in range(n)])


def gather_z(x):
    return [x] + [swap(x, "wt", 2 * q) for q in range(1, lax.axis_size("wt") // 2)]


def gather_seq(x):
    return [x] + [swap(x, "seq", q) for q in range(1, lax.axis_size("seq"))]


def block_order(ns, nw):
    return [s * nw + 2 * z + c for c in range(2) for s in range(ns) for z in range(nw // 2)]


def low(t):
    return t.astype(BF16)


def up(t):
    return t.astype(F32)


def scatter_core(kept, got):
    return [low(up(kept[q]) + up(got[q])) for q in range(kept.shape[0])]


def scatter_seq(a, got=None):
    if got is None:
        got = [swap(a[q], "seq", q) for q in range(1, len(a))]
    total = lambda z: sum((up(t[z]) for t in got), up(a[0][z]))
    return [low(total(z)) for z in range(a[0].shape[0])]


def scatter_z(b, got=None):
    if got is None:
        got = [swap(b[q], "wt", 2 * q) for q in range(1, len(b))]
    return sum((up(t) for t in got), up(b[0]))


def sum_steps(ns, nw):
    return [("seq", q) for q in (1, 2, 4, 8) if q < ns] + [("wt", q) for q in (2, 4, 8, 16) if q < nw] + [("wt", 1)]


def after(x, *others):
    return lax.optimization_barrier((x, *others))[0]


def unpack_kernel(order, me_ref, *refs):
    parts, (z_ref, o_ref) = refs[:-2], refs[-2:]
    half = o_ref.shape[2]
    count = parts[0].shape[0] // 4
    for p, offset in enumerate(order):
        x_ref, k = parts[p // count], 4 * (p % count)
        z_ref[p, :, :half] = x_ref[k]
        z_ref[p, :, half:] = x_ref[k + 1]
        target = 2 * jnp.bitwise_xor(me_ref[0], offset)
        o_ref[target] = x_ref[k + 2]
        o_ref[target + 1] = x_ref[k + 3]


def unpack(order, me, parts):
    _, share, half = parts[0].shape
    n = len(order)
    shapes = [(n, share, 2 * half), (2 * n, share, half)]
    return pl.pallas_call(
        functools.partial(unpack_kernel, order),
        grid=(1,),
        out_shape=[jax.ShapeDtypeStruct(s, parts[0].dtype) for s in shapes],
        in_specs=[pl.BlockSpec(memory_space=pltpu.SMEM)] + [whole(t.shape) for t in parts],
        out_specs=[whole(s) for s in shapes],
        compiler_params=params(12),
        cost_estimate=cost(0, 16 * n * share * half),
        name="unpack",
    )(me, *parts)


def pack_kernel(order, me_ref, z_ref, o_ref, a_ref, b_ref):
    half = a_ref.shape[2]
    count = a_ref.shape[0] // 4
    for p, offset in enumerate(order):
        x_ref, k = (a_ref, 4 * p) if p < count else (b_ref, 4 * (p - count))
        x_ref[k] = z_ref[p, :, :half]
        x_ref[k + 1] = z_ref[p, :, half:]
        source = 2 * jnp.bitwise_xor(me_ref[0], offset)
        x_ref[k + 2] = o_ref[source]
        x_ref[k + 3] = o_ref[source + 1]


def pack(order, me, z, o):
    n, share, wide = z.shape
    shape = (2 * n, share, wide // 2)
    return pl.pallas_call(
        functools.partial(pack_kernel, order),
        grid=(1,),
        out_shape=[jax.ShapeDtypeStruct(shape, z.dtype)] * 2,
        in_specs=[pl.BlockSpec(memory_space=pltpu.SMEM), whole(z.shape), whole(o.shape)],
        out_specs=[whole(shape)] * 2,
        compiler_params=params(12),
        cost_estimate=cost(0, 8 * z.size),
        name="pack",
    )(me, z, o)


BLOCK = 256


SHIFTS = [k for k in range(TAPS) if k != TAPS // 2]
MARGIN = 16
WINDOW = STRETCH + 2 * MARGIN


def fill_shifts(shift_ref, sign):
    for n, k in enumerate(SHIFTS):
        picked = iota((STRETCH, WINDOW), 0) + (MARGIN + sign * (k - TAPS // 2))
        same = iota((STRETCH, WINDOW), 1) == picked
        shift_ref[n * STRETCH : (n + 1) * STRETCH, :] = jnp.where(same, 1.0, 0.0).astype(BF16)


def shifted_rows(shift_ref, pad_ref, first):
    rows = dot(shift_ref[...], pad_ref[first : first + WINDOW, :])
    out = {k: rows[n * STRETCH : (n + 1) * STRETCH] for n, k in enumerate(SHIFTS)}
    out[TAPS // 2] = pad_ref[first + MARGIN : first + MARGIN + STRETCH, :].astype(F32)
    return out


def conv_kernel(
    nx_ref, wa_ref, wb_ref, da_ref, db_ref, taps_ref, conv_ref, act_ref, slope_ref, dt_ref, pad_ref, shift_ref
):
    length = act_ref.shape[0]

    @pl.when(pl.program_id(0) == 0)
    def _():
        fill_shifts(shift_ref, 1)
        pad_ref[...] = jnp.zeros_like(pad_ref)

    w = jnp.concatenate([wa_ref[...], wb_ref[...]], axis=0)
    zeros = jnp.zeros((EDGE, BLOCK), BF16)
    r = dot(nx_ref[length:], w).astype(BF16)
    conv_ref[length:] = r
    pad_ref[:MARGIN] = jnp.concatenate([zeros, r[:EDGE]], axis=0)
    pad_ref[MARGIN + length :] = jnp.concatenate([r[EDGE:], zeros], axis=0)
    count = length // STRETCH
    for c in range(count + 1):
        if c < count:
            rows = slice(c * STRETCH, (c + 1) * STRETCH)
            r = dot(nx_ref[rows], w).astype(BF16)
            conv_ref[rows] = r
            pad_ref[MARGIN + rows.start : MARGIN + rows.stop] = r
        if c > 0:
            first = (c - 1) * STRETCH
            pre = jnp.broadcast_to(taps_ref[TAPS : TAPS + 1, :], (STRETCH, BLOCK))
            for k, x in shifted_rows(shift_ref, pad_ref, first).items():
                pre = pre + taps_ref[k : k + 1, :] * x
            sig = jax.nn.sigmoid(pre)
            act = pre * sig
            rows = slice(first, first + STRETCH)
            act_ref[rows] = act.astype(BF16)
            slope_ref[rows] = (sig + act * (1.0 - sig)).astype(BF16)

    @pl.when(pl.program_id(0) == pl.num_programs(0) - 1)
    def _():
        w = jnp.concatenate([da_ref[...], db_ref[...]], axis=0)
        dt_ref[...] = dot(nx_ref[:length], w)


def conv_forward(normed, wa, wb, taps):
    ext, d = normed.shape
    length = ext - 2 * EDGE
    col = lambda j: (0, j)
    steps = pl.BlockSpec((d // 2, LANES), lambda j: (0, CHANNELS // LANES))
    return pl.pallas_call(
        conv_kernel,
        grid=(CHANNELS // BLOCK,),
        in_specs=[
            whole((ext, d)),
            pl.BlockSpec((d // 2, BLOCK), col),
            pl.BlockSpec((d // 2, BLOCK), col),
            steps,
            steps,
            pl.BlockSpec((8, BLOCK), col),
        ],
        out_specs=[
            pl.BlockSpec((ext, BLOCK), col),
            pl.BlockSpec((length, BLOCK), col),
            pl.BlockSpec((length, BLOCK), col),
            whole((length, LANES)),
        ],
        out_shape=[
            hbm((ext, CHANNELS), BF16),
            hbm((length, CHANNELS), BF16),
            hbm((length, CHANNELS), BF16),
            jax.ShapeDtypeStruct((length, LANES), F32),
        ],
        scratch_shapes=[
            pltpu.VMEM((length + 2 * MARGIN, BLOCK), BF16),
            pltpu.VMEM((len(SHIFTS) * STRETCH, WINDOW), BF16),
        ],
        compiler_params=params(14),
        cost_estimate=cost(2 * ext * d * WIDE, 16 << 20),
        name="conv_forward",
    )(normed, wa, wb, wa, wb, taps)


def hbm(shape, kind):
    return pltpu.HBM(shape, kind)


def in_hbm(x):
    return pltpu.with_memory_space_constraint(x, pltpu.HBM)


def iota(shape, dim):
    return lax.broadcasted_iota(jnp.int32, shape, dim)


def fill_expand(exp_ref):
    for c in range(2 * E // LANES):
        row = jnp.bitwise_and(iota((2 * LANES, LANES), 0), LANES - 1)
        head = 2 * c + jnp.where(iota((2 * LANES, LANES), 1) >= HDIM, 1, 0)
        exp_ref[:, c * LANES : (c + 1) * LANES] = jnp.where(row == head, 1.0, 0.0).astype(BF16)


def fill_heads(heads_ref):
    for c in range(2 * PAIRS):
        row = iota((LANES, LANES), 0)
        head = 2 * (c % PAIRS) + jnp.where(row >= HDIM, 1, 0)
        head = head + jnp.where(jnp.bitwise_and(row, HDIM - 1) >= HDIM // 2, HEADS, 0)
        same = iota((LANES, LANES), 1) == head
        heads_ref[c * LANES : (c + 1) * LANES, :] = jnp.where(same, 1.0, 0.0).astype(BF16)


def fold_pair(f, r, first):
    half = HDIM // 2
    return jnp.where(first, f + pltpu.roll(f, LANES - half, 1), r + pltpu.roll(r, half, 1))


def two_parts(x):
    hi = x.astype(BF16)
    lo = (x - hi.astype(F32)).astype(BF16)
    return jnp.concatenate([hi, lo], axis=1)


CHUNKS = [slice(c * 2 * LANES, (c + 1) * 2 * LANES) for c in range(E // (2 * LANES))]
PAIR_COLS = [slice(p * LANES, (p + 1) * LANES) for p in range(PAIRS)]


def shifted(cols):
    return slice(cols.start + E, cols.stop + E)


def pair_rows(row, p, first):
    h = first + 2 * p
    left = iota((8, LANES), 1) < HDIM
    return jnp.where(left, row[:, h : h + 1], row[:, h + 1 : h + 2])


def scan_states(out_ref, state_ref, tot_ref, add_ref, first, backward):
    rows = slice(0, STATE) if first == 0 else slice(STATE, 2 * STATE)
    order = range(add_ref.shape[0])
    for c in reversed(order) if backward else order:
        dec = jnp.exp2(tot_ref[c])
        for p, cols in enumerate(PAIR_COLS):
            state = state_ref[:, cols]
            out_ref[c, rows, cols] = state.astype(BF16)
            state_ref[:, cols] = pair_rows(dec, p, first)[0:1] * state + add_ref[c, rows, cols].astype(F32)


def step_sizes(dtraw, hp_ref):
    lane = iota(dtraw.shape, 1)
    pre = jnp.where(lane < 2 * HEADS, dtraw + hp_ref[0:1, :], 0.0)
    dt = jnp.maximum(pre, 0.0) + jnp.log1p(jnp.exp(-jnp.abs(pre)))
    return pre, dt, hp_ref[1:2, :] * dt


def states_kernel(
    act_ref, dtraw_ref, hp_ref, u_ref, v_ref, ut_ref, vt_ref, eu_ref, wv_ref, tot_ref, s_ref, pay_ref,
    exp_ref, dev_ref, cum_ref, z_ref,
):
    b = pl.program_id(0)
    nb = pl.num_programs(0)

    @pl.when(b == 0)
    def _():
        fill_expand(exp_ref)
        dev_ref[...] = jnp.zeros_like(dev_ref)
        cum_ref[...] = jnp.zeros_like(cum_ref)

    sq = (STRETCH, LANES)
    lane = iota(sq, 1)
    forward = lane < HEADS
    _, dt, lg = step_sizes(dtraw_ref[...], hp_ref)
    dtb = dt.astype(BF16).astype(F32)
    lgb = lg.astype(BF16)
    upto = jnp.where(iota(sq, 0) >= iota(sq, 1), 1.0, 0.0).astype(BF16)
    run = dot(upto, lgb)
    before = run - lgb.astype(F32)
    total = run[STRETCH - 1 : STRETCH, :] * LOG2E
    logdt = jnp.where(dtb > 0.0, jnp.log(jnp.where(dtb > 0.0, dtb, 1.0)) * LOG2E, -1e30)
    u = jnp.where(forward, before, -run) * LOG2E
    v = jnp.where(forward, -run, before) * LOG2E + logdt
    u_ref[...] = u
    v_ref[...] = v
    ut_ref[0] = u.T
    vt_ref[0] = v.T
    eu = jnp.exp2(u + jnp.where(forward, 0.0, total))
    wv = jnp.exp2(v + jnp.where(forward, total, 0.0))
    eu_ref[...] = eu
    wv_ref[...] = wv
    total8 = jnp.broadcast_to(total, (8, LANES))
    tot_ref[0] = total8

    bt = act_ref[:, E : E + LANES].T
    w2 = two_parts(wv)
    for cols in CHUNKS:
        x = act_ref[:, cols].astype(F32)
        z_ref[:, cols] = (x * dot(w2, exp_ref[:, cols])).astype(BF16)
        z_ref[:, shifted(cols)] = (x * dot(w2, exp_ref[:, shifted(cols)])).astype(BF16)
    dec = jnp.exp2(total8)
    pre = jnp.exp2(cum_ref[...])
    for c, cols in enumerate(CHUNKS):
        sf = dot(bt[:STATE], z_ref[:, cols])
        sr = dot(bt[STATE:], z_ref[:, shifted(cols)])
        s_ref[0, :STATE, cols] = sf.astype(BF16)
        s_ref[0, STATE:, cols] = sr.astype(BF16)
        dec_f = jnp.concatenate([pair_rows(dec, 2 * c, 0), pair_rows(dec, 2 * c + 1, 0)], axis=1)
        pre_r = jnp.concatenate([pair_rows(pre, 2 * c, HEADS), pair_rows(pre, 2 * c + 1, HEADS)], axis=1)
        dev_ref[:STATE, cols] = dec_f[0:1] * dev_ref[:STATE, cols] + sf
        dev_ref[STATE:, cols] = dev_ref[STATE:, cols] + pre_r[0:1] * sr
    cum_ref[...] = cum_ref[...] + total8

    @pl.when(b == nb - 1)
    def _():
        write_payload(pay_ref, dev_ref, cum_ref)


def write_payload(pay_ref, dev_ref, cum_ref):
    cum = cum_ref[...]
    pay_ref[0, :STATE] = dev_ref[:STATE].astype(BF16)
    pay_ref[1, :STATE] = dev_ref[STATE:].astype(BF16)
    for k in range(2):
        for p, cols in enumerate(PAIR_COLS):
            row = pair_rows(cum, p, k * HEADS)
            pay_ref[k, STATE:, cols] = jnp.concatenate([row, row], axis=0).astype(BF16)


PAY = STATE + 16


def block_states(act, dtraw, hp):
    length = act.shape[0]
    nb = length // STRETCH
    sq = pl.BlockSpec((STRETCH, LANES), lambda b: (b, 0))
    cube = pl.BlockSpec((1, STRETCH, LANES), lambda b: (b, 0, 0))
    flat = jax.ShapeDtypeStruct((length, LANES), F32)
    deep = jax.ShapeDtypeStruct((nb, LANES, STRETCH), F32)
    return pl.pallas_call(
        states_kernel,
        grid=(nb,),
        in_specs=[pl.BlockSpec((STRETCH, CHANNELS), lambda b: (b, 0)), sq, whole((8, LANES))],
        out_specs=[
            sq, sq, cube, cube, sq, sq,
            pl.BlockSpec((1, 8, LANES), lambda b: (b, 0, 0)),
            pl.BlockSpec((1, 2 * STATE, E), lambda b: (b, 0, 0)),
            whole((2, PAY, E)),
        ],
        out_shape=[
            flat, hbm((length, LANES), F32), hbm((nb, LANES, STRETCH), F32), deep, flat, hbm((length, LANES), F32),
            jax.ShapeDtypeStruct((nb, 8, LANES), F32),
            hbm((nb, 2 * STATE, E), BF16),
            jax.ShapeDtypeStruct((2, PAY, E), BF16),
        ],
        scratch_shapes=[
            pltpu.VMEM((2 * LANES, 2 * E), BF16),
            pltpu.VMEM((2 * STATE, E), F32),
            pltpu.VMEM((8, LANES), F32),
            pltpu.VMEM((STRETCH, 2 * E), BF16),
        ],
        compiler_params=params(12),
        cost_estimate=cost(4e9, 12 << 20),
        name="block_states",
    )(in_hbm(act), dtraw, hp)


def from_others(me, got_ref, upward):
    n = got_ref.shape[0] + 1
    side = lambda d: (d < me) if upward else (d > me)
    total = jnp.zeros((STATE, E), F32)
    for q in range(1, n):
        d = jnp.bitwise_xor(me, q)
        log = jnp.zeros((1, E), F32)
        for k in range(1, n):
            if k != q:
                e = jnp.bitwise_xor(me, k)
                between = ((d < e) & (e < me)) if upward else ((me < e) & (e < d))
                row = got_ref[k - 1, STATE : STATE + 1, :].astype(F32)
                log = log + jnp.where(between, row, 0.0)
        term = jnp.exp2(log) * got_ref[q - 1, :STATE, :].astype(F32)
        total = total + jnp.where(side(d), term, 0.0)
    return total


MAPS = slice(E, E + LANES), slice(E + LANES, E + 2 * LANES)


def split_store(ref, rows, cols, value):
    hi = value.astype(BF16)
    ref[rows, cols] = hi
    ref[rows, shifted(cols)] = (value - hi.astype(F32)).astype(BF16)


def sigmoid(x):
    return 0.5 * jnp.tanh(0.5 * x) + 0.5


def gate_kernel(
    me_ref, act_ref, z_ref, dg_ref, u_ref, vt_ref, eu_ref, s_ref, got_ref, tot_ref, rows_ref,
    gated_ref, dz_ref, dy_ref, yz_ref, gain_ref, ent_ref, p_ref, pay_ref, skip_ref,
    exp_ref, heads_ref, dev_ref, cum_ref, e_ref, y_ref, yv_ref, sig_ref, prod_ref, sums_ref, state_ref,
):
    b = pl.program_id(0)
    nb = pl.num_programs(0)

    @pl.when(b == 0)
    def _():
        fill_expand(exp_ref)
        fill_heads(heads_ref)
        dev_ref[...] = jnp.zeros_like(dev_ref)
        cum_ref[...] = jnp.zeros_like(cum_ref)
        sums_ref[...] = jnp.zeros_like(sums_ref)
        me = me_ref[0]
        state_ref[...] = from_others(me, got_ref, True)
        scan_states(ent_ref, state_ref, tot_ref, s_ref, 0, False)
        state_ref[...] = from_others(me, got_ref, False)
        scan_states(ent_ref, state_ref, tot_ref, s_ref, HEADS, True)

    sq = (STRETCH, STRETCH)
    i, j = iota(sq, 0), iota(sq, 1)
    after_j, at = i > j, i >= j
    lower = jnp.where(after_j, 1.0, 0.0).astype(BF16)
    upper = jnp.where(at, 0.0, 1.0).astype(BF16)
    bm, cm = act_ref[:, MAPS[0]], act_ref[:, MAPS[1]]
    cf, cr = cm[:, :STATE], cm[:, STATE:]
    gram = jnp.where(after_j, dot_nt(cf, bm[:, :STATE]), jnp.where(at, 0.0, dot_nt(cr, bm[:, STATE:])))
    left = iota((STRETCH, LANES), 1) < HDIM
    first_half = jnp.bitwise_and(iota((STRETCH, LANES), 1), HDIM - 1) < HDIM // 2

    e2 = two_parts(eu_ref[...])
    for cols in CHUNKS:
        for c, state in ((cf, ent_ref[b, :STATE, cols]), (cr, ent_ref[b, STATE:, cols])):
            at_cols = cols if c is cf else shifted(cols)
            e = dot(e2, exp_ref[:, at_cols])
            e_ref[:, at_cols] = e
            y_ref[:, at_cols] = e * dot(c, state)

    square = jnp.zeros((STRETCH, LANES), F32)
    cross = jnp.zeros((STRETCH, LANES), F32)
    for p, cols in enumerate(PAIR_COLS):
        mats = []
        for h in (2 * p, 2 * p + 1):
            r = HEADS + h
            row = jnp.where(at, u_ref[:, h : h + 1], u_ref[:, r : r + 1])
            col = jnp.where(after_j, vt_ref[0, h : h + 1, :], vt_ref[0, r : r + 1, :])
            mats.append((jnp.exp2(row + col) * gram).astype(BF16))
        mats = [m * lower for m in mats] + [m * upper for m in mats]
        y = dot(jnp.concatenate(mats, axis=0), act_ref[:, cols])
        yf = y_ref[:, cols] + jnp.where(left, y[:STRETCH], y[STRETCH : 2 * STRETCH])
        yr = y_ref[:, shifted(cols)] + jnp.where(left, y[2 * STRETCH : 3 * STRETCH], y[3 * STRETCH :])
        y_ref[:, cols] = yf
        y_ref[:, shifted(cols)] = yr
        yv = yf + yr + rows_ref[0:1, cols] * act_ref[:, cols].astype(F32)
        yv_ref[:, cols] = yv
        z = z_ref[:, cols].astype(F32)
        sig = sigmoid(z)
        sig_ref[:, cols] = sig
        yg = yv * (z * sig)
        square = square + yg * yg
        cross = cross + rows_ref[1:2, cols] * dg_ref[:, cols].astype(F32) * yg
    inv = lax.rsqrt(jnp.sum(square, axis=1, keepdims=True) / E + EPSILON)
    back = inv * inv * inv * (jnp.sum(cross, axis=1, keepdims=True) / E)

    for p, cols in enumerate(PAIR_COLS):
        z = z_ref[:, cols].astype(F32)
        sig = sig_ref[:, cols]
        ga = z * sig
        yv = yv_ref[:, cols]
        yg = yv * ga
        gain = rows_ref[1:2, cols]
        gated_ref[:, cols] = (yg * inv * gain).astype(BF16)
        dyg = inv * (gain * dg_ref[:, cols].astype(F32)) - yg * back
        dy = dyg * ga
        dz_ref[:, cols] = (dyg * yv * (sig + ga * (1.0 - sig))).astype(BF16)
        low_dy = dy.astype(BF16)
        dy_ref[:, cols] = low_dy
        fold = lambda t: jnp.sum(t.reshape(STRETCH // 8, 8, LANES), axis=0)
        sums_ref[:, cols] = sums_ref[:, cols] + fold(dy * act_ref[:, cols].astype(F32))
        dy = low_dy.astype(F32)
        yz_ref[:, cols] = (e_ref[:, cols] * dy).astype(BF16)
        yz_ref[:, shifted(cols)] = (e_ref[:, shifted(cols)] * dy).astype(BF16)
        pair = fold_pair(y_ref[:, cols] * dy, y_ref[:, shifted(cols)] * dy, first_half)
        split_store(prod_ref, slice(None), cols, pair)
    gain_ref[...] = dot(prod_ref[...], heads_ref[...])

    total8 = tot_ref[b]
    dec = jnp.exp2(total8)
    pre = jnp.exp2(cum_ref[...])
    ct = cm.T
    for c, cols in enumerate(CHUNKS):
        pf = dot(ct[:STATE], yz_ref[:, cols])
        pr = dot(ct[STATE:], yz_ref[:, shifted(cols)])
        p_ref[0, :STATE, cols] = pf.astype(BF16)
        p_ref[0, STATE:, cols] = pr.astype(BF16)
        pre_f = jnp.concatenate([pair_rows(pre, 2 * c, 0), pair_rows(pre, 2 * c + 1, 0)], axis=1)
        dec_r = jnp.concatenate([pair_rows(dec, 2 * c, HEADS), pair_rows(dec, 2 * c + 1, HEADS)], axis=1)
        dev_ref[:STATE, cols] = dev_ref[:STATE, cols] + pre_f[0:1] * pf
        dev_ref[STATE:, cols] = dec_r[0:1] * dev_ref[STATE:, cols] + pr
    cum_ref[...] = cum_ref[...] + total8

    @pl.when(b == nb - 1)
    def _():
        write_payload(pay_ref, dev_ref, cum_ref)
        skip_ref[...] = lax.dot_general(
            sums_ref[...], exp_ref[:LANES, :E].astype(F32), NT,
            precision=lax.Precision.HIGHEST, preferred_element_type=F32,
        )


def gate(me, act, z, dg, u, vt, eu, s, got, tot, rows):
    length = act.shape[0]
    nb = length // STRETCH
    line = pl.BlockSpec((STRETCH, E), lambda b: (b, 0))
    sq = pl.BlockSpec((STRETCH, LANES), lambda b: (b, 0))
    low_line = jax.ShapeDtypeStruct((length, E), BF16)
    return pl.pallas_call(
        gate_kernel,
        grid=(nb,),
        in_specs=[
            pl.BlockSpec(memory_space=pltpu.SMEM),
            pl.BlockSpec((STRETCH, CHANNELS), lambda b: (b, 0)),
            line,
            line,
            sq,
            pl.BlockSpec((1, LANES, STRETCH), lambda b: (b, 0, 0)),
            sq,
            whole(s.shape),
            whole(got.shape),
            whole(tot.shape),
            whole((8, E)),
        ],
        out_specs=[
            line,
            line,
            line,
            pl.BlockSpec((STRETCH, 2 * E), lambda b: (b, 0)),
            sq,
            whole(s.shape),
            pl.BlockSpec((1, 2 * STATE, E), lambda b: (b, 0, 0)),
            whole((2, PAY, E)),
            whole((8, LANES)),
        ],
        out_shape=[
            low_line,
            low_line,
            low_line,
            jax.ShapeDtypeStruct((length, 2 * E), BF16),
            jax.ShapeDtypeStruct((length, LANES), F32),
            jax.ShapeDtypeStruct(s.shape, BF16),
            jax.ShapeDtypeStruct(s.shape, BF16),
            jax.ShapeDtypeStruct((2, PAY, E), BF16),
            jax.ShapeDtypeStruct((8, LANES), F32),
        ],
        scratch_shapes=[
            pltpu.VMEM((2 * LANES, 2 * E), BF16),
            pltpu.VMEM((2 * E, LANES), BF16),
            pltpu.VMEM((2 * STATE, E), F32),
            pltpu.VMEM((8, LANES), F32),
            pltpu.VMEM((STRETCH, 2 * E), F32),
            pltpu.VMEM((STRETCH, 2 * E), F32),
            pltpu.VMEM((STRETCH, E), F32),
            pltpu.VMEM((STRETCH, E), F32),
            pltpu.VMEM((STRETCH, 2 * E), BF16),
            pltpu.VMEM((8, E), F32),
            pltpu.VMEM((STATE, E), F32),
        ],
        compiler_params=params(30),
        cost_estimate=cost(16e9, 32 << 20),
        name="gate",
    )(me, in_hbm(act), z, dg, u, vt, eu, in_hbm(s), got, tot, rows)


def mixer_back_kernel(
    me_ref, act_ref, dy_ref, yz_ref, v_ref, ut_ref, wv_ref, gain_ref, ent_ref, p_ref, got_ref, tot_ref,
    dtraw_ref, hp_ref,
    dx_ref, dmap_ref, ddt_ref, sums_ref,
    exp_ref, heads_ref, out_ref, v_in_ref, xz_ref, prod_ref, state_ref, row_ref,
):
    b = pl.program_id(0)
    sq = (STRETCH, STRETCH)
    j, i = iota(sq, 0), iota(sq, 1)
    after_j, at = i > j, i >= j

    @pl.when(b == 0)
    def _():
        fill_expand(exp_ref)
        fill_heads(heads_ref)
        sums_ref[...] = jnp.zeros_like(sums_ref)
        row_ref[...] = jnp.zeros_like(row_ref)
        me = me_ref[0]
        state_ref[...] = from_others(me, got_ref, False)
        scan_states(out_ref, state_ref, tot_ref, p_ref, 0, True)
        state_ref[...] = from_others(me, got_ref, True)
        scan_states(out_ref, state_ref, tot_ref, p_ref, HEADS, False)

    bm, cm = act_ref[:, MAPS[0]], act_ref[:, MAPS[1]]
    bf, br, cf, cr = bm[:, :STATE], bm[:, STATE:], cm[:, :STATE], cm[:, STATE:]
    gram = jnp.where(after_j, dot_nt(bf, cf), jnp.where(at, 0.0, dot_nt(br, cr)))
    lower = jnp.where(after_j, 1.0, 0.0).astype(BF16)
    upper = jnp.where(at, 0.0, 1.0).astype(BF16)
    left = iota((STRETCH, LANES), 1) < HDIM
    first_half = jnp.bitwise_and(iota((STRETCH, LANES), 1), HDIM - 1) < HDIM // 2
    left_low = jnp.where(left, 1.0, 0.0).astype(BF16)
    right_low = jnp.where(left, 0.0, 1.0).astype(BF16)

    w2 = two_parts(wv_ref[...])
    for cols in CHUNKS:
        x = act_ref[:, cols].astype(F32)
        for k, m, state in ((0, bf, out_ref[b, :STATE, cols]), (1, br, out_ref[b, STATE:, cols])):
            at_cols = cols if k == 0 else shifted(cols)
            w = dot(w2, exp_ref[:, at_cols])
            v_in = w * dot(m, state)
            v_in_ref[:, at_cols] = v_in
            xz_ref[:, at_cols] = (w * x).astype(BF16)
            row_ref[k : k + 1, cols] = jnp.sum(v_in * x, axis=0, keepdims=True)
    p_out, s_in = out_ref[b], ent_ref[0]
    db_f = dot_nt(xz_ref[:, :E], p_out[:STATE])
    db_r = dot_nt(xz_ref[:, E:], p_out[STATE:])
    dc_f = dot_nt(yz_ref[:, :E], s_in[:STATE])
    dc_r = dot_nt(yz_ref[:, E:], s_in[STATE:])

    dgram = jnp.zeros(sq, F32)
    for p, cols in enumerate(PAIR_COLS):
        xb, dyb = act_ref[:, cols], dy_ref[:, cols]
        x = xb.astype(F32)
        dm = dot_nt(jnp.concatenate([xb * left_low, xb * right_low], axis=0), dyb)
        mats = []
        for k, h in enumerate((2 * p, 2 * p + 1)):
            r = HEADS + h
            row = jnp.where(after_j, v_ref[:, h : h + 1], v_ref[:, r : r + 1])
            col = jnp.where(at, ut_ref[0, h : h + 1, :], ut_ref[0, r : r + 1, :])
            decay = jnp.exp2(row + col)
            mats.append((decay * gram).astype(BF16))
            dgram = dgram + dm[k * STRETCH : (k + 1) * STRETCH] * decay
        mats = [m * lower for m in mats] + [m * upper for m in mats]
        d4 = dot(jnp.concatenate(mats, axis=0), dyb)
        vf = v_in_ref[:, cols] + jnp.where(left, d4[:STRETCH], d4[STRETCH : 2 * STRETCH])
        vr = v_in_ref[:, shifted(cols)] + jnp.where(left, d4[2 * STRETCH : 3 * STRETCH], d4[3 * STRETCH :])
        dx_ref[:, cols] = (vf + vr).astype(BF16)
        split_store(prod_ref, slice(0, STRETCH), cols, fold_pair(vf * x, vr * x, first_half))
    pe = p_out.astype(F32) * s_in.astype(F32)
    col_sum = lambda t: jnp.sum(t, axis=0, keepdims=True)
    row_ref[2:3, :] = col_sum(pe[:STATE])
    row_ref[3:4, :] = col_sum(pe[STATE:])
    for cols in PAIR_COLS:
        f = jnp.concatenate([row_ref[0:1, cols], row_ref[2:3, cols], jnp.zeros((14, LANES), F32)], axis=0)
        r = jnp.concatenate([row_ref[1:2, cols], row_ref[3:4, cols], jnp.zeros((14, LANES), F32)], axis=0)
        split_store(prod_ref, slice(STRETCH, STRETCH + 16), cols, fold_pair(f, r, first_half[:16]))
    sums = dot(prod_ref[...], heads_ref[...])
    dlog = sums[:STRETCH]
    through = sums[STRETCH : STRETCH + 1] + jnp.exp2(tot_ref[b])[0:1] * sums[STRETCH + 1 : STRETCH + 2]

    gfwd = jnp.where(after_j, dgram, 0.0).astype(BF16)
    grev = jnp.where(at, 0.0, dgram).astype(BF16)
    gfwd_t = gfwd.T
    grev_t = grev.T
    dmap_ref[:, :LANES] = jnp.concatenate([db_f + dot(gfwd, cf), db_r + dot(grev, cr)], axis=1)
    dmap_ref[:, LANES:] = jnp.concatenate([dc_f + dot(gfwd_t, bf), dc_r + dot(grev_t, br)], axis=1)

    lane = iota((STRETCH, LANES), 1)
    forward = lane < HEADS
    gain = gain_ref[...]
    both = jnp.concatenate([gain, dlog], axis=1)
    top = both.astype(BF16)
    rest = both - top.astype(F32)
    mid = rest.astype(BF16)
    end = (rest - mid.astype(F32)).astype(BF16)
    later = dot(lower, top) + dot(lower, mid) + dot(lower, end)
    later_gain, later_dlog = later[:, :LANES], later[:, LANES:]
    dlg = jnp.where(
        forward,
        later_gain - later_dlog - dlog,
        (col_sum(gain) - later_gain - gain) - (col_sum(dlog) - later_dlog),
    )
    dlg = dlg + through
    pre, dt, lg = step_sizes(dtraw_ref[...], hp_ref)
    dtb = dt.astype(BF16).astype(F32)
    ok = (dtb > 0.0) & (lane < 2 * HEADS)
    ddt = jnp.where(ok, dlog / jnp.where(ok, dtb, 1.0), 0.0)
    ddt = ddt.astype(BF16).astype(F32)
    dlg = jnp.where(lane < 2 * HEADS, dlg, 0.0).astype(BF16).astype(F32)
    draw = (ddt + dlg * hp_ref[1:2, :]) * jax.nn.sigmoid(pre)
    ddt_ref[...] = draw.astype(BF16)
    fold = lambda t: jnp.sum(t.reshape(STRETCH // 8, 8, LANES), axis=0)
    sums_ref[0:8] = sums_ref[0:8] + fold(draw)
    sums_ref[8:16] = sums_ref[8:16] + fold(dlg * lg)


def mixer_back(me, act, dy, yz, v, ut, wv, gain, ent, p, got, tot, dtraw, hp):
    length = act.shape[0]
    nb = length // STRETCH
    sq = pl.BlockSpec((STRETCH, LANES), lambda b: (b, 0))
    line = pl.BlockSpec((STRETCH, E), lambda b: (b, 0))
    states = pl.BlockSpec((1, 2 * STATE, E), lambda b: (b, 0, 0))
    return pl.pallas_call(
        mixer_back_kernel,
        grid=(nb,),
        in_specs=[
            pl.BlockSpec(memory_space=pltpu.SMEM),
            pl.BlockSpec((STRETCH, CHANNELS), lambda b: (b, 0)),
            line,
            pl.BlockSpec((STRETCH, 2 * E), lambda b: (b, 0)),
            sq,
            pl.BlockSpec((1, LANES, STRETCH), lambda b: (b, 0, 0)),
            sq,
            sq,
            states,
            whole(p.shape),
            whole(got.shape),
            whole(tot.shape),
            sq,
            whole((8, LANES)),
        ],
        out_specs=[
            line,
            pl.BlockSpec((STRETCH, 2 * LANES), lambda b: (b, 0)),
            sq,
            whole((16, LANES)),
        ],
        out_shape=[
            jax.ShapeDtypeStruct((length, E), BF16),
            jax.ShapeDtypeStruct((length, 2 * LANES), F32),
            jax.ShapeDtypeStruct((length, LANES), BF16),
            jax.ShapeDtypeStruct((16, LANES), F32),
        ],
        scratch_shapes=[
            pltpu.VMEM((2 * LANES, 2 * E), BF16),
            pltpu.VMEM((2 * E, LANES), BF16),
            pltpu.VMEM(p.shape, BF16),
            pltpu.VMEM((STRETCH, 2 * E), F32),
            pltpu.VMEM((STRETCH, 2 * E), BF16),
            pltpu.VMEM((STRETCH + 16, 2 * E), BF16),
            pltpu.VMEM((STATE, E), F32),
            pltpu.VMEM((8, E), F32),
        ],
        compiler_params=params(26),
        cost_estimate=cost(16e9, 20 << 20),
        name="mixer_back",
    )(me, in_hbm(act), dy, yz, in_hbm(v), in_hbm(ut), in_hbm(wv), gain, ent, p, got, tot, dtraw, hp)


def conv_back_block(length, dact_ref, slope_ref, conv_ref, taps_ref, dconv_ref, sums_ref, dpad_ref, edge_ref, shift_ref):
    half = TAPS // 2
    fold = lambda t: jnp.sum(t.reshape(t.shape[0] // 8, 8, BLOCK), axis=0)
    sums = [jnp.zeros((8, BLOCK), F32) for _ in range(TAPS + 1)]
    zeros = jnp.zeros((MARGIN, BLOCK), BF16)
    dpad_ref[:MARGIN] = zeros
    dpad_ref[MARGIN + length :] = zeros
    for c in range(length // STRETCH):
        rows = slice(c * STRETCH, (c + 1) * STRETCH)
        dpre = dact_ref[rows] * slope_ref[rows].astype(F32)
        sums[TAPS] = sums[TAPS] + fold(dpre)
        dpad_ref[MARGIN + rows.start : MARGIN + rows.stop] = dpre.astype(BF16)
    for c in range(length // STRETCH):
        rows = slice(c * STRETCH, (c + 1) * STRETCH)
        x = conv_ref[rows].astype(F32)
        out = jnp.zeros((STRETCH, BLOCK), F32)
        for k, moved in shifted_rows(shift_ref, dpad_ref, rows.start).items():
            out = out + taps_ref[k : k + 1, :] * moved
            sums[k] = sums[k] + fold(x * moved)
        dconv_ref[rows] = out.astype(BF16)
    edge_ref[: 2 * MARGIN] = dpad_ref[: 2 * MARGIN].astype(F32)
    edge_ref[2 * MARGIN :] = dpad_ref[length:].astype(F32)
    edges = []
    for where, base in ((0, MARGIN - EDGE), (1, 3 * MARGIN)):
        first = length + where * EDGE
        x = conv_ref[length:].astype(F32)[where * EDGE : (where + 1) * EDGE]
        out = jnp.zeros((EDGE, BLOCK), F32)
        for k in range(TAPS):
            moved = edge_ref[base - k + half : base - k + half + EDGE]
            out = out + taps_ref[k : k + 1, :] * moved
            sums[k] = sums[k] + x * moved
        edges.append(out)
    dconv_ref[length:] = jnp.concatenate(edges, axis=0).astype(BF16)
    sums_ref[...] = jnp.concatenate([jnp.sum(t, axis=0, keepdims=True) for t in sums], axis=0)


def conv_back_kernel(
    dx_ref, dy_ref, dmap_ref, slope_ref, conv_ref, taps_ref, skip_ref, ddt_ref, hsum_ref, ssum_ref,
    dconv_ref, sums_ref, dact_ref, dpad_ref, edge_ref, shift_ref,
):
    j = pl.program_id(0)
    maps = E // BLOCK
    length = slope_ref.shape[0]

    @pl.when(j == 0)
    def _():
        fill_shifts(shift_ref, -1)

    @pl.when(j < maps)
    def _():
        dact_ref[...] = dx_ref[...].astype(F32) + skip_ref[0:1, :] * dy_ref[...].astype(F32)

    @pl.when(j == maps)
    def _():
        dact_ref[...] = dmap_ref[...]

    @pl.when(j <= maps)
    def _():
        conv_back_block(
            length, dact_ref, slope_ref, conv_ref, taps_ref, dconv_ref, sums_ref, dpad_ref, edge_ref, shift_ref
        )

    @pl.when(j > maps)
    def _():
        dconv_ref[:length, :LANES] = ddt_ref[...]
        dconv_ref[length:, :LANES] = jnp.zeros((2 * EDGE, LANES), BF16)
        parts = [hsum_ref[:8], hsum_ref[8:], ssum_ref[...]]
        parts = [jnp.sum(t, axis=0, keepdims=True) for t in parts]
        sums_ref[:, :LANES] = jnp.concatenate(parts + [jnp.zeros((5, LANES), F32)], axis=0)


def conv_back(dx, dy, dmap, slope, conv, taps, skip, ddt, hsums, ssums):
    ext = conv.shape[0]
    length = ext - 2 * EDGE
    early = lambda j: (0, jnp.minimum(j, E // BLOCK - 1))
    inner = lambda j: (0, jnp.minimum(j, CHANNELS // BLOCK - 1))
    col = lambda j: (0, j)
    return pl.pallas_call(
        conv_back_kernel,
        grid=(CHANNELS // BLOCK + 1,),
        in_specs=[
            pl.BlockSpec((length, BLOCK), early),
            pl.BlockSpec((length, BLOCK), early),
            whole((length, 2 * LANES)),
            pl.BlockSpec((length, BLOCK), inner),
            pl.BlockSpec((ext, BLOCK), inner),
            pl.BlockSpec((8, BLOCK), inner),
            pl.BlockSpec((8, BLOCK), early),
            whole((length, LANES)),
            whole((16, LANES)),
            whole((8, LANES)),
        ],
        out_specs=[pl.BlockSpec((ext, BLOCK), col), pl.BlockSpec((8, BLOCK), col)],
        out_shape=[
            jax.ShapeDtypeStruct((ext, WIDE), BF16),
            jax.ShapeDtypeStruct((8, WIDE), F32),
        ],
        scratch_shapes=[
            pltpu.VMEM((length, BLOCK), F32),
            pltpu.VMEM((length + 2 * MARGIN, BLOCK), BF16),
            pltpu.VMEM((4 * MARGIN, BLOCK), F32),
            pltpu.VMEM((len(SHIFTS) * STRETCH, WINDOW), BF16),
        ],
        compiler_params=params(14),
        cost_estimate=cost(2e9, 20 << 20),
        name="conv_back",
    )(dx, dy, dmap, in_hbm(slope), in_hbm(conv), taps, skip, ddt, hsums, ssums)


def send_states(payload, to_later):
    n, me = lax.axis_size("seq"), lax.axis_index("seq")
    sent, got = [], []
    for q in range(1, n):
        later = (me ^ q) > me
        first = later if to_later else ~later
        sent.append(jnp.where(first, payload[0], payload[1]))
        got.append(swap(sent[-1], "seq", q))
    return sent, got


def per_device(
    layer_in, norm_gain, in_weight, conv_weight, conv_bias, head_params, out_gain, out_weight, out_cotangent
):
    ns, nw = lax.axis_size("seq"), lax.axis_size("wt")
    ndev = ns * nw
    seq_me = lax.axis_index("seq").astype(jnp.int32)
    me = seq_me * nw + lax.axis_index("wt").astype(jnp.int32)
    me_arr, seq_arr = me.reshape(1), seq_me.reshape(1)
    tokens = layer_in[0]
    cotangent = out_cotangent[0]
    length, d = tokens.shape
    share = in_weight.shape[0]
    cshare = conv_bias.shape[0]
    gshare = out_gain.shape[0]
    spare = WIDE - (in_weight.shape[1] - E)

    small = jnp.concatenate([conv_weight.reshape(-1), conv_bias, out_gain, norm_gain])
    n_small = small.shape[0]
    small = jnp.pad(small, (0, 8 * LANES - n_small)).reshape(8, LANES)
    first = jnp.pad(in_weight[:, E:], ((0, 0), (0, spare)))
    half = E // 2
    rest = jnp.concatenate(
        [in_weight[None, :, :half], in_weight[None, :, half:E], out_weight.reshape(2, share, d)], axis=0
    )
    s1 = jnp.stack(gather_z(small)).reshape(-1, LANES)
    ends = jnp.concatenate([tokens[:EDGE], tokens[length - EDGE :]], axis=0).reshape(-1, LANES)
    s1 = jnp.concatenate([s1, ends], axis=0)
    a1 = jnp.stack(gather_z(first))
    a2 = gather_seq(a1)
    b1 = jnp.stack(gather_z(rest))
    s2 = gather_seq(after(s1, a2[1]))
    a2 = jnp.stack(a2)
    wa, wb = a2.reshape(d // 2, WIDE), swap(after(a2, b1), "wt", 1).reshape(d // 2, WIDE)

    cut = s1.shape[0] - ends.shape[0]
    around = [t[cut:].reshape(2 * EDGE, d) for t in s2]
    s2 = jnp.stack([t[:cut] for t in s2])
    s3 = swap(s2, "wt", 1)
    b2 = gather_seq(after(b1, a2, s3))
    nothing = jnp.zeros((EDGE, d), BF16)
    pick = lambda rows, other: sum((jnp.where(seq_me ^ q == other, around[q][rows], nothing) for q in range(ns)), nothing)
    ext = jnp.concatenate([tokens, pick(slice(EDGE, None), seq_me - 1), pick(slice(0, EDGE), seq_me + 1)], axis=0)

    blocks = jnp.arange(d, dtype=jnp.int32) // share
    offsets = block_order(ns, nw)
    offset_of = jnp.array(offsets, jnp.int32)
    natural = (offset_of[blocks] ^ me) * share + jnp.arange(d, dtype=jnp.int32) % share
    perm = (jnp.arange(d, dtype=jnp.int32)[:, None] == natural[None, :]).astype(BF16)
    u_x = dot(ext, perm)
    inv_in = lax.rsqrt(jnp.mean(jnp.square(ext.astype(F32)), axis=1, keepdims=True) + EPSILON)

    extras = jnp.stack([s2, s3]).reshape(ndev, 8 * LANES)
    order = jnp.arange(ndev, dtype=jnp.int32)[:, None] == (offset_of[None, :] ^ me)
    nat = dot(order.astype(BF16), extras[:, :n_small])
    taps = jnp.transpose(nat[:, : TAPS * cshare].reshape(ndev, TAPS, cshare), (1, 0, 2)).reshape(TAPS, CHANNELS)
    bias = nat[:, TAPS * cshare : (TAPS + 1) * cshare].reshape(1, CHANNELS)
    taps = jnp.concatenate([taps, bias], axis=0)
    gain_out = nat[:, (TAPS + 1) * cshare : (TAPS + 1) * cshare + gshare].reshape(1, E)
    gain_x = extras[:, n_small - share : n_small].reshape(1, d).astype(F32)

    normed = (u_x * inv_in * gain_x).astype(BF16)
    conv, act, slope, dtraw = conv_forward(normed, wa, wb, taps)

    twice = jnp.concatenate([head_params, head_params], axis=1)
    rates = jnp.stack([twice[0], -jnp.exp(twice[1])])
    hp = jnp.pad(rates, ((0, 6), (0, LANES - 2 * HEADS)))
    u, v, ut, vt, eu, wv, tot, s, pay = block_states(act, dtraw, hp)
    sent, got = send_states(pay, True)
    b2 = [after(t, *sent).reshape(-1, share, half) for t in b2]
    w_z, w_out = unpack(offsets, me_arr, b2 + [swap(t, "wt", 1) for t in b2])
    w_z, w_out = w_z.reshape(d, E), w_out.reshape(E, d)
    own = normed[:length]
    z = dot(own, w_z).astype(BF16)
    dgated = dot_nt(cotangent, w_out).astype(BF16)
    skip = jnp.repeat(head_params[2], HDIM)[None]
    rows = jnp.concatenate([skip, gain_out, jnp.zeros((6, E), F32)], axis=0)
    got = jnp.stack([after(t, z, dgated) for t in got])
    gated, dz, dy, yz, gain, ent, p, pay, ssums = gate(seq_arr, act, z, dgated, u, vt, eu, s, got, tot, rows)
    sent, got = send_states(pay, False)

    gated_then, dz_then = after(gated, *sent), after(dz, *sent)
    g_out = lax.dot_general(gated_then, cotangent, TN, preferred_element_type=F32).astype(BF16)
    g_z = lax.dot_general(own, dz_then, TN, preferred_element_type=F32).astype(BF16)
    dn_z = dot_nt(dz_then, w_z)
    layer_out = (tokens.astype(F32) + dot(gated_then, w_out)).astype(BF16)[None]
    got = [after(t, g_out, g_z, dn_z, layer_out) for t in got]
    kept, moved = pack(offsets, me_arr, g_z.reshape(ndev, share, E), g_out.reshape(2 * ndev, share, d))
    moved = swap(moved, "wt", 1)
    split = lambda t: t.reshape(ns, nw // 2, 4, share, half)
    r1 = scatter_core(split(kept), split(after(moved, *got)))
    r_got = [swap(r1[q], "seq", q) for q in range(1, ns)]
    dx, dmap, ddt, hsums = mixer_back(
        seq_arr, act, after(dy, *r1), yz, v, ut, wv, gain, ent, p, jnp.stack(got), tot, dtraw, hp
    )
    r2 = scatter_seq(r1, [after(t, dx) for t in r_got])
    z_got = [swap(r2[q], "wt", 2 * q) for q in range(1, nw // 2)]
    dconv, csums = conv_back(after(dx, *r2), dy, dmap, slope, conv, taps, rows, ddt, hsums, ssums)
    r3 = scatter_z(r2, [after(t, dconv) for t in z_got])

    g_c = lax.dot_general(normed, dconv, TN, preferred_element_type=F32).astype(BF16)
    g_c = g_c.reshape(2, ns, nw // 2, share, WIDE)
    steps = sum_steps(ns, nw)
    csums = csums + swap(csums, *steps[0])
    sent = after(g_c[1], r3, csums)
    f1 = scatter_core(g_c[0], swap(sent, "wt", 1))
    w_first = jnp.concatenate([wa, wb])
    dn = dot_nt(after(dconv, *f1), w_first)
    f_got = [swap(f1[q], "seq", q) for q in range(1, ns)]
    f2 = scatter_seq(f1, f_got)
    dn = dn + jnp.concatenate([dn_z, jnp.zeros((2 * EDGE, d), F32)], axis=0)
    grad_first = scatter_z(f2)
    for (axis, q), wait in zip(steps[1:], [f1, [dn]] + [[]] * len(steps)):
        csums = csums + after(swap(csums, axis, q), *wait)

    forward = [(i, i + 1) for i in range(ns - 1)]
    backward = [(i + 1, i) for i in range(ns - 1)]
    dn_hi = dn.astype(BF16)
    dn_lo = (dn - dn_hi.astype(F32)).astype(BF16)
    dn = dot_nt(dn_hi, perm) + dot_nt(dn_lo, perm)
    edges = after(dn[length:], f_got[0])
    prev_edge = lax.ppermute(edges[:EDGE], "seq", backward)
    next_edge = lax.ppermute(edges[EDGE:], "seq", forward)
    middle = jnp.zeros((length - 2 * EDGE, d), F32)
    dn = dn[:length] + jnp.concatenate([next_edge, middle, prev_edge], axis=0)
    u, inv = tokens.astype(F32), inv_in[:length]
    scaled = nat[:, n_small - share :].reshape(1, d) * dn
    in_grad = after(cotangent, *f2).astype(F32) + inv * scaled
    in_grad = in_grad - u * inv**3 * jnp.mean(scaled * u, axis=1, keepdims=True)

    grad_z = jnp.concatenate([r3[0], r3[1]], axis=1)
    grad_out = r3[2:].reshape(gshare, d)
    vec = lax.dynamic_slice(csums, (0, me * cshare), (8, cshare))
    pair = csums[:3, CHANNELS : CHANNELS + 2 * HEADS]
    head_grad = pair[:, :HEADS] + pair[:, HEADS:]
    grad_in = jnp.concatenate([grad_z, grad_first[:, : WIDE - spare]], axis=1)
    gain_grad = jnp.sum(in_weight.astype(F32) * grad_in, axis=1) / norm_gain.astype(F32)
    out_gain_grad = jnp.sum(out_weight.astype(F32) * grad_out, axis=1) / out_gain.astype(F32)
    return (
        layer_out,
        in_grad[None],
        gain_grad,
        grad_in,
        vec[:TAPS],
        vec[TAPS],
        head_grad,
        out_gain_grad,
        grad_out,
    )


def solution(mesh):
    rows = P(("seq", "wt"))
    table = P(("seq", "wt"), None)
    tokens = P("wt", "seq", None)
    taps = P(None, ("seq", "wt"))
    return jax.shard_map(
        per_device,
        mesh=mesh,
        in_specs=(tokens, rows, table, taps, rows, P(), rows, table, tokens),
        out_specs=(tokens, tokens, rows, table, taps, rows, P(), rows, table),
        check_vma=False,
    )
```

```python
import functools

import jax
import jax.numpy as jnp
from jax import lax
from jax.experimental import pallas as pl
from jax.experimental.pallas import tpu as pltpu
from jax.sharding import PartitionSpec as P

HEADS = 24
HDIM = 64
STATE = 64
STRETCH = 128
TAPS = 7
E = 1536
CHANNELS = 1792
PAIRS = HEADS // 2
LANES = 128
WIDE = 1920
EDGE = 8
EPSILON = 1e-05
LOG2E = 1.4426950408889634

F32 = jnp.float32
BF16 = jnp.bfloat16
NT = (((1,), (1,)), ((), ()))
TN = (((0,), (0,)), ((), ()))


def dot(a, b):
    return jnp.dot(a, b, preferred_element_type=F32)


def dot_nt(a, b):
    return lax.dot_general(a, b, NT, preferred_element_type=F32)


def params(limit=56):
    return pltpu.CompilerParams(vmem_limit_bytes=limit << 20)


def cost(flops, moved, trans=0):
    return pl.CostEstimate(flops=int(flops), bytes_accessed=int(moved), transcendentals=int(trans))


def whole(shape):
    return pl.BlockSpec(shape, lambda *_: (0,) * len(shape), pipeline_mode=pl.Buffered(1))


def swap(x, axis, q):
    n = lax.axis_size(axis)
    return lax.ppermute(x, axis, [(i, i ^ q) for i in range(n)])


def gather_z(x):
    return [x] + [swap(x, "wt", 2 * q) for q in range(1, lax.axis_size("wt") // 2)]


def gather_seq(x):
    return [x] + [swap(x, "seq", q) for q in range(1, lax.axis_size("seq"))]


def block_order(ns, nw):
    return [s * nw + 2 * z + c for c in range(2) for s in range(ns) for z in range(nw // 2)]


def low(t):
    return t.astype(BF16)


def up(t):
    return t.astype(F32)


def scatter_core(kept, got):
    return [low(up(kept[q]) + up(got[q])) for q in range(kept.shape[0])]


def scatter_seq(a, got=None):
    if got is None:
        got = [swap(a[q], "seq", q) for q in range(1, len(a))]
    total = lambda z: sum((up(t[z]) for t in got), up(a[0][z]))
    return [low(total(z)) for z in range(a[0].shape[0])]


def scatter_z(b, got=None):
    if got is None:
        got = [swap(b[q], "wt", 2 * q) for q in range(1, len(b))]
    return sum((up(t) for t in got), up(b[0]))


def sum_steps(ns, nw):
    return [("seq", q) for q in (1, 2, 4, 8) if q < ns] + [("wt", q) for q in (2, 4, 8, 16) if q < nw] + [("wt", 1)]


def after(x, *others):
    return lax.optimization_barrier((x, *others))[0]


def unpack_kernel(order, me_ref, *refs):
    parts, (z_ref, o_ref) = refs[:-2], refs[-2:]
    half = o_ref.shape[2]
    count = parts[0].shape[0] // 4
    for p, offset in enumerate(order):
        x_ref, k = parts[p // count], 4 * (p % count)
        z_ref[p, :, :half] = x_ref[k]
        z_ref[p, :, half:] = x_ref[k + 1]
        target = 2 * jnp.bitwise_xor(me_ref[0], offset)
        o_ref[target] = x_ref[k + 2]
        o_ref[target + 1] = x_ref[k + 3]


def unpack(order, me, parts):
    _, share, half = parts[0].shape
    n = len(order)
    shapes = [(n, share, 2 * half), (2 * n, share, half)]
    return pl.pallas_call(
        functools.partial(unpack_kernel, order),
        grid=(1,),
        out_shape=[jax.ShapeDtypeStruct(s, parts[0].dtype) for s in shapes],
        in_specs=[pl.BlockSpec(memory_space=pltpu.SMEM)] + [whole(t.shape) for t in parts],
        out_specs=[whole(s) for s in shapes],
        compiler_params=params(12),
        cost_estimate=cost(0, 16 * n * share * half),
        name="unpack",
    )(me, *parts)


def pack_kernel(order, me_ref, z_ref, o_ref, a_ref, b_ref):
    half = a_ref.shape[2]
    count = a_ref.shape[0] // 4
    for p, offset in enumerate(order):
        x_ref, k = (a_ref, 4 * p) if p < count else (b_ref, 4 * (p - count))
        x_ref[k] = z_ref[p, :, :half]
        x_ref[k + 1] = z_ref[p, :, half:]
        source = 2 * jnp.bitwise_xor(me_ref[0], offset)
        x_ref[k + 2] = o_ref[source]
        x_ref[k + 3] = o_ref[source + 1]


def pack(order, me, z, o):
    n, share, wide = z.shape
    shape = (2 * n, share, wide // 2)
    return pl.pallas_call(
        functools.partial(pack_kernel, order),
        grid=(1,),
        out_shape=[jax.ShapeDtypeStruct(shape, z.dtype)] * 2,
        in_specs=[pl.BlockSpec(memory_space=pltpu.SMEM), whole(z.shape), whole(o.shape)],
        out_specs=[whole(shape)] * 2,
        compiler_params=params(12),
        cost_estimate=cost(0, 8 * z.size),
        name="pack",
    )(me, z, o)


BLOCK = 256


SHIFTS = [k for k in range(TAPS) if k != TAPS // 2]
MARGIN = 16
WINDOW = STRETCH + 2 * MARGIN


def fill_shifts(shift_ref, sign):
    for n, k in enumerate(SHIFTS):
        picked = iota((STRETCH, WINDOW), 0) + (MARGIN + sign * (k - TAPS // 2))
        same = iota((STRETCH, WINDOW), 1) == picked
        shift_ref[n * STRETCH : (n + 1) * STRETCH, :] = jnp.where(same, 1.0, 0.0).astype(BF16)


def shifted_rows(shift_ref, pad_ref, first):
    rows = dot(shift_ref[...], pad_ref[first : first + WINDOW, :])
    out = {k: rows[n * STRETCH : (n + 1) * STRETCH] for n, k in enumerate(SHIFTS)}
    out[TAPS // 2] = pad_ref[first + MARGIN : first + MARGIN + STRETCH, :].astype(F32)
    return out


def conv_kernel(
    nx_ref, wa_ref, wb_ref, da_ref, db_ref, taps_ref, conv_ref, act_ref, slope_ref, dt_ref, pad_ref, shift_ref
):
    length = act_ref.shape[0]

    @pl.when(pl.program_id(0) == 0)
    def _():
        fill_shifts(shift_ref, 1)
        pad_ref[...] = jnp.zeros_like(pad_ref)

    w = jnp.concatenate([wa_ref[...], wb_ref[...]], axis=0)
    zeros = jnp.zeros((EDGE, BLOCK), BF16)
    r = dot(nx_ref[length:], w).astype(BF16)
    conv_ref[length:] = r
    pad_ref[:MARGIN] = jnp.concatenate([zeros, r[:EDGE]], axis=0)
    pad_ref[MARGIN + length :] = jnp.concatenate([r[EDGE:], zeros], axis=0)
    count = length // STRETCH
    for c in range(count + 1):
        if c < count:
            rows = slice(c * STRETCH, (c + 1) * STRETCH)
            r = dot(nx_ref[rows], w).astype(BF16)
            conv_ref[rows] = r
            pad_ref[MARGIN + rows.start : MARGIN + rows.stop] = r
        if c > 0:
            first = (c - 1) * STRETCH
            pre = jnp.broadcast_to(taps_ref[TAPS : TAPS + 1, :], (STRETCH, BLOCK))
            for k, x in shifted_rows(shift_ref, pad_ref, first).items():
                pre = pre + taps_ref[k : k + 1, :] * x
            sig = jax.nn.sigmoid(pre)
            act = pre * sig
            rows = slice(first, first + STRETCH)
            act_ref[rows] = act.astype(BF16)
            slope_ref[rows] = (sig + act * (1.0 - sig)).astype(BF16)

    @pl.when(pl.program_id(0) == pl.num_programs(0) - 1)
    def _():
        w = jnp.concatenate([da_ref[...], db_ref[...]], axis=0)
        dt_ref[...] = dot(nx_ref[:length], w)


def conv_forward(normed, wa, wb, taps):
    ext, d = normed.shape
    length = ext - 2 * EDGE
    col = lambda j: (0, j)
    steps = pl.BlockSpec((d // 2, LANES), lambda j: (0, CHANNELS // LANES))
    return pl.pallas_call(
        conv_kernel,
        grid=(CHANNELS // BLOCK,),
        in_specs=[
            whole((ext, d)),
            pl.BlockSpec((d // 2, BLOCK), col),
            pl.BlockSpec((d // 2, BLOCK), col),
            steps,
            steps,
            pl.BlockSpec((8, BLOCK), col),
        ],
        out_specs=[
            pl.BlockSpec((ext, BLOCK), col),
            pl.BlockSpec((length, BLOCK), col),
            pl.BlockSpec((length, BLOCK), col),
            whole((length, LANES)),
        ],
        out_shape=[
            hbm((ext, CHANNELS), BF16),
            hbm((length, CHANNELS), BF16),
            hbm((length, CHANNELS), BF16),
            jax.ShapeDtypeStruct((length, LANES), F32),
        ],
        scratch_shapes=[
            pltpu.VMEM((length + 2 * MARGIN, BLOCK), BF16),
            pltpu.VMEM((len(SHIFTS) * STRETCH, WINDOW), BF16),
        ],
        compiler_params=params(14),
        cost_estimate=cost(2 * ext * d * WIDE, 16 << 20),
        name="conv_forward",
    )(normed, wa, wb, wa, wb, taps)


def hbm(shape, kind):
    return pltpu.HBM(shape, kind)


def in_hbm(x):
    return pltpu.with_memory_space_constraint(x, pltpu.HBM)


def iota(shape, dim):
    return lax.broadcasted_iota(jnp.int32, shape, dim)


def fill_expand(exp_ref):
    for c in range(2 * E // LANES):
        row = jnp.bitwise_and(iota((2 * LANES, LANES), 0), LANES - 1)
        head = 2 * c + jnp.where(iota((2 * LANES, LANES), 1) >= HDIM, 1, 0)
        exp_ref[:, c * LANES : (c + 1) * LANES] = jnp.where(row == head, 1.0, 0.0).astype(BF16)


def fill_heads(heads_ref):
    for c in range(2 * PAIRS):
        row = iota((LANES, LANES), 0)
        head = 2 * (c % PAIRS) + jnp.where(row >= HDIM, 1, 0)
        head = head + jnp.where(jnp.bitwise_and(row, HDIM - 1) >= HDIM // 2, HEADS, 0)
        same = iota((LANES, LANES), 1) == head
        heads_ref[c * LANES : (c + 1) * LANES, :] = jnp.where(same, 1.0, 0.0).astype(BF16)


def fold_pair(f, r, first):
    half = HDIM // 2
    return jnp.where(first, f + pltpu.roll(f, LANES - half, 1), r + pltpu.roll(r, half, 1))


def two_parts(x):
    hi = x.astype(BF16)
    lo = (x - hi.astype(F32)).astype(BF16)
    return jnp.concatenate([hi, lo], axis=1)


CHUNKS = [slice(c * 2 * LANES, (c + 1) * 2 * LANES) for c in range(E // (2 * LANES))]
PAIR_COLS = [slice(p * LANES, (p + 1) * LANES) for p in range(PAIRS)]


def shifted(cols):
    return slice(cols.start + E, cols.stop + E)


def pair_rows(row, p, first):
    h = first + 2 * p
    left = iota((8, LANES), 1) < HDIM
    return jnp.where(left, row[:, h : h + 1], row[:, h + 1 : h + 2])


def scan_states(out_ref, state_ref, tot_ref, add_ref, first, backward):
    rows = slice(0, STATE) if first == 0 else slice(STATE, 2 * STATE)
    order = range(add_ref.shape[0])
    for c in reversed(order) if backward else order:
        dec = jnp.exp2(tot_ref[c])
        for p, cols in enumerate(PAIR_COLS):
            state = state_ref[:, cols]
            out_ref[c, rows, cols] = state.astype(BF16)
            state_ref[:, cols] = pair_rows(dec, p, first)[0:1] * state + add_ref[c, rows, cols].astype(F32)


def step_sizes(dtraw, hp_ref):
    lane = iota(dtraw.shape, 1)
    pre = jnp.where(lane < 2 * HEADS, dtraw + hp_ref[0:1, :], 0.0)
    dt = jnp.maximum(pre, 0.0) + jnp.log1p(jnp.exp(-jnp.abs(pre)))
    return pre, dt, hp_ref[1:2, :] * dt


def states_kernel(
    act_ref, dtraw_ref, hp_ref, u_ref, v_ref, ut_ref, vt_ref, eu_ref, wv_ref, tot_ref, s_ref, pay_ref,
    exp_ref, dev_ref, cum_ref, z_ref,
):
    b = pl.program_id(0)
    nb = pl.num_programs(0)

    @pl.when(b == 0)
    def _():
        fill_expand(exp_ref)
        dev_ref[...] = jnp.zeros_like(dev_ref)
        cum_ref[...] = jnp.zeros_like(cum_ref)

    sq = (STRETCH, LANES)
    lane = iota(sq, 1)
    forward = lane < HEADS
    _, dt, lg = step_sizes(dtraw_ref[...], hp_ref)
    dtb = dt.astype(BF16).astype(F32)
    lgb = lg.astype(BF16)
    upto = jnp.where(iota(sq, 0) >= iota(sq, 1), 1.0, 0.0).astype(BF16)
    run = dot(upto, lgb)
    before = run - lgb.astype(F32)
    total = run[STRETCH - 1 : STRETCH, :] * LOG2E
    logdt = jnp.where(dtb > 0.0, jnp.log(jnp.where(dtb > 0.0, dtb, 1.0)) * LOG2E, -1e30)
    u = jnp.where(forward, before, -run) * LOG2E
    v = jnp.where(forward, -run, before) * LOG2E + logdt
    u_ref[...] = u
    v_ref[...] = v
    ut_ref[0] = u.T
    vt_ref[0] = v.T
    eu = jnp.exp2(u + jnp.where(forward, 0.0, total))
    wv = jnp.exp2(v + jnp.where(forward, total, 0.0))
    eu_ref[...] = eu
    wv_ref[...] = wv
    total8 = jnp.broadcast_to(total, (8, LANES))
    tot_ref[0] = total8

    bt = act_ref[:, E : E + LANES].T
    w2 = two_parts(wv)
    for cols in CHUNKS:
        x = act_ref[:, cols].astype(F32)
        z_ref[:, cols] = (x * dot(w2, exp_ref[:, cols])).astype(BF16)
        z_ref[:, shifted(cols)] = (x * dot(w2, exp_ref[:, shifted(cols)])).astype(BF16)
    dec = jnp.exp2(total8)
    pre = jnp.exp2(cum_ref[...])
    for c, cols in enumerate(CHUNKS):
        sf = dot(bt[:STATE], z_ref[:, cols])
        sr = dot(bt[STATE:], z_ref[:, shifted(cols)])
        s_ref[0, :STATE, cols] = sf.astype(BF16)
        s_ref[0, STATE:, cols] = sr.astype(BF16)
        dec_f = jnp.concatenate([pair_rows(dec, 2 * c, 0), pair_rows(dec, 2 * c + 1, 0)], axis=1)
        pre_r = jnp.concatenate([pair_rows(pre, 2 * c, HEADS), pair_rows(pre, 2 * c + 1, HEADS)], axis=1)
        dev_ref[:STATE, cols] = dec_f[0:1] * dev_ref[:STATE, cols] + sf
        dev_ref[STATE:, cols] = dev_ref[STATE:, cols] + pre_r[0:1] * sr
    cum_ref[...] = cum_ref[...] + total8

    @pl.when(b == nb - 1)
    def _():
        write_payload(pay_ref, dev_ref, cum_ref)


def write_payload(pay_ref, dev_ref, cum_ref):
    cum = cum_ref[...]
    pay_ref[0, :STATE] = dev_ref[:STATE].astype(BF16)
    pay_ref[1, :STATE] = dev_ref[STATE:].astype(BF16)
    for k in range(2):
        for p, cols in enumerate(PAIR_COLS):
            row = pair_rows(cum, p, k * HEADS)
            pay_ref[k, STATE:, cols] = jnp.concatenate([row, row], axis=0).astype(BF16)


PAY = STATE + 16


def block_states(act, dtraw, hp):
    length = act.shape[0]
    nb = length // STRETCH
    sq = pl.BlockSpec((STRETCH, LANES), lambda b: (b, 0))
    cube = pl.BlockSpec((1, STRETCH, LANES), lambda b: (b, 0, 0))
    flat = jax.ShapeDtypeStruct((length, LANES), F32)
    deep = jax.ShapeDtypeStruct((nb, LANES, STRETCH), F32)
    return pl.pallas_call(
        states_kernel,
        grid=(nb,),
        in_specs=[pl.BlockSpec((STRETCH, CHANNELS), lambda b: (b, 0)), sq, whole((8, LANES))],
        out_specs=[
            sq, sq, cube, cube, sq, sq,
            pl.BlockSpec((1, 8, LANES), lambda b: (b, 0, 0)),
            pl.BlockSpec((1, 2 * STATE, E), lambda b: (b, 0, 0)),
            whole((2, PAY, E)),
        ],
        out_shape=[
            flat, hbm((length, LANES), F32), hbm((nb, LANES, STRETCH), F32), deep, flat, hbm((length, LANES), F32),
            jax.ShapeDtypeStruct((nb, 8, LANES), F32),
            hbm((nb, 2 * STATE, E), BF16),
            jax.ShapeDtypeStruct((2, PAY, E), BF16),
        ],
        scratch_shapes=[
            pltpu.VMEM((2 * LANES, 2 * E), BF16),
            pltpu.VMEM((2 * STATE, E), F32),
            pltpu.VMEM((8, LANES), F32),
            pltpu.VMEM((STRETCH, 2 * E), BF16),
        ],
        compiler_params=params(12),
        cost_estimate=cost(4e9, 12 << 20),
        name="block_states",
    )(in_hbm(act), dtraw, hp)


def from_others(me, got_ref, upward):
    n = got_ref.shape[0] + 1
    side = lambda d: (d < me) if upward else (d > me)
    total = jnp.zeros((STATE, E), F32)
    for q in range(1, n):
        d = jnp.bitwise_xor(me, q)
        log = jnp.zeros((1, E), F32)
        for k in range(1, n):
            if k != q:
                e = jnp.bitwise_xor(me, k)
                between = ((d < e) & (e < me)) if upward else ((me < e) & (e < d))
                row = got_ref[k - 1, STATE : STATE + 1, :].astype(F32)
                log = log + jnp.where(between, row, 0.0)
        term = jnp.exp2(log) * got_ref[q - 1, :STATE, :].astype(F32)
        total = total + jnp.where(side(d), term, 0.0)
    return total


MAPS = slice(E, E + LANES), slice(E + LANES, E + 2 * LANES)


def split_store(ref, rows, cols, value):
    hi = value.astype(BF16)
    ref[rows, cols] = hi
    ref[rows, shifted(cols)] = (value - hi.astype(F32)).astype(BF16)


def sigmoid(x):
    return 0.5 * jnp.tanh(0.5 * x) + 0.5


def gate_kernel(
    me_ref, act_ref, z_ref, dg_ref, u_ref, vt_ref, eu_ref, s_ref, got_ref, tot_ref, rows_ref,
    gated_ref, dz_ref, dy_ref, yz_ref, gain_ref, ent_ref, p_ref, pay_ref, skip_ref,
    exp_ref, heads_ref, dev_ref, cum_ref, e_ref, y_ref, yv_ref, sig_ref, prod_ref, sums_ref, state_ref,
):
    b = pl.program_id(0)
    nb = pl.num_programs(0)

    @pl.when(b == 0)
    def _():
        fill_expand(exp_ref)
        fill_heads(heads_ref)
        dev_ref[...] = jnp.zeros_like(dev_ref)
        cum_ref[...] = jnp.zeros_like(cum_ref)
        sums_ref[...] = jnp.zeros_like(sums_ref)
        me = me_ref[0]
        state_ref[...] = from_others(me, got_ref, True)
        scan_states(ent_ref, state_ref, tot_ref, s_ref, 0, False)
        state_ref[...] = from_others(me, got_ref, False)
        scan_states(ent_ref, state_ref, tot_ref, s_ref, HEADS, True)

    sq = (STRETCH, STRETCH)
    i, j = iota(sq, 0), iota(sq, 1)
    after_j, at = i > j, i >= j
    lower = jnp.where(after_j, 1.0, 0.0).astype(BF16)
    upper = jnp.where(at, 0.0, 1.0).astype(BF16)
    bm, cm = act_ref[:, MAPS[0]], act_ref[:, MAPS[1]]
    cf, cr = cm[:, :STATE], cm[:, STATE:]
    gram = jnp.where(after_j, dot_nt(cf, bm[:, :STATE]), jnp.where(at, 0.0, dot_nt(cr, bm[:, STATE:])))
    left = iota((STRETCH, LANES), 1) < HDIM
    first_half = jnp.bitwise_and(iota((STRETCH, LANES), 1), HDIM - 1) < HDIM // 2

    e2 = two_parts(eu_ref[...])
    for cols in CHUNKS:
        for c, state in ((cf, ent_ref[b, :STATE, cols]), (cr, ent_ref[b, STATE:, cols])):
            at_cols = cols if c is cf else shifted(cols)
            e = dot(e2, exp_ref[:, at_cols])
            e_ref[:, at_cols] = e
            y_ref[:, at_cols] = e * dot(c, state)

    square = jnp.zeros((STRETCH, LANES), F32)
    cross = jnp.zeros((STRETCH, LANES), F32)
    for p, cols in enumerate(PAIR_COLS):
        mats = []
        for h in (2 * p, 2 * p + 1):
            r = HEADS + h
            row = jnp.where(at, u_ref[:, h : h + 1], u_ref[:, r : r + 1])
            col = jnp.where(after_j, vt_ref[0, h : h + 1, :], vt_ref[0, r : r + 1, :])
            mats.append((jnp.exp2(row + col) * gram).astype(BF16))
        mats = [m * lower for m in mats] + [m * upper for m in mats]
        y = dot(jnp.concatenate(mats, axis=0), act_ref[:, cols])
        yf = y_ref[:, cols] + jnp.where(left, y[:STRETCH], y[STRETCH : 2 * STRETCH])
        yr = y_ref[:, shifted(cols)] + jnp.where(left, y[2 * STRETCH : 3 * STRETCH], y[3 * STRETCH :])
        y_ref[:, cols] = yf
        y_ref[:, shifted(cols)] = yr
        yv = yf + yr + rows_ref[0:1, cols] * act_ref[:, cols].astype(F32)
        yv_ref[:, cols] = yv
        z = z_ref[:, cols].astype(F32)
        sig = sigmoid(z)
        sig_ref[:, cols] = sig
        yg = yv * (z * sig)
        square = square + yg * yg
        cross = cross + rows_ref[1:2, cols] * dg_ref[:, cols].astype(F32) * yg
    inv = lax.rsqrt(jnp.sum(square, axis=1, keepdims=True) / E + EPSILON)
    back = inv * inv * inv * (jnp.sum(cross, axis=1, keepdims=True) / E)

    for p, cols in enumerate(PAIR_COLS):
        z = z_ref[:, cols].astype(F32)
        sig = sig_ref[:, cols]
        ga = z * sig
        yv = yv_ref[:, cols]
        yg = yv * ga
        gain = rows_ref[1:2, cols]
        gated_ref[:, cols] = (yg * inv * gain).astype(BF16)
        dyg = inv * (gain * dg_ref[:, cols].astype(F32)) - yg * back
        dy = dyg * ga
        dz_ref[:, cols] = (dyg * yv * (sig + ga * (1.0 - sig))).astype(BF16)
        low_dy = dy.astype(BF16)
        dy_ref[:, cols] = low_dy
        fold = lambda t: jnp.sum(t.reshape(STRETCH // 8, 8, LANES), axis=0)
        sums_ref[:, cols] = sums_ref[:, cols] + fold(dy * act_ref[:, cols].astype(F32))
        dy = low_dy.astype(F32)
        yz_ref[:, cols] = (e_ref[:, cols] * dy).astype(BF16)
        yz_ref[:, shifted(cols)] = (e_ref[:, shifted(cols)] * dy).astype(BF16)
        pair = fold_pair(y_ref[:, cols] * dy, y_ref[:, shifted(cols)] * dy, first_half)
        split_store(prod_ref, slice(None), cols, pair)
    gain_ref[...] = dot(prod_ref[...], heads_ref[...])

    total8 = tot_ref[b]
    dec = jnp.exp2(total8)
    pre = jnp.exp2(cum_ref[...])
    ct = cm.T
    for c, cols in enumerate(CHUNKS):
        pf = dot(ct[:STATE], yz_ref[:, cols])
        pr = dot(ct[STATE:], yz_ref[:, shifted(cols)])
        p_ref[0, :STATE, cols] = pf.astype(BF16)
        p_ref[0, STATE:, cols] = pr.astype(BF16)
        pre_f = jnp.concatenate([pair_rows(pre, 2 * c, 0), pair_rows(pre, 2 * c + 1, 0)], axis=1)
        dec_r = jnp.concatenate([pair_rows(dec, 2 * c, HEADS), pair_rows(dec, 2 * c + 1, HEADS)], axis=1)
        dev_ref[:STATE, cols] = dev_ref[:STATE, cols] + pre_f[0:1] * pf
        dev_ref[STATE:, cols] = dec_r[0:1] * dev_ref[STATE:, cols] + pr
    cum_ref[...] = cum_ref[...] + total8

    @pl.when(b == nb - 1)
    def _():
        write_payload(pay_ref, dev_ref, cum_ref)
        skip_ref[...] = lax.dot_general(
            sums_ref[...], exp_ref[:LANES, :E].astype(F32), NT,
            precision=lax.Precision.HIGHEST, preferred_element_type=F32,
        )


def gate(me, act, z, dg, u, vt, eu, s, got, tot, rows):
    length = act.shape[0]
    nb = length // STRETCH
    line = pl.BlockSpec((STRETCH, E), lambda b: (b, 0))
    sq = pl.BlockSpec((STRETCH, LANES), lambda b: (b, 0))
    low_line = jax.ShapeDtypeStruct((length, E), BF16)
    return pl.pallas_call(
        gate_kernel,
        grid=(nb,),
        in_specs=[
            pl.BlockSpec(memory_space=pltpu.SMEM),
            pl.BlockSpec((STRETCH, CHANNELS), lambda b: (b, 0)),
            line,
            line,
            sq,
            pl.BlockSpec((1, LANES, STRETCH), lambda b: (b, 0, 0)),
            sq,
            whole(s.shape),
            whole(got.shape),
            whole(tot.shape),
            whole((8, E)),
        ],
        out_specs=[
            line,
            line,
            line,
            pl.BlockSpec((STRETCH, 2 * E), lambda b: (b, 0)),
            sq,
            whole(s.shape),
            pl.BlockSpec((1, 2 * STATE, E), lambda b: (b, 0, 0)),
            whole((2, PAY, E)),
            whole((8, LANES)),
        ],
        out_shape=[
            low_line,
            low_line,
            low_line,
            jax.ShapeDtypeStruct((length, 2 * E), BF16),
            jax.ShapeDtypeStruct((length, LANES), F32),
            jax.ShapeDtypeStruct(s.shape, BF16),
            jax.ShapeDtypeStruct(s.shape, BF16),
            jax.ShapeDtypeStruct((2, PAY, E), BF16),
            jax.ShapeDtypeStruct((8, LANES), F32),
        ],
        scratch_shapes=[
            pltpu.VMEM((2 * LANES, 2 * E), BF16),
            pltpu.VMEM((2 * E, LANES), BF16),
            pltpu.VMEM((2 * STATE, E), F32),
            pltpu.VMEM((8, LANES), F32),
            pltpu.VMEM((STRETCH, 2 * E), F32),
            pltpu.VMEM((STRETCH, 2 * E), F32),
            pltpu.VMEM((STRETCH, E), F32),
            pltpu.VMEM((STRETCH, E), F32),
            pltpu.VMEM((STRETCH, 2 * E), BF16),
            pltpu.VMEM((8, E), F32),
            pltpu.VMEM((STATE, E), F32),
        ],
        compiler_params=params(30),
        cost_estimate=cost(16e9, 32 << 20),
        name="gate",
    )(me, in_hbm(act), z, dg, u, vt, eu, in_hbm(s), got, tot, rows)


def mixer_back_kernel(
    me_ref, act_ref, dy_ref, yz_ref, v_ref, ut_ref, wv_ref, gain_ref, ent_ref, p_ref, got_ref, tot_ref,
    dtraw_ref, hp_ref,
    dx_ref, dmap_ref, ddt_ref, sums_ref,
    exp_ref, heads_ref, out_ref, v_in_ref, xz_ref, prod_ref, state_ref, row_ref,
):
    b = pl.program_id(0)
    sq = (STRETCH, STRETCH)
    j, i = iota(sq, 0), iota(sq, 1)
    after_j, at = i > j, i >= j

    @pl.when(b == 0)
    def _():
        fill_expand(exp_ref)
        fill_heads(heads_ref)
        sums_ref[...] = jnp.zeros_like(sums_ref)
        row_ref[...] = jnp.zeros_like(row_ref)
        me = me_ref[0]
        state_ref[...] = from_others(me, got_ref, False)
        scan_states(out_ref, state_ref, tot_ref, p_ref, 0, True)
        state_ref[...] = from_others(me, got_ref, True)
        scan_states(out_ref, state_ref, tot_ref, p_ref, HEADS, False)

    bm, cm = act_ref[:, MAPS[0]], act_ref[:, MAPS[1]]
    bf, br, cf, cr = bm[:, :STATE], bm[:, STATE:], cm[:, :STATE], cm[:, STATE:]
    gram = jnp.where(after_j, dot_nt(bf, cf), jnp.where(at, 0.0, dot_nt(br, cr)))
    lower = jnp.where(after_j, 1.0, 0.0).astype(BF16)
    upper = jnp.where(at, 0.0, 1.0).astype(BF16)
    left = iota((STRETCH, LANES), 1) < HDIM
    first_half = jnp.bitwise_and(iota((STRETCH, LANES), 1), HDIM - 1) < HDIM // 2
    left_low = jnp.where(left, 1.0, 0.0).astype(BF16)
    right_low = jnp.where(left, 0.0, 1.0).astype(BF16)

    w2 = two_parts(wv_ref[...])
    for cols in CHUNKS:
        x = act_ref[:, cols].astype(F32)
        for k, m, state in ((0, bf, out_ref[b, :STATE, cols]), (1, br, out_ref[b, STATE:, cols])):
            at_cols = cols if k == 0 else shifted(cols)
            w = dot(w2, exp_ref[:, at_cols])
            v_in = w * dot(m, state)
            v_in_ref[:, at_cols] = v_in
            xz_ref[:, at_cols] = (w * x).astype(BF16)
            row_ref[k : k + 1, cols] = jnp.sum(v_in * x, axis=0, keepdims=True)
    p_out, s_in = out_ref[b], ent_ref[0]
    db_f = dot_nt(xz_ref[:, :E], p_out[:STATE])
    db_r = dot_nt(xz_ref[:, E:], p_out[STATE:])
    dc_f = dot_nt(yz_ref[:, :E], s_in[:STATE])
    dc_r = dot_nt(yz_ref[:, E:], s_in[STATE:])

    dgram = jnp.zeros(sq, F32)
    for p, cols in enumerate(PAIR_COLS):
        xb, dyb = act_ref[:, cols], dy_ref[:, cols]
        x = xb.astype(F32)
        dm = dot_nt(jnp.concatenate([xb * left_low, xb * right_low], axis=0), dyb)
        mats = []
        for k, h in enumerate((2 * p, 2 * p + 1)):
            r = HEADS + h
            row = jnp.where(after_j, v_ref[:, h : h + 1], v_ref[:, r : r + 1])
            col = jnp.where(at, ut_ref[0, h : h + 1, :], ut_ref[0, r : r + 1, :])
            decay = jnp.exp2(row + col)
            mats.append((decay * gram).astype(BF16))
            dgram = dgram + dm[k * STRETCH : (k + 1) * STRETCH] * decay
        mats = [m * lower for m in mats] + [m * upper for m in mats]
        d4 = dot(jnp.concatenate(mats, axis=0), dyb)
        vf = v_in_ref[:, cols] + jnp.where(left, d4[:STRETCH], d4[STRETCH : 2 * STRETCH])
        vr = v_in_ref[:, shifted(cols)] + jnp.where(left, d4[2 * STRETCH : 3 * STRETCH], d4[3 * STRETCH :])
        dx_ref[:, cols] = (vf + vr).astype(BF16)
        split_store(prod_ref, slice(0, STRETCH), cols, fold_pair(vf * x, vr * x, first_half))
    pe = p_out.astype(F32) * s_in.astype(F32)
    col_sum = lambda t: jnp.sum(t, axis=0, keepdims=True)
    row_ref[2:3, :] = col_sum(pe[:STATE])
    row_ref[3:4, :] = col_sum(pe[STATE:])
    for cols in PAIR_COLS:
        f = jnp.concatenate([row_ref[0:1, cols], row_ref[2:3, cols], jnp.zeros((14, LANES), F32)], axis=0)
        r = jnp.concatenate([row_ref[1:2, cols], row_ref[3:4, cols], jnp.zeros((14, LANES), F32)], axis=0)
        split_store(prod_ref, slice(STRETCH, STRETCH + 16), cols, fold_pair(f, r, first_half[:16]))
    sums = dot(prod_ref[...], heads_ref[...])
    dlog = sums[:STRETCH]
    through = sums[STRETCH : STRETCH + 1] + jnp.exp2(tot_ref[b])[0:1] * sums[STRETCH + 1 : STRETCH + 2]

    gfwd = jnp.where(after_j, dgram, 0.0).astype(BF16)
    grev = jnp.where(at, 0.0, dgram).astype(BF16)
    gfwd_t = gfwd.T
    grev_t = grev.T
    dmap_ref[:, :LANES] = jnp.concatenate([db_f + dot(gfwd, cf), db_r + dot(grev, cr)], axis=1)
    dmap_ref[:, LANES:] = jnp.concatenate([dc_f + dot(gfwd_t, bf), dc_r + dot(grev_t, br)], axis=1)

    lane = iota((STRETCH, LANES), 1)
    forward = lane < HEADS
    gain = gain_ref[...]
    both = jnp.concatenate([gain, dlog], axis=1)
    top = both.astype(BF16)
    rest = both - top.astype(F32)
    mid = rest.astype(BF16)
    end = (rest - mid.astype(F32)).astype(BF16)
    later = dot(lower, top) + dot(lower, mid) + dot(lower, end)
    later_gain, later_dlog = later[:, :LANES], later[:, LANES:]
    dlg = jnp.where(
        forward,
        later_gain - later_dlog - dlog,
        (col_sum(gain) - later_gain - gain) - (col_sum(dlog) - later_dlog),
    )
    dlg = dlg + through
    pre, dt, lg = step_sizes(dtraw_ref[...], hp_ref)
    dtb = dt.astype(BF16).astype(F32)
    ok = (dtb > 0.0) & (lane < 2 * HEADS)
    ddt = jnp.where(ok, dlog / jnp.where(ok, dtb, 1.0), 0.0)
    ddt = ddt.astype(BF16).astype(F32)
    dlg = jnp.where(lane < 2 * HEADS, dlg, 0.0).astype(BF16).astype(F32)
    draw = (ddt + dlg * hp_ref[1:2, :]) * jax.nn.sigmoid(pre)
    ddt_ref[...] = draw.astype(BF16)
    fold = lambda t: jnp.sum(t.reshape(STRETCH // 8, 8, LANES), axis=0)
    sums_ref[0:8] = sums_ref[0:8] + fold(draw)
    sums_ref[8:16] = sums_ref[8:16] + fold(dlg * lg)


def mixer_back(me, act, dy, yz, v, ut, wv, gain, ent, p, got, tot, dtraw, hp):
    length = act.shape[0]
    nb = length // STRETCH
    sq = pl.BlockSpec((STRETCH, LANES), lambda b: (b, 0))
    line = pl.BlockSpec((STRETCH, E), lambda b: (b, 0))
    states = pl.BlockSpec((1, 2 * STATE, E), lambda b: (b, 0, 0))
    return pl.pallas_call(
        mixer_back_kernel,
        grid=(nb,),
        in_specs=[
            pl.BlockSpec(memory_space=pltpu.SMEM),
            pl.BlockSpec((STRETCH, CHANNELS), lambda b: (b, 0)),
            line,
            pl.BlockSpec((STRETCH, 2 * E), lambda b: (b, 0)),
            sq,
            pl.BlockSpec((1, LANES, STRETCH), lambda b: (b, 0, 0)),
            sq,
            sq,
            states,
            whole(p.shape),
            whole(got.shape),
            whole(tot.shape),
            sq,
            whole((8, LANES)),
        ],
        out_specs=[
            line,
            pl.BlockSpec((STRETCH, 2 * LANES), lambda b: (b, 0)),
            sq,
            whole((16, LANES)),
        ],
        out_shape=[
            jax.ShapeDtypeStruct((length, E), BF16),
            jax.ShapeDtypeStruct((length, 2 * LANES), F32),
            jax.ShapeDtypeStruct((length, LANES), BF16),
            jax.ShapeDtypeStruct((16, LANES), F32),
        ],
        scratch_shapes=[
            pltpu.VMEM((2 * LANES, 2 * E), BF16),
            pltpu.VMEM((2 * E, LANES), BF16),
            pltpu.VMEM(p.shape, BF16),
            pltpu.VMEM((STRETCH, 2 * E), F32),
            pltpu.VMEM((STRETCH, 2 * E), BF16),
            pltpu.VMEM((STRETCH + 16, 2 * E), BF16),
            pltpu.VMEM((STATE, E), F32),
            pltpu.VMEM((8, E), F32),
        ],
        compiler_params=params(26),
        cost_estimate=cost(16e9, 20 << 20),
        name="mixer_back",
    )(me, in_hbm(act), dy, yz, in_hbm(v), in_hbm(ut), in_hbm(wv), gain, ent, p, got, tot, dtraw, hp)


def conv_back_block(length, dact_ref, slope_ref, conv_ref, taps_ref, dconv_ref, sums_ref, dpad_ref, edge_ref, shift_ref):
    half = TAPS // 2
    fold = lambda t: jnp.sum(t.reshape(t.shape[0] // 8, 8, BLOCK), axis=0)
    sums = [jnp.zeros((8, BLOCK), F32) for _ in range(TAPS + 1)]
    zeros = jnp.zeros((MARGIN, BLOCK), BF16)
    dpad_ref[:MARGIN] = zeros
    dpad_ref[MARGIN + length :] = zeros
    for c in range(length // STRETCH):
        rows = slice(c * STRETCH, (c + 1) * STRETCH)
        dpre = dact_ref[rows] * slope_ref[rows].astype(F32)
        sums[TAPS] = sums[TAPS] + fold(dpre)
        dpad_ref[MARGIN + rows.start : MARGIN + rows.stop] = dpre.astype(BF16)
    for c in range(length // STRETCH):
        rows = slice(c * STRETCH, (c + 1) * STRETCH)
        x = conv_ref[rows].astype(F32)
        out = jnp.zeros((STRETCH, BLOCK), F32)
        for k, moved in shifted_rows(shift_ref, dpad_ref, rows.start).items():
            out = out + taps_ref[k : k + 1, :] * moved
            sums[k] = sums[k] + fold(x * moved)
        dconv_ref[rows] = out.astype(BF16)
    edge_ref[: 2 * MARGIN] = dpad_ref[: 2 * MARGIN].astype(F32)
    edge_ref[2 * MARGIN :] = dpad_ref[length:].astype(F32)
    edges = []
    for where, base in ((0, MARGIN - EDGE), (1, 3 * MARGIN)):
        first = length + where * EDGE
        x = conv_ref[length:].astype(F32)[where * EDGE : (where + 1) * EDGE]
        out = jnp.zeros((EDGE, BLOCK), F32)
        for k in range(TAPS):
            moved = edge_ref[base - k + half : base - k + half + EDGE]
            out = out + taps_ref[k : k + 1, :] * moved
            sums[k] = sums[k] + x * moved
        edges.append(out)
    dconv_ref[length:] = jnp.concatenate(edges, axis=0).astype(BF16)
    sums_ref[...] = jnp.concatenate([jnp.sum(t, axis=0, keepdims=True) for t in sums], axis=0)


def conv_back_kernel(
    dx_ref, dy_ref, dmap_ref, slope_ref, conv_ref, taps_ref, skip_ref, ddt_ref, hsum_ref, ssum_ref,
    dconv_ref, sums_ref, dact_ref, dpad_ref, edge_ref, shift_ref,
):
    j = pl.program_id(0)
    maps = E // BLOCK
    length = slope_ref.shape[0]

    @pl.when(j == 0)
    def _():
        fill_shifts(shift_ref, -1)

    @pl.when(j < maps)
    def _():
        dact_ref[...] = dx_ref[...].astype(F32) + skip_ref[0:1, :] * dy_ref[...].astype(F32)

    @pl.when(j == maps)
    def _():
        dact_ref[...] = dmap_ref[...]

    @pl.when(j <= maps)
    def _():
        conv_back_block(
            length, dact_ref, slope_ref, conv_ref, taps_ref, dconv_ref, sums_ref, dpad_ref, edge_ref, shift_ref
        )

    @pl.when(j > maps)
    def _():
        dconv_ref[:length, :LANES] = ddt_ref[...]
        dconv_ref[length:, :LANES] = jnp.zeros((2 * EDGE, LANES), BF16)
        parts = [hsum_ref[:8], hsum_ref[8:], ssum_ref[...]]
        parts = [jnp.sum(t, axis=0, keepdims=True) for t in parts]
        sums_ref[:, :LANES] = jnp.concatenate(parts + [jnp.zeros((5, LANES), F32)], axis=0)


def conv_back(dx, dy, dmap, slope, conv, taps, skip, ddt, hsums, ssums):
    ext = conv.shape[0]
    length = ext - 2 * EDGE
    early = lambda j: (0, jnp.minimum(j, E // BLOCK - 1))
    inner = lambda j: (0, jnp.minimum(j, CHANNELS // BLOCK - 1))
    col = lambda j: (0, j)
    return pl.pallas_call(
        conv_back_kernel,
        grid=(CHANNELS // BLOCK + 1,),
        in_specs=[
            pl.BlockSpec((length, BLOCK), early),
            pl.BlockSpec((length, BLOCK), early),
            whole((length, 2 * LANES)),
            pl.BlockSpec((length, BLOCK), inner),
            pl.BlockSpec((ext, BLOCK), inner),
            pl.BlockSpec((8, BLOCK), inner),
            pl.BlockSpec((8, BLOCK), early),
            whole((length, LANES)),
            whole((16, LANES)),
            whole((8, LANES)),
        ],
        out_specs=[pl.BlockSpec((ext, BLOCK), col), pl.BlockSpec((8, BLOCK), col)],
        out_shape=[
            jax.ShapeDtypeStruct((ext, WIDE), BF16),
            jax.ShapeDtypeStruct((8, WIDE), F32),
        ],
        scratch_shapes=[
            pltpu.VMEM((length, BLOCK), F32),
            pltpu.VMEM((length + 2 * MARGIN, BLOCK), BF16),
            pltpu.VMEM((4 * MARGIN, BLOCK), F32),
            pltpu.VMEM((len(SHIFTS) * STRETCH, WINDOW), BF16),
        ],
        compiler_params=params(14),
        cost_estimate=cost(2e9, 20 << 20),
        name="conv_back",
    )(dx, dy, dmap, in_hbm(slope), in_hbm(conv), taps, skip, ddt, hsums, ssums)


def send_states(payload, to_later):
    n, me = lax.axis_size("seq"), lax.axis_index("seq")
    sent, got = [], []
    for q in range(1, n):
        later = (me ^ q) > me
        first = later if to_later else ~later
        sent.append(jnp.where(first, payload[0], payload[1]))
        got.append(swap(sent[-1], "seq", q))
    return sent, got


def per_device(
    layer_in, norm_gain, in_weight, conv_weight, conv_bias, head_params, out_gain, out_weight, out_cotangent
):
    ns, nw = lax.axis_size("seq"), lax.axis_size("wt")
    ndev = ns * nw
    seq_me = lax.axis_index("seq").astype(jnp.int32)
    me = seq_me * nw + lax.axis_index("wt").astype(jnp.int32)
    me_arr, seq_arr = me.reshape(1), seq_me.reshape(1)
    tokens = layer_in[0]
    cotangent = out_cotangent[0]
    length, d = tokens.shape
    share = in_weight.shape[0]
    cshare = conv_bias.shape[0]
    gshare = out_gain.shape[0]
    spare = WIDE - (in_weight.shape[1] - E)

    small = jnp.concatenate([conv_weight.reshape(-1), conv_bias, out_gain, norm_gain])
    n_small = small.shape[0]
    small = jnp.pad(small, (0, 8 * LANES - n_small)).reshape(8, LANES)
    first = jnp.pad(in_weight[:, E:], ((0, 0), (0, spare)))
    half = E // 2
    rest = jnp.concatenate(
        [in_weight[None, :, :half], in_weight[None, :, half:E], out_weight.reshape(2, share, d)], axis=0
    )
    s1 = jnp.stack(gather_z(small)).reshape(-1, LANES)
    ends = jnp.concatenate([tokens[:EDGE], tokens[length - EDGE :]], axis=0).reshape(-1, LANES)
    s1 = jnp.concatenate([s1, ends], axis=0)
    a1 = jnp.stack(gather_z(first))
    a2 = gather_seq(a1)
    b1 = jnp.stack(gather_z(rest))
    s2 = gather_seq(after(s1, a2[1]))
    a2 = jnp.stack(a2)
    wa, wb = a2.reshape(d // 2, WIDE), swap(after(a2, b1), "wt", 1).reshape(d // 2, WIDE)

    cut = s1.shape[0] - ends.shape[0]
    around = [t[cut:].reshape(2 * EDGE, d) for t in s2]
    s2 = jnp.stack([t[:cut] for t in s2])
    s3 = swap(s2, "wt", 1)
    b2 = gather_seq(after(b1, a2, s2))
    nothing = jnp.zeros((EDGE, d), BF16)
    pick = lambda rows, other: sum((jnp.where(seq_me ^ q == other, around[q][rows], nothing) for q in range(ns)), nothing)
    ext = jnp.concatenate([tokens, pick(slice(EDGE, None), seq_me - 1), pick(slice(0, EDGE), seq_me + 1)], axis=0)

    blocks = jnp.arange(d, dtype=jnp.int32) // share
    offsets = block_order(ns, nw)
    offset_of = jnp.array(offsets, jnp.int32)
    natural = (offset_of[blocks] ^ me) * share + jnp.arange(d, dtype=jnp.int32) % share
    perm = (jnp.arange(d, dtype=jnp.int32)[:, None] == natural[None, :]).astype(BF16)
    u_x = dot(ext, perm)
    inv_in = lax.rsqrt(jnp.mean(jnp.square(ext.astype(F32)), axis=1, keepdims=True) + EPSILON)

    extras = jnp.stack([s2, s3]).reshape(ndev, 8 * LANES)
    order = jnp.arange(ndev, dtype=jnp.int32)[:, None] == (offset_of[None, :] ^ me)
    nat = dot(order.astype(BF16), extras[:, :n_small])
    taps = jnp.transpose(nat[:, : TAPS * cshare].reshape(ndev, TAPS, cshare), (1, 0, 2)).reshape(TAPS, CHANNELS)
    bias = nat[:, TAPS * cshare : (TAPS + 1) * cshare].reshape(1, CHANNELS)
    taps = jnp.concatenate([taps, bias], axis=0)
    gain_out = nat[:, (TAPS + 1) * cshare : (TAPS + 1) * cshare + gshare].reshape(1, E)
    gain_x = extras[:, n_small - share : n_small].reshape(1, d).astype(F32)

    normed = (u_x * inv_in * gain_x).astype(BF16)
    conv, act, slope, dtraw = conv_forward(normed, wa, wb, taps)

    twice = jnp.concatenate([head_params, head_params], axis=1)
    rates = jnp.stack([twice[0], -jnp.exp(twice[1])])
    hp = jnp.pad(rates, ((0, 6), (0, LANES - 2 * HEADS)))
    u, v, ut, vt, eu, wv, tot, s, pay = block_states(act, dtraw, hp)
    sent, got = send_states(pay, True)
    b2 = [after(t, *sent).reshape(-1, share, half) for t in b2]
    w_z, w_out = unpack(offsets, me_arr, b2 + [swap(t, "wt", 1) for t in b2])
    w_z, w_out = w_z.reshape(d, E), w_out.reshape(E, d)
    own = normed[:length]
    z = dot(own, w_z).astype(BF16)
    dgated = dot_nt(cotangent, w_out).astype(BF16)
    skip = jnp.repeat(head_params[2], HDIM)[None]
    rows = jnp.concatenate([skip, gain_out, jnp.zeros((6, E), F32)], axis=0)
    got = jnp.stack([after(t, z, dgated) for t in got])
    gated, dz, dy, yz, gain, ent, p, pay, ssums = gate(seq_arr, act, z, dgated, u, vt, eu, s, got, tot, rows)
    sent, got = send_states(pay, False)

    gated_then, dz_then = after(gated, *sent), after(dz, *sent)
    g_out = lax.dot_general(gated_then, cotangent, TN, preferred_element_type=F32).astype(BF16)
    g_z = lax.dot_general(own, dz_then, TN, preferred_element_type=F32).astype(BF16)
    dn_z = dot_nt(dz_then, w_z)
    layer_out = (tokens.astype(F32) + dot(gated_then, w_out)).astype(BF16)[None]
    got = [after(t, g_out, g_z, dn_z, layer_out) for t in got]
    kept, moved = pack(offsets, me_arr, g_z.reshape(ndev, share, E), g_out.reshape(2 * ndev, share, d))
    moved = swap(moved, "wt", 1)
    split = lambda t: t.reshape(ns, nw // 2, 4, share, half)
    r1 = scatter_core(split(kept), split(after(moved, *got)))
    r_got = [swap(r1[q], "seq", q) for q in range(1, ns)]
    dx, dmap, ddt, hsums = mixer_back(
        seq_arr, act, after(dy, *r1), yz, v, ut, wv, gain, ent, p, jnp.stack(got), tot, dtraw, hp
    )
    r2 = scatter_seq(r1, [after(t, dx) for t in r_got])
    z_got = [swap(r2[q], "wt", 2 * q) for q in range(1, nw // 2)]
    dconv, csums = conv_back(after(dx, *r2), dy, dmap, slope, conv, taps, rows, ddt, hsums, ssums)
    r3 = scatter_z(r2, [after(t, dconv) for t in z_got])

    g_c = lax.dot_general(normed, dconv, TN, preferred_element_type=F32).astype(BF16)
    g_c = g_c.reshape(2, ns, nw // 2, share, WIDE)
    steps = sum_steps(ns, nw)
    csums = csums + swap(csums, *steps[0])
    sent = after(g_c[1], r3, csums)
    f1 = scatter_core(g_c[0], swap(sent, "wt", 1))
    w_first = jnp.concatenate([wa, wb])
    dn = dot_nt(after(dconv, *f1), w_first)
    f_got = [swap(f1[q], "seq", q) for q in range(1, ns)]
    f2 = scatter_seq(f1, f_got)
    dn = dn + jnp.concatenate([dn_z, jnp.zeros((2 * EDGE, d), F32)], axis=0)
    grad_first = scatter_z(f2)
    for (axis, q), wait in zip(steps[1:], [f1, [dn]] + [[]] * len(steps)):
        csums = csums + after(swap(csums, axis, q), *wait)

    forward = [(i, i + 1) for i in range(ns - 1)]
    backward = [(i + 1, i) for i in range(ns - 1)]
    dn_hi = dn.astype(BF16)
    dn_lo = (dn - dn_hi.astype(F32)).astype(BF16)
    dn = dot_nt(dn_hi, perm) + dot_nt(dn_lo, perm)
    edges = after(dn[length:], f_got[0])
    prev_edge = lax.ppermute(edges[:EDGE], "seq", backward)
    next_edge = lax.ppermute(edges[EDGE:], "seq", forward)
    middle = jnp.zeros((length - 2 * EDGE, d), F32)
    dn = dn[:length] + jnp.concatenate([next_edge, middle, prev_edge], axis=0)
    u, inv = tokens.astype(F32), inv_in[:length]
    scaled = nat[:, n_small - share :].reshape(1, d) * dn
    in_grad = after(cotangent, *f2).astype(F32) + inv * scaled
    in_grad = in_grad - u * inv**3 * jnp.mean(scaled * u, axis=1, keepdims=True)

    grad_z = jnp.concatenate([r3[0], r3[1]], axis=1)
    grad_out = r3[2:].reshape(gshare, d)
    vec = lax.dynamic_slice(csums, (0, me * cshare), (8, cshare))
    pair = csums[:3, CHANNELS : CHANNELS + 2 * HEADS]
    head_grad = pair[:, :HEADS] + pair[:, HEADS:]
    grad_in = jnp.concatenate([grad_z, grad_first[:, : WIDE - spare]], axis=1)
    gain_grad = jnp.sum(in_weight.astype(F32) * grad_in, axis=1) / norm_gain.astype(F32)
    out_gain_grad = jnp.sum(out_weight.astype(F32) * grad_out, axis=1) / out_gain.astype(F32)
    return (
        layer_out,
        in_grad[None],
        gain_grad,
        grad_in,
        vec[:TAPS],
        vec[TAPS],
        head_grad,
        out_gain_grad,
        grad_out,
    )


def solution(mesh):
    rows = P(("seq", "wt"))
    table = P(("seq", "wt"), None)
    tokens = P("wt", "seq", None)
    taps = P(None, ("seq", "wt"))
    return jax.shard_map(
        per_device,
        mesh=mesh,
        in_specs=(tokens, rows, table, taps, rows, P(), rows, table, tokens),
        out_specs=(tokens, tokens, rows, table, taps, rows, P(), rows, table),
        check_vma=False,
    )
```

```python
import functools

import jax
import jax.numpy as jnp
from jax import lax
from jax.experimental import pallas as pl
from jax.experimental.pallas import tpu as pltpu
from jax.sharding import PartitionSpec as P

HEADS = 24
HDIM = 64
STATE = 64
STRETCH = 128
TAPS = 7
E = 1536
CHANNELS = 1792
PAIRS = HEADS // 2
LANES = 128
WIDE = 1920
EDGE = 8
EPSILON = 1e-05
LOG2E = 1.4426950408889634

F32 = jnp.float32
BF16 = jnp.bfloat16
NT = (((1,), (1,)), ((), ()))
TN = (((0,), (0,)), ((), ()))


def dot(a, b):
    return jnp.dot(a, b, preferred_element_type=F32)


def dot_nt(a, b):
    return lax.dot_general(a, b, NT, preferred_element_type=F32)


def params(limit=56):
    return pltpu.CompilerParams(vmem_limit_bytes=limit << 20)


def cost(flops, moved, trans=0):
    return pl.CostEstimate(flops=int(flops), bytes_accessed=int(moved), transcendentals=int(trans))


def whole(shape):
    return pl.BlockSpec(shape, lambda *_: (0,) * len(shape), pipeline_mode=pl.Buffered(1))


def swap(x, axis, q):
    n = lax.axis_size(axis)
    return lax.ppermute(x, axis, [(i, i ^ q) for i in range(n)])


def gather_z(x):
    return [x] + [swap(x, "wt", 2 * q) for q in range(1, lax.axis_size("wt") // 2)]


def gather_seq(x):
    return [x] + [swap(x, "seq", q) for q in range(1, lax.axis_size("seq"))]


def block_order(ns, nw):
    return [s * nw + 2 * z + c for c in range(2) for s in range(ns) for z in range(nw // 2)]


def low(t):
    return t.astype(BF16)


def up(t):
    return t.astype(F32)


def scatter_core(kept, got):
    return [low(up(kept[q]) + up(got[q])) for q in range(kept.shape[0])]


def scatter_seq(a, got=None):
    if got is None:
        got = [swap(a[q], "seq", q) for q in range(1, len(a))]
    total = lambda z: sum((up(t[z]) for t in got), up(a[0][z]))
    return [low(total(z)) for z in range(a[0].shape[0])]


def scatter_z(b, got=None):
    if got is None:
        got = [swap(b[q], "wt", 2 * q) for q in range(1, len(b))]
    return sum((up(t) for t in got), up(b[0]))


def sum_steps(ns, nw):
    return [("seq", q) for q in (1, 2, 4, 8) if q < ns] + [("wt", q) for q in (2, 4, 8, 16) if q < nw] + [("wt", 1)]


def after(x, *others):
    return lax.optimization_barrier((x, *others))[0]


def unpack_kernel(order, me_ref, *refs):
    parts, (z_ref, o_ref) = refs[:-2], refs[-2:]
    half = o_ref.shape[2]
    count = parts[0].shape[0] // 4
    for p, offset in enumerate(order):
        x_ref, k = parts[p // count], 4 * (p % count)
        z_ref[p, :, :half] = x_ref[k]
        z_ref[p, :, half:] = x_ref[k + 1]
        target = 2 * jnp.bitwise_xor(me_ref[0], offset)
        o_ref[target] = x_ref[k + 2]
        o_ref[target + 1] = x_ref[k + 3]


def unpack(order, me, parts):
    _, share, half = parts[0].shape
    n = len(order)
    shapes = [(n, share, 2 * half), (2 * n, share, half)]
    return pl.pallas_call(
        functools.partial(unpack_kernel, order),
        grid=(1,),
        out_shape=[jax.ShapeDtypeStruct(s, parts[0].dtype) for s in shapes],
        in_specs=[pl.BlockSpec(memory_space=pltpu.SMEM)] + [whole(t.shape) for t in parts],
        out_specs=[whole(s) for s in shapes],
        compiler_params=params(12),
        cost_estimate=cost(0, 16 * n * share * half),
        name="unpack",
    )(me, *parts)


def pack_kernel(order, me_ref, z_ref, o_ref, a_ref, b_ref):
    half = a_ref.shape[2]
    count = a_ref.shape[0] // 4
    for p, offset in enumerate(order):
        x_ref, k = (a_ref, 4 * p) if p < count else (b_ref, 4 * (p - count))
        x_ref[k] = z_ref[p, :, :half]
        x_ref[k + 1] = z_ref[p, :, half:]
        source = 2 * jnp.bitwise_xor(me_ref[0], offset)
        x_ref[k + 2] = o_ref[source]
        x_ref[k + 3] = o_ref[source + 1]


def pack(order, me, z, o):
    n, share, wide = z.shape
    shape = (2 * n, share, wide // 2)
    return pl.pallas_call(
        functools.partial(pack_kernel, order),
        grid=(1,),
        out_shape=[jax.ShapeDtypeStruct(shape, z.dtype)] * 2,
        in_specs=[pl.BlockSpec(memory_space=pltpu.SMEM), whole(z.shape), whole(o.shape)],
        out_specs=[whole(shape)] * 2,
        compiler_params=params(12),
        cost_estimate=cost(0, 8 * z.size),
        name="pack",
    )(me, z, o)


BLOCK = 256


SHIFTS = [k for k in range(TAPS) if k != TAPS // 2]
MARGIN = 16
WINDOW = STRETCH + 2 * MARGIN


def fill_shifts(shift_ref, sign):
    for n, k in enumerate(SHIFTS):
        picked = iota((STRETCH, WINDOW), 0) + (MARGIN + sign * (k - TAPS // 2))
        same = iota((STRETCH, WINDOW), 1) == picked
        shift_ref[n * STRETCH : (n + 1) * STRETCH, :] = jnp.where(same, 1.0, 0.0).astype(BF16)


def shifted_rows(shift_ref, pad_ref, first):
    rows = dot(shift_ref[...], pad_ref[first : first + WINDOW, :])
    out = {k: rows[n * STRETCH : (n + 1) * STRETCH] for n, k in enumerate(SHIFTS)}
    out[TAPS // 2] = pad_ref[first + MARGIN : first + MARGIN + STRETCH, :].astype(F32)
    return out


def conv_kernel(
    nx_ref, wa_ref, wb_ref, da_ref, db_ref, taps_ref, conv_ref, act_ref, slope_ref, dt_ref, pad_ref, shift_ref
):
    length = act_ref.shape[0]

    @pl.when(pl.program_id(0) == 0)
    def _():
        fill_shifts(shift_ref, 1)
        pad_ref[...] = jnp.zeros_like(pad_ref)

    w = jnp.concatenate([wa_ref[...], wb_ref[...]], axis=0)
    zeros = jnp.zeros((EDGE, BLOCK), BF16)
    r = dot(nx_ref[length:], w).astype(BF16)
    conv_ref[length:] = r
    pad_ref[:MARGIN] = jnp.concatenate([zeros, r[:EDGE]], axis=0)
    pad_ref[MARGIN + length :] = jnp.concatenate([r[EDGE:], zeros], axis=0)
    count = length // STRETCH
    for c in range(count + 1):
        if c < count:
            rows = slice(c * STRETCH, (c + 1) * STRETCH)
            r = dot(nx_ref[rows], w).astype(BF16)
            conv_ref[rows] = r
            pad_ref[MARGIN + rows.start : MARGIN + rows.stop] = r
        if c > 0:
            first = (c - 1) * STRETCH
            pre = jnp.broadcast_to(taps_ref[TAPS : TAPS + 1, :], (STRETCH, BLOCK))
            for k, x in shifted_rows(shift_ref, pad_ref, first).items():
                pre = pre + taps_ref[k : k + 1, :] * x
            sig = jax.nn.sigmoid(pre)
            act = pre * sig
            rows = slice(first, first + STRETCH)
            act_ref[rows] = act.astype(BF16)
            slope_ref[rows] = (sig + act * (1.0 - sig)).astype(BF16)

    @pl.when(pl.program_id(0) == pl.num_programs(0) - 1)
    def _():
        w = jnp.concatenate([da_ref[...], db_ref[...]], axis=0)
        dt_ref[...] = dot(nx_ref[:length], w)


def conv_forward(normed, wa, wb, taps):
    ext, d = normed.shape
    length = ext - 2 * EDGE
    col = lambda j: (0, j)
    steps = pl.BlockSpec((d // 2, LANES), lambda j: (0, CHANNELS // LANES))
    return pl.pallas_call(
        conv_kernel,
        grid=(CHANNELS // BLOCK,),
        in_specs=[
            whole((ext, d)),
            pl.BlockSpec((d // 2, BLOCK), col),
            pl.BlockSpec((d // 2, BLOCK), col),
            steps,
            steps,
            pl.BlockSpec((8, BLOCK), col),
        ],
        out_specs=[
            pl.BlockSpec((ext, BLOCK), col),
            pl.BlockSpec((length, BLOCK), col),
            pl.BlockSpec((length, BLOCK), col),
            whole((length, LANES)),
        ],
        out_shape=[
            hbm((ext, CHANNELS), BF16),
            hbm((length, CHANNELS), BF16),
            hbm((length, CHANNELS), BF16),
            jax.ShapeDtypeStruct((length, LANES), F32),
        ],
        scratch_shapes=[
            pltpu.VMEM((length + 2 * MARGIN, BLOCK), BF16),
            pltpu.VMEM((len(SHIFTS) * STRETCH, WINDOW), BF16),
        ],
        compiler_params=params(14),
        cost_estimate=cost(2 * ext * d * WIDE, 16 << 20),
        name="conv_forward",
    )(normed, wa, wb, wa, wb, taps)


def hbm(shape, kind):
    return pltpu.HBM(shape, kind)


def in_hbm(x):
    return pltpu.with_memory_space_constraint(x, pltpu.HBM)


def iota(shape, dim):
    return lax.broadcasted_iota(jnp.int32, shape, dim)


def fill_expand(exp_ref):
    for c in range(2 * E // LANES):
        row = jnp.bitwise_and(iota((2 * LANES, LANES), 0), LANES - 1)
        head = 2 * c + jnp.where(iota((2 * LANES, LANES), 1) >= HDIM, 1, 0)
        exp_ref[:, c * LANES : (c + 1) * LANES] = jnp.where(row == head, 1.0, 0.0).astype(BF16)


def fill_heads(heads_ref):
    for c in range(2 * PAIRS):
        row = iota((LANES, LANES), 0)
        head = 2 * (c % PAIRS) + jnp.where(row >= HDIM, 1, 0)
        head = head + jnp.where(jnp.bitwise_and(row, HDIM - 1) >= HDIM // 2, HEADS, 0)
        same = iota((LANES, LANES), 1) == head
        heads_ref[c * LANES : (c + 1) * LANES, :] = jnp.where(same, 1.0, 0.0).astype(BF16)


def fold_pair(f, r, first):
    half = HDIM // 2
    return jnp.where(first, f + pltpu.roll(f, LANES - half, 1), r + pltpu.roll(r, half, 1))


def two_parts(x):
    hi = x.astype(BF16)
    lo = (x - hi.astype(F32)).astype(BF16)
    return jnp.concatenate([hi, lo], axis=1)


CHUNKS = [slice(c * 2 * LANES, (c + 1) * 2 * LANES) for c in range(E // (2 * LANES))]
PAIR_COLS = [slice(p * LANES, (p + 1) * LANES) for p in range(PAIRS)]


def shifted(cols):
    return slice(cols.start + E, cols.stop + E)


def pair_rows(row, p, first):
    h = first + 2 * p
    left = iota((8, LANES), 1) < HDIM
    return jnp.where(left, row[:, h : h + 1], row[:, h + 1 : h + 2])


def scan_states(out_ref, state_ref, tot_ref, add_ref, first, backward):
    rows = slice(0, STATE) if first == 0 else slice(STATE, 2 * STATE)
    order = range(add_ref.shape[0])
    for c in reversed(order) if backward else order:
        dec = jnp.exp2(tot_ref[c])
        for p, cols in enumerate(PAIR_COLS):
            state = state_ref[:, cols]
            out_ref[c, rows, cols] = state.astype(BF16)
            state_ref[:, cols] = pair_rows(dec, p, first)[0:1] * state + add_ref[c, rows, cols].astype(F32)


def step_sizes(dtraw, hp_ref):
    lane = iota(dtraw.shape, 1)
    pre = jnp.where(lane < 2 * HEADS, dtraw + hp_ref[0:1, :], 0.0)
    dt = jnp.maximum(pre, 0.0) + jnp.log1p(jnp.exp(-jnp.abs(pre)))
    return pre, dt, hp_ref[1:2, :] * dt


def states_kernel(
    act_ref, dtraw_ref, hp_ref, u_ref, v_ref, ut_ref, vt_ref, eu_ref, wv_ref, tot_ref, s_ref, pay_ref,
    exp_ref, dev_ref, cum_ref, z_ref,
):
    b = pl.program_id(0)
    nb = pl.num_programs(0)

    @pl.when(b == 0)
    def _():
        fill_expand(exp_ref)
        dev_ref[...] = jnp.zeros_like(dev_ref)
        cum_ref[...] = jnp.zeros_like(cum_ref)

    sq = (STRETCH, LANES)
    lane = iota(sq, 1)
    forward = lane < HEADS
    _, dt, lg = step_sizes(dtraw_ref[...], hp_ref)
    dtb = dt.astype(BF16).astype(F32)
    lgb = lg.astype(BF16)
    upto = jnp.where(iota(sq, 0) >= iota(sq, 1), 1.0, 0.0).astype(BF16)
    run = dot(upto, lgb)
    before = run - lgb.astype(F32)
    total = run[STRETCH - 1 : STRETCH, :] * LOG2E
    logdt = jnp.where(dtb > 0.0, jnp.log(jnp.where(dtb > 0.0, dtb, 1.0)) * LOG2E, -1e30)
    u = jnp.where(forward, before, -run) * LOG2E
    v = jnp.where(forward, -run, before) * LOG2E + logdt
    u_ref[...] = u
    v_ref[...] = v
    ut_ref[0] = u.T
    vt_ref[0] = v.T
    eu = jnp.exp2(u + jnp.where(forward, 0.0, total))
    wv = jnp.exp2(v + jnp.where(forward, total, 0.0))
    eu_ref[...] = eu
    wv_ref[...] = wv
    total8 = jnp.broadcast_to(total, (8, LANES))
    tot_ref[0] = total8

    bt = act_ref[:, E : E + LANES].T
    w2 = two_parts(wv)
    for cols in CHUNKS:
        x = act_ref[:, cols].astype(F32)
        z_ref[:, cols] = (x * dot(w2, exp_ref[:, cols])).astype(BF16)
        z_ref[:, shifted(cols)] = (x * dot(w2, exp_ref[:, shifted(cols)])).astype(BF16)
    dec = jnp.exp2(total8)
    pre = jnp.exp2(cum_ref[...])
    for c, cols in enumerate(CHUNKS):
        sf = dot(bt[:STATE], z_ref[:, cols])
        sr = dot(bt[STATE:], z_ref[:, shifted(cols)])
        s_ref[0, :STATE, cols] = sf.astype(BF16)
        s_ref[0, STATE:, cols] = sr.astype(BF16)
        dec_f = jnp.concatenate([pair_rows(dec, 2 * c, 0), pair_rows(dec, 2 * c + 1, 0)], axis=1)
        pre_r = jnp.concatenate([pair_rows(pre, 2 * c, HEADS), pair_rows(pre, 2 * c + 1, HEADS)], axis=1)
        dev_ref[:STATE, cols] = dec_f[0:1] * dev_ref[:STATE, cols] + sf
        dev_ref[STATE:, cols] = dev_ref[STATE:, cols] + pre_r[0:1] * sr
    cum_ref[...] = cum_ref[...] + total8

    @pl.when(b == nb - 1)
    def _():
        write_payload(pay_ref, dev_ref, cum_ref)


def write_payload(pay_ref, dev_ref, cum_ref):
    cum = cum_ref[...]
    pay_ref[0, :STATE] = dev_ref[:STATE].astype(BF16)
    pay_ref[1, :STATE] = dev_ref[STATE:].astype(BF16)
    for k in range(2):
        for p, cols in enumerate(PAIR_COLS):
            row = pair_rows(cum, p, k * HEADS)
            pay_ref[k, STATE:, cols] = jnp.concatenate([row, row], axis=0).astype(BF16)


PAY = STATE + 16


def block_states(act, dtraw, hp):
    length = act.shape[0]
    nb = length // STRETCH
    sq = pl.BlockSpec((STRETCH, LANES), lambda b: (b, 0))
    cube = pl.BlockSpec((1, STRETCH, LANES), lambda b: (b, 0, 0))
    flat = jax.ShapeDtypeStruct((length, LANES), F32)
    deep = jax.ShapeDtypeStruct((nb, LANES, STRETCH), F32)
    return pl.pallas_call(
        states_kernel,
        grid=(nb,),
        in_specs=[pl.BlockSpec((STRETCH, CHANNELS), lambda b: (b, 0)), sq, whole((8, LANES))],
        out_specs=[
            sq, sq, cube, cube, sq, sq,
            pl.BlockSpec((1, 8, LANES), lambda b: (b, 0, 0)),
            pl.BlockSpec((1, 2 * STATE, E), lambda b: (b, 0, 0)),
            whole((2, PAY, E)),
        ],
        out_shape=[
            flat, hbm((length, LANES), F32), hbm((nb, LANES, STRETCH), F32), deep, flat, hbm((length, LANES), F32),
            jax.ShapeDtypeStruct((nb, 8, LANES), F32),
            hbm((nb, 2 * STATE, E), BF16),
            jax.ShapeDtypeStruct((2, PAY, E), BF16),
        ],
        scratch_shapes=[
            pltpu.VMEM((2 * LANES, 2 * E), BF16),
            pltpu.VMEM((2 * STATE, E), F32),
            pltpu.VMEM((8, LANES), F32),
            pltpu.VMEM((STRETCH, 2 * E), BF16),
        ],
        compiler_params=params(12),
        cost_estimate=cost(4e9, 12 << 20),
        name="block_states",
    )(in_hbm(act), dtraw, hp)


def from_others(me, got_ref, upward):
    n = got_ref.shape[0] + 1
    side = lambda d: (d < me) if upward else (d > me)
    total = jnp.zeros((STATE, E), F32)
    for q in range(1, n):
        d = jnp.bitwise_xor(me, q)
        log = jnp.zeros((1, E), F32)
        for k in range(1, n):
            if k != q:
                e = jnp.bitwise_xor(me, k)
                between = ((d < e) & (e < me)) if upward else ((me < e) & (e < d))
                row = got_ref[k - 1, STATE : STATE + 1, :].astype(F32)
                log = log + jnp.where(between, row, 0.0)
        term = jnp.exp2(log) * got_ref[q - 1, :STATE, :].astype(F32)
        total = total + jnp.where(side(d), term, 0.0)
    return total


MAPS = slice(E, E + LANES), slice(E + LANES, E + 2 * LANES)


def split_store(ref, rows, cols, value):
    hi = value.astype(BF16)
    ref[rows, cols] = hi
    ref[rows, shifted(cols)] = (value - hi.astype(F32)).astype(BF16)


def sigmoid(x):
    return 0.5 * jnp.tanh(0.5 * x) + 0.5


def gate_kernel(
    me_ref, act_ref, z_ref, dg_ref, u_ref, vt_ref, eu_ref, s_ref, got_ref, tot_ref, rows_ref,
    gated_ref, dz_ref, dy_ref, yz_ref, gain_ref, ent_ref, p_ref, pay_ref, skip_ref,
    exp_ref, heads_ref, dev_ref, cum_ref, e_ref, y_ref, yv_ref, sig_ref, prod_ref, sums_ref, state_ref,
):
    b = pl.program_id(0)
    nb = pl.num_programs(0)

    @pl.when(b == 0)
    def _():
        fill_expand(exp_ref)
        fill_heads(heads_ref)
        dev_ref[...] = jnp.zeros_like(dev_ref)
        cum_ref[...] = jnp.zeros_like(cum_ref)
        sums_ref[...] = jnp.zeros_like(sums_ref)
        me = me_ref[0]
        state_ref[...] = from_others(me, got_ref, True)
        scan_states(ent_ref, state_ref, tot_ref, s_ref, 0, False)
        state_ref[...] = from_others(me, got_ref, False)
        scan_states(ent_ref, state_ref, tot_ref, s_ref, HEADS, True)

    sq = (STRETCH, STRETCH)
    i, j = iota(sq, 0), iota(sq, 1)
    after_j, at = i > j, i >= j
    lower = jnp.where(after_j, 1.0, 0.0).astype(BF16)
    upper = jnp.where(at, 0.0, 1.0).astype(BF16)
    bm, cm = act_ref[:, MAPS[0]], act_ref[:, MAPS[1]]
    cf, cr = cm[:, :STATE], cm[:, STATE:]
    gram = jnp.where(after_j, dot_nt(cf, bm[:, :STATE]), jnp.where(at, 0.0, dot_nt(cr, bm[:, STATE:])))
    left = iota((STRETCH, LANES), 1) < HDIM
    first_half = jnp.bitwise_and(iota((STRETCH, LANES), 1), HDIM - 1) < HDIM // 2

    e2 = eu_ref[...].astype(BF16)
    for cols in CHUNKS:
        for c, state in ((cf, ent_ref[b, :STATE, cols]), (cr, ent_ref[b, STATE:, cols])):
            at_cols = cols if c is cf else shifted(cols)
            e = dot(e2, exp_ref[:LANES, at_cols])
            e_ref[:, at_cols] = e
            y_ref[:, at_cols] = e * dot(c, state)

    square = jnp.zeros((STRETCH, LANES), F32)
    cross = jnp.zeros((STRETCH, LANES), F32)
    for p, cols in enumerate(PAIR_COLS):
        mats = []
        for h in (2 * p, 2 * p + 1):
            r = HEADS + h
            row = jnp.where(at, u_ref[:, h : h + 1], u_ref[:, r : r + 1])
            col = jnp.where(after_j, vt_ref[0, h : h + 1, :], vt_ref[0, r : r + 1, :])
            mats.append((jnp.exp2(row + col) * gram).astype(BF16))
        mats = [m * lower for m in mats] + [m * upper for m in mats]
        y = dot(jnp.concatenate(mats, axis=0), act_ref[:, cols])
        yf = y_ref[:, cols] + jnp.where(left, y[:STRETCH], y[STRETCH : 2 * STRETCH])
        yr = y_ref[:, shifted(cols)] + jnp.where(left, y[2 * STRETCH : 3 * STRETCH], y[3 * STRETCH :])
        y_ref[:, cols] = yf
        y_ref[:, shifted(cols)] = yr
        yv = yf + yr + rows_ref[0:1, cols] * act_ref[:, cols].astype(F32)
        yv_ref[:, cols] = yv
        z = z_ref[:, cols].astype(F32)
        sig = sigmoid(z)
        sig_ref[:, cols] = sig
        yg = yv * (z * sig)
        square = square + yg * yg
        cross = cross + rows_ref[1:2, cols] * dg_ref[:, cols].astype(F32) * yg
    inv = lax.rsqrt(jnp.sum(square, axis=1, keepdims=True) / E + EPSILON)
    back = inv * inv * inv * (jnp.sum(cross, axis=1, keepdims=True) / E)

    for p, cols in enumerate(PAIR_COLS):
        z = z_ref[:, cols].astype(F32)
        sig = sig_ref[:, cols]
        ga = z * sig
        yv = yv_ref[:, cols]
        yg = yv * ga
        gain = rows_ref[1:2, cols]
        gated_ref[:, cols] = (yg * inv * gain).astype(BF16)
        dyg = inv * (gain * dg_ref[:, cols].astype(F32)) - yg * back
        dy = dyg * ga
        dz_ref[:, cols] = (dyg * yv * (sig + ga * (1.0 - sig))).astype(BF16)
        low_dy = dy.astype(BF16)
        dy_ref[:, cols] = low_dy
        fold = lambda t: jnp.sum(t.reshape(STRETCH // 8, 8, LANES), axis=0)
        sums_ref[:, cols] = sums_ref[:, cols] + fold(dy * act_ref[:, cols].astype(F32))
        dy = low_dy.astype(F32)
        yz_ref[:, cols] = (e_ref[:, cols] * dy).astype(BF16)
        yz_ref[:, shifted(cols)] = (e_ref[:, shifted(cols)] * dy).astype(BF16)
        pair = fold_pair(y_ref[:, cols] * dy, y_ref[:, shifted(cols)] * dy, first_half)
        split_store(prod_ref, slice(None), cols, pair)
    gain_ref[...] = dot(prod_ref[...], heads_ref[...])

    total8 = tot_ref[b]
    dec = jnp.exp2(total8)
    pre = jnp.exp2(cum_ref[...])
    ct = cm.T
    for c, cols in enumerate(CHUNKS):
        pf = dot(ct[:STATE], yz_ref[:, cols])
        pr = dot(ct[STATE:], yz_ref[:, shifted(cols)])
        p_ref[0, :STATE, cols] = pf.astype(BF16)
        p_ref[0, STATE:, cols] = pr.astype(BF16)
        pre_f = jnp.concatenate([pair_rows(pre, 2 * c, 0), pair_rows(pre, 2 * c + 1, 0)], axis=1)
        dec_r = jnp.concatenate([pair_rows(dec, 2 * c, HEADS), pair_rows(dec, 2 * c + 1, HEADS)], axis=1)
        dev_ref[:STATE, cols] = dev_ref[:STATE, cols] + pre_f[0:1] * pf
        dev_ref[STATE:, cols] = dec_r[0:1] * dev_ref[STATE:, cols] + pr
    cum_ref[...] = cum_ref[...] + total8

    @pl.when(b == nb - 1)
    def _():
        write_payload(pay_ref, dev_ref, cum_ref)
        skip_ref[...] = lax.dot_general(
            sums_ref[...], exp_ref[:LANES, :E].astype(F32), NT,
            precision=lax.Precision.HIGHEST, preferred_element_type=F32,
        )


def gate(me, act, z, dg, u, vt, eu, s, got, tot, rows):
    length = act.shape[0]
    nb = length // STRETCH
    line = pl.BlockSpec((STRETCH, E), lambda b: (b, 0))
    sq = pl.BlockSpec((STRETCH, LANES), lambda b: (b, 0))
    low_line = jax.ShapeDtypeStruct((length, E), BF16)
    return pl.pallas_call(
        gate_kernel,
        grid=(nb,),
        in_specs=[
            pl.BlockSpec(memory_space=pltpu.SMEM),
            pl.BlockSpec((STRETCH, CHANNELS), lambda b: (b, 0)),
            line,
            line,
            sq,
            pl.BlockSpec((1, LANES, STRETCH), lambda b: (b, 0, 0)),
            sq,
            whole(s.shape),
            whole(got.shape),
            whole(tot.shape),
            whole((8, E)),
        ],
        out_specs=[
            line,
            line,
            line,
            pl.BlockSpec((STRETCH, 2 * E), lambda b: (b, 0)),
            sq,
            whole(s.shape),
            pl.BlockSpec((1, 2 * STATE, E), lambda b: (b, 0, 0)),
            whole((2, PAY, E)),
            whole((8, LANES)),
        ],
        out_shape=[
            low_line,
            low_line,
            low_line,
            jax.ShapeDtypeStruct((length, 2 * E), BF16),
            jax.ShapeDtypeStruct((length, LANES), F32),
            jax.ShapeDtypeStruct(s.shape, BF16),
            jax.ShapeDtypeStruct(s.shape, BF16),
            jax.ShapeDtypeStruct((2, PAY, E), BF16),
            jax.ShapeDtypeStruct((8, LANES), F32),
        ],
        scratch_shapes=[
            pltpu.VMEM((2 * LANES, 2 * E), BF16),
            pltpu.VMEM((2 * E, LANES), BF16),
            pltpu.VMEM((2 * STATE, E), F32),
            pltpu.VMEM((8, LANES), F32),
            pltpu.VMEM((STRETCH, 2 * E), F32),
            pltpu.VMEM((STRETCH, 2 * E), F32),
            pltpu.VMEM((STRETCH, E), F32),
            pltpu.VMEM((STRETCH, E), F32),
            pltpu.VMEM((STRETCH, 2 * E), BF16),
            pltpu.VMEM((8, E), F32),
            pltpu.VMEM((STATE, E), F32),
        ],
        compiler_params=params(30),
        cost_estimate=cost(16e9, 32 << 20),
        name="gate",
    )(me, in_hbm(act), z, dg, u, vt, eu, in_hbm(s), got, tot, rows)


def mixer_back_kernel(
    me_ref, act_ref, dy_ref, yz_ref, v_ref, ut_ref, wv_ref, gain_ref, ent_ref, p_ref, got_ref, tot_ref,
    dtraw_ref, hp_ref,
    dx_ref, dmap_ref, ddt_ref, sums_ref,
    exp_ref, heads_ref, out_ref, v_in_ref, xz_ref, prod_ref, state_ref, row_ref,
):
    b = pl.program_id(0)
    sq = (STRETCH, STRETCH)
    j, i = iota(sq, 0), iota(sq, 1)
    after_j, at = i > j, i >= j

    @pl.when(b == 0)
    def _():
        fill_expand(exp_ref)
        fill_heads(heads_ref)
        sums_ref[...] = jnp.zeros_like(sums_ref)
        row_ref[...] = jnp.zeros_like(row_ref)
        me = me_ref[0]
        state_ref[...] = from_others(me, got_ref, False)
        scan_states(out_ref, state_ref, tot_ref, p_ref, 0, True)
        state_ref[...] = from_others(me, got_ref, True)
        scan_states(out_ref, state_ref, tot_ref, p_ref, HEADS, False)

    bm, cm = act_ref[:, MAPS[0]], act_ref[:, MAPS[1]]
    bf, br, cf, cr = bm[:, :STATE], bm[:, STATE:], cm[:, :STATE], cm[:, STATE:]
    gram = jnp.where(after_j, dot_nt(bf, cf), jnp.where(at, 0.0, dot_nt(br, cr)))
    lower = jnp.where(after_j, 1.0, 0.0).astype(BF16)
    upper = jnp.where(at, 0.0, 1.0).astype(BF16)
    left = iota((STRETCH, LANES), 1) < HDIM
    first_half = jnp.bitwise_and(iota((STRETCH, LANES), 1), HDIM - 1) < HDIM // 2
    left_low = jnp.where(left, 1.0, 0.0).astype(BF16)
    right_low = jnp.where(left, 0.0, 1.0).astype(BF16)

    w2 = wv_ref[...].astype(BF16)
    for cols in CHUNKS:
        x = act_ref[:, cols].astype(F32)
        for k, m, state in ((0, bf, out_ref[b, :STATE, cols]), (1, br, out_ref[b, STATE:, cols])):
            at_cols = cols if k == 0 else shifted(cols)
            w = dot(w2, exp_ref[:LANES, at_cols])
            v_in = w * dot(m, state)
            v_in_ref[:, at_cols] = v_in
            xz_ref[:, at_cols] = (w * x).astype(BF16)
            row_ref[k : k + 1, cols] = jnp.sum(v_in * x, axis=0, keepdims=True)
    p_out, s_in = out_ref[b], ent_ref[0]
    db_f = dot_nt(xz_ref[:, :E], p_out[:STATE])
    db_r = dot_nt(xz_ref[:, E:], p_out[STATE:])
    dc_f = dot_nt(yz_ref[:, :E], s_in[:STATE])
    dc_r = dot_nt(yz_ref[:, E:], s_in[STATE:])

    dgram = jnp.zeros(sq, F32)
    for p, cols in enumerate(PAIR_COLS):
        xb, dyb = act_ref[:, cols], dy_ref[:, cols]
        x = xb.astype(F32)
        dm = dot_nt(jnp.concatenate([xb * left_low, xb * right_low], axis=0), dyb)
        mats = []
        for k, h in enumerate((2 * p, 2 * p + 1)):
            r = HEADS + h
            row = jnp.where(after_j, v_ref[:, h : h + 1], v_ref[:, r : r + 1])
            col = jnp.where(at, ut_ref[0, h : h + 1, :], ut_ref[0, r : r + 1, :])
            decay = jnp.exp2(row + col)
            mats.append((decay * gram).astype(BF16))
            dgram = dgram + dm[k * STRETCH : (k + 1) * STRETCH] * decay
        mats = [m * lower for m in mats] + [m * upper for m in mats]
        d4 = dot(jnp.concatenate(mats, axis=0), dyb)
        vf = v_in_ref[:, cols] + jnp.where(left, d4[:STRETCH], d4[STRETCH : 2 * STRETCH])
        vr = v_in_ref[:, shifted(cols)] + jnp.where(left, d4[2 * STRETCH : 3 * STRETCH], d4[3 * STRETCH :])
        dx_ref[:, cols] = (vf + vr).astype(BF16)
        split_store(prod_ref, slice(0, STRETCH), cols, fold_pair(vf * x, vr * x, first_half))
    pe = p_out.astype(F32) * s_in.astype(F32)
    col_sum = lambda t: jnp.sum(t, axis=0, keepdims=True)
    row_ref[2:3, :] = col_sum(pe[:STATE])
    row_ref[3:4, :] = col_sum(pe[STATE:])
    for cols in PAIR_COLS:
        f = jnp.concatenate([row_ref[0:1, cols], row_ref[2:3, cols], jnp.zeros((14, LANES), F32)], axis=0)
        r = jnp.concatenate([row_ref[1:2, cols], row_ref[3:4, cols], jnp.zeros((14, LANES), F32)], axis=0)
        split_store(prod_ref, slice(STRETCH, STRETCH + 16), cols, fold_pair(f, r, first_half[:16]))
    sums = dot(prod_ref[...], heads_ref[...])
    dlog = sums[:STRETCH]
    through = sums[STRETCH : STRETCH + 1] + jnp.exp2(tot_ref[b])[0:1] * sums[STRETCH + 1 : STRETCH + 2]

    gfwd = jnp.where(after_j, dgram, 0.0).astype(BF16)
    grev = jnp.where(at, 0.0, dgram).astype(BF16)
    gfwd_t = gfwd.T
    grev_t = grev.T
    dmap_ref[:, :LANES] = jnp.concatenate([db_f + dot(gfwd, cf), db_r + dot(grev, cr)], axis=1)
    dmap_ref[:, LANES:] = jnp.concatenate([dc_f + dot(gfwd_t, bf), dc_r + dot(grev_t, br)], axis=1)

    lane = iota((STRETCH, LANES), 1)
    forward = lane < HEADS
    gain = gain_ref[...]
    both = jnp.concatenate([gain, dlog], axis=1)
    top = both.astype(BF16)
    rest = both - top.astype(F32)
    mid = rest.astype(BF16)
    end = (rest - mid.astype(F32)).astype(BF16)
    later = dot(lower, top) + dot(lower, mid) + dot(lower, end)
    later_gain, later_dlog = later[:, :LANES], later[:, LANES:]
    dlg = jnp.where(
        forward,
        later_gain - later_dlog - dlog,
        (col_sum(gain) - later_gain - gain) - (col_sum(dlog) - later_dlog),
    )
    dlg = dlg + through
    pre, dt, lg = step_sizes(dtraw_ref[...], hp_ref)
    dtb = dt.astype(BF16).astype(F32)
    ok = (dtb > 0.0) & (lane < 2 * HEADS)
    ddt = jnp.where(ok, dlog / jnp.where(ok, dtb, 1.0), 0.0)
    ddt = ddt.astype(BF16).astype(F32)
    dlg = jnp.where(lane < 2 * HEADS, dlg, 0.0).astype(BF16).astype(F32)
    draw = (ddt + dlg * hp_ref[1:2, :]) * jax.nn.sigmoid(pre)
    ddt_ref[...] = draw.astype(BF16)
    fold = lambda t: jnp.sum(t.reshape(STRETCH // 8, 8, LANES), axis=0)
    sums_ref[0:8] = sums_ref[0:8] + fold(draw)
    sums_ref[8:16] = sums_ref[8:16] + fold(dlg * lg)


def mixer_back(me, act, dy, yz, v, ut, wv, gain, ent, p, got, tot, dtraw, hp):
    length = act.shape[0]
    nb = length // STRETCH
    sq = pl.BlockSpec((STRETCH, LANES), lambda b: (b, 0))
    line = pl.BlockSpec((STRETCH, E), lambda b: (b, 0))
    states = pl.BlockSpec((1, 2 * STATE, E), lambda b: (b, 0, 0))
    return pl.pallas_call(
        mixer_back_kernel,
        grid=(nb,),
        in_specs=[
            pl.BlockSpec(memory_space=pltpu.SMEM),
            pl.BlockSpec((STRETCH, CHANNELS), lambda b: (b, 0)),
            line,
            pl.BlockSpec((STRETCH, 2 * E), lambda b: (b, 0)),
            sq,
            pl.BlockSpec((1, LANES, STRETCH), lambda b: (b, 0, 0)),
            sq,
            sq,
            states,
            whole(p.shape),
            whole(got.shape),
            whole(tot.shape),
            sq,
            whole((8, LANES)),
        ],
        out_specs=[
            line,
            pl.BlockSpec((STRETCH, 2 * LANES), lambda b: (b, 0)),
            sq,
            whole((16, LANES)),
        ],
        out_shape=[
            jax.ShapeDtypeStruct((length, E), BF16),
            jax.ShapeDtypeStruct((length, 2 * LANES), F32),
            jax.ShapeDtypeStruct((length, LANES), BF16),
            jax.ShapeDtypeStruct((16, LANES), F32),
        ],
        scratch_shapes=[
            pltpu.VMEM((2 * LANES, 2 * E), BF16),
            pltpu.VMEM((2 * E, LANES), BF16),
            pltpu.VMEM(p.shape, BF16),
            pltpu.VMEM((STRETCH, 2 * E), F32),
            pltpu.VMEM((STRETCH, 2 * E), BF16),
            pltpu.VMEM((STRETCH + 16, 2 * E), BF16),
            pltpu.VMEM((STATE, E), F32),
            pltpu.VMEM((8, E), F32),
        ],
        compiler_params=params(26),
        cost_estimate=cost(16e9, 20 << 20),
        name="mixer_back",
    )(me, in_hbm(act), dy, yz, in_hbm(v), in_hbm(ut), in_hbm(wv), gain, ent, p, got, tot, dtraw, hp)


def conv_back_block(length, dact_ref, slope_ref, conv_ref, taps_ref, dconv_ref, sums_ref, dpad_ref, edge_ref, shift_ref):
    half = TAPS // 2
    fold = lambda t: jnp.sum(t.reshape(t.shape[0] // 8, 8, BLOCK), axis=0)
    sums = [jnp.zeros((8, BLOCK), F32) for _ in range(TAPS + 1)]
    zeros = jnp.zeros((MARGIN, BLOCK), BF16)
    dpad_ref[:MARGIN] = zeros
    dpad_ref[MARGIN + length :] = zeros
    for c in range(length // STRETCH):
        rows = slice(c * STRETCH, (c + 1) * STRETCH)
        dpre = dact_ref[rows] * slope_ref[rows].astype(F32)
        sums[TAPS] = sums[TAPS] + fold(dpre)
        dpad_ref[MARGIN + rows.start : MARGIN + rows.stop] = dpre.astype(BF16)
    for c in range(length // STRETCH):
        rows = slice(c * STRETCH, (c + 1) * STRETCH)
        x = conv_ref[rows].astype(F32)
        out = jnp.zeros((STRETCH, BLOCK), F32)
        for k, moved in shifted_rows(shift_ref, dpad_ref, rows.start).items():
            out = out + taps_ref[k : k + 1, :] * moved
            sums[k] = sums[k] + fold(x * moved)
        dconv_ref[rows] = out.astype(BF16)
    edge_ref[: 2 * MARGIN] = dpad_ref[: 2 * MARGIN].astype(F32)
    edge_ref[2 * MARGIN :] = dpad_ref[length:].astype(F32)
    edges = []
    for where, base in ((0, MARGIN - EDGE), (1, 3 * MARGIN)):
        first = length + where * EDGE
        x = conv_ref[length:].astype(F32)[where * EDGE : (where + 1) * EDGE]
        out = jnp.zeros((EDGE, BLOCK), F32)
        for k in range(TAPS):
            moved = edge_ref[base - k + half : base - k + half + EDGE]
            out = out + taps_ref[k : k + 1, :] * moved
            sums[k] = sums[k] + x * moved
        edges.append(out)
    dconv_ref[length:] = jnp.concatenate(edges, axis=0).astype(BF16)
    sums_ref[...] = jnp.concatenate([jnp.sum(t, axis=0, keepdims=True) for t in sums], axis=0)


def conv_back_kernel(
    dx_ref, dy_ref, dmap_ref, slope_ref, conv_ref, taps_ref, skip_ref, ddt_ref, hsum_ref, ssum_ref,
    dconv_ref, sums_ref, dact_ref, dpad_ref, edge_ref, shift_ref,
):
    j = pl.program_id(0)
    maps = E // BLOCK
    length = slope_ref.shape[0]

    @pl.when(j == 0)
    def _():
        fill_shifts(shift_ref, -1)

    @pl.when(j < maps)
    def _():
        dact_ref[...] = dx_ref[...].astype(F32) + skip_ref[0:1, :] * dy_ref[...].astype(F32)

    @pl.when(j == maps)
    def _():
        dact_ref[...] = dmap_ref[...]

    @pl.when(j <= maps)
    def _():
        conv_back_block(
            length, dact_ref, slope_ref, conv_ref, taps_ref, dconv_ref, sums_ref, dpad_ref, edge_ref, shift_ref
        )

    @pl.when(j > maps)
    def _():
        dconv_ref[:length, :LANES] = ddt_ref[...]
        dconv_ref[length:, :LANES] = jnp.zeros((2 * EDGE, LANES), BF16)
        parts = [hsum_ref[:8], hsum_ref[8:], ssum_ref[...]]
        parts = [jnp.sum(t, axis=0, keepdims=True) for t in parts]
        sums_ref[:, :LANES] = jnp.concatenate(parts + [jnp.zeros((5, LANES), F32)], axis=0)


def conv_back(dx, dy, dmap, slope, conv, taps, skip, ddt, hsums, ssums):
    ext = conv.shape[0]
    length = ext - 2 * EDGE
    early = lambda j: (0, jnp.minimum(j, E // BLOCK - 1))
    inner = lambda j: (0, jnp.minimum(j, CHANNELS // BLOCK - 1))
    col = lambda j: (0, j)
    return pl.pallas_call(
        conv_back_kernel,
        grid=(CHANNELS // BLOCK + 1,),
        in_specs=[
            pl.BlockSpec((length, BLOCK), early),
            pl.BlockSpec((length, BLOCK), early),
            whole((length, 2 * LANES)),
            pl.BlockSpec((length, BLOCK), inner),
            pl.BlockSpec((ext, BLOCK), inner),
            pl.BlockSpec((8, BLOCK), inner),
            pl.BlockSpec((8, BLOCK), early),
            whole((length, LANES)),
            whole((16, LANES)),
            whole((8, LANES)),
        ],
        out_specs=[pl.BlockSpec((ext, BLOCK), col), pl.BlockSpec((8, BLOCK), col)],
        out_shape=[
            jax.ShapeDtypeStruct((ext, WIDE), BF16),
            jax.ShapeDtypeStruct((8, WIDE), F32),
        ],
        scratch_shapes=[
            pltpu.VMEM((length, BLOCK), F32),
            pltpu.VMEM((length + 2 * MARGIN, BLOCK), BF16),
            pltpu.VMEM((4 * MARGIN, BLOCK), F32),
            pltpu.VMEM((len(SHIFTS) * STRETCH, WINDOW), BF16),
        ],
        compiler_params=params(14),
        cost_estimate=cost(2e9, 20 << 20),
        name="conv_back",
    )(dx, dy, dmap, in_hbm(slope), in_hbm(conv), taps, skip, ddt, hsums, ssums)


def send_states(payload, to_later):
    n, me = lax.axis_size("seq"), lax.axis_index("seq")
    sent, got = [], []
    for q in range(1, n):
        later = (me ^ q) > me
        first = later if to_later else ~later
        sent.append(jnp.where(first, payload[0], payload[1]))
        got.append(swap(sent[-1], "seq", q))
    return sent, got


def per_device(
    layer_in, norm_gain, in_weight, conv_weight, conv_bias, head_params, out_gain, out_weight, out_cotangent
):
    ns, nw = lax.axis_size("seq"), lax.axis_size("wt")
    ndev = ns * nw
    seq_me = lax.axis_index("seq").astype(jnp.int32)
    me = seq_me * nw + lax.axis_index("wt").astype(jnp.int32)
    me_arr, seq_arr = me.reshape(1), seq_me.reshape(1)
    tokens = layer_in[0]
    cotangent = out_cotangent[0]
    length, d = tokens.shape
    share = in_weight.shape[0]
    cshare = conv_bias.shape[0]
    gshare = out_gain.shape[0]
    spare = WIDE - (in_weight.shape[1] - E)

    small = jnp.concatenate([conv_weight.reshape(-1), conv_bias, out_gain, norm_gain])
    n_small = small.shape[0]
    small = jnp.pad(small, (0, 8 * LANES - n_small)).reshape(8, LANES)
    first = jnp.pad(in_weight[:, E:], ((0, 0), (0, spare)))
    half = E // 2
    rest = jnp.concatenate(
        [in_weight[None, :, :half], in_weight[None, :, half:E], out_weight.reshape(2, share, d)], axis=0
    )
    s1 = jnp.stack(gather_z(small)).reshape(-1, LANES)
    ends = jnp.concatenate([tokens[:EDGE], tokens[length - EDGE :]], axis=0).reshape(-1, LANES)
    s1 = jnp.concatenate([s1, ends], axis=0)
    a1 = jnp.stack(gather_z(first))
    a2 = gather_seq(a1)
    b1 = jnp.stack(gather_z(rest))
    s2 = gather_seq(after(s1, a2[1]))
    a2 = jnp.stack(a2)
    wa, wb = a2.reshape(d // 2, WIDE), swap(after(a2, b1), "wt", 1).reshape(d // 2, WIDE)

    cut = s1.shape[0] - ends.shape[0]
    around = [t[cut:].reshape(2 * EDGE, d) for t in s2]
    s2 = jnp.stack([t[:cut] for t in s2])
    s3 = swap(s2, "wt", 1)
    b2 = gather_seq(after(b1, a2, s2))
    nothing = jnp.zeros((EDGE, d), BF16)
    pick = lambda rows, other: sum((jnp.where(seq_me ^ q == other, around[q][rows], nothing) for q in range(ns)), nothing)
    ext = jnp.concatenate([tokens, pick(slice(EDGE, None), seq_me - 1), pick(slice(0, EDGE), seq_me + 1)], axis=0)

    blocks = jnp.arange(d, dtype=jnp.int32) // share
    offsets = block_order(ns, nw)
    offset_of = jnp.array(offsets, jnp.int32)
    natural = (offset_of[blocks] ^ me) * share + jnp.arange(d, dtype=jnp.int32) % share
    perm = (jnp.arange(d, dtype=jnp.int32)[:, None] == natural[None, :]).astype(BF16)
    u_x = dot(ext, perm)
    inv_in = lax.rsqrt(jnp.mean(jnp.square(ext.astype(F32)), axis=1, keepdims=True) + EPSILON)

    extras = jnp.stack([s2, s3]).reshape(ndev, 8 * LANES)
    order = jnp.arange(ndev, dtype=jnp.int32)[:, None] == (offset_of[None, :] ^ me)
    nat = dot(order.astype(BF16), extras[:, :n_small])
    taps = jnp.transpose(nat[:, : TAPS * cshare].reshape(ndev, TAPS, cshare), (1, 0, 2)).reshape(TAPS, CHANNELS)
    bias = nat[:, TAPS * cshare : (TAPS + 1) * cshare].reshape(1, CHANNELS)
    taps = jnp.concatenate([taps, bias], axis=0)
    gain_out = nat[:, (TAPS + 1) * cshare : (TAPS + 1) * cshare + gshare].reshape(1, E)
    gain_x = extras[:, n_small - share : n_small].reshape(1, d).astype(F32)

    normed = (u_x * inv_in * gain_x).astype(BF16)
    conv, act, slope, dtraw = conv_forward(normed, wa, wb, taps)

    twice = jnp.concatenate([head_params, head_params], axis=1)
    rates = jnp.stack([twice[0], -jnp.exp(twice[1])])
    hp = jnp.pad(rates, ((0, 6), (0, LANES - 2 * HEADS)))
    u, v, ut, vt, eu, wv, tot, s, pay = block_states(act, dtraw, hp)
    sent, got = send_states(pay, True)
    b2 = [after(t, *sent).reshape(-1, share, half) for t in b2]
    w_z, w_out = unpack(offsets, me_arr, b2 + [swap(t, "wt", 1) for t in b2])
    w_z, w_out = w_z.reshape(d, E), w_out.reshape(E, d)
    own = normed[:length]
    z = dot(own, w_z).astype(BF16)
    dgated = dot_nt(cotangent, w_out).astype(BF16)
    skip = jnp.repeat(head_params[2], HDIM)[None]
    rows = jnp.concatenate([skip, gain_out, jnp.zeros((6, E), F32)], axis=0)
    got = jnp.stack([after(t, z, dgated) for t in got])
    gated, dz, dy, yz, gain, ent, p, pay, ssums = gate(seq_arr, act, z, dgated, u, vt, eu, s, got, tot, rows)
    sent, got = send_states(pay, False)

    gated_then, dz_then = after(gated, *sent), after(dz, *sent)
    g_out = lax.dot_general(gated_then, cotangent, TN, preferred_element_type=F32).astype(BF16)
    g_z = lax.dot_general(own, dz_then, TN, preferred_element_type=F32).astype(BF16)
    dn_z = dot_nt(dz_then, w_z)
    layer_out = (tokens.astype(F32) + dot(gated_then, w_out)).astype(BF16)[None]
    got = [after(t, g_out, g_z, dn_z, layer_out) for t in got]
    kept, moved = pack(offsets, me_arr, g_z.reshape(ndev, share, E), g_out.reshape(2 * ndev, share, d))
    moved = swap(moved, "wt", 1)
    split = lambda t: t.reshape(ns, nw // 2, 4, share, half)
    r1 = scatter_core(split(kept), split(after(moved, *got)))
    r_got = [swap(r1[q], "seq", q) for q in range(1, ns)]
    dx, dmap, ddt, hsums = mixer_back(
        seq_arr, act, after(dy, *r1), yz, v, ut, wv, gain, ent, p, jnp.stack(got), tot, dtraw, hp
    )
    r2 = scatter_seq(r1, [after(t, dx) for t in r_got])
    z_got = [swap(r2[q], "wt", 2 * q) for q in range(1, nw // 2)]
    dconv, csums = conv_back(after(dx, *r2), dy, dmap, slope, conv, taps, rows, ddt, hsums, ssums)
    r3 = scatter_z(r2, [after(t, dconv) for t in z_got])

    g_c = lax.dot_general(normed, dconv, TN, preferred_element_type=F32).astype(BF16)
    g_c = g_c.reshape(2, ns, nw // 2, share, WIDE)
    steps = sum_steps(ns, nw)
    csums = csums + swap(csums, *steps[0])
    sent = after(g_c[1], r3, csums)
    f1 = scatter_core(g_c[0], swap(sent, "wt", 1))
    w_first = jnp.concatenate([wa, wb])
    dn = dot_nt(after(dconv, *f1), w_first)
    f_got = [swap(f1[q], "seq", q) for q in range(1, ns)]
    f2 = scatter_seq(f1, f_got)
    dn = dn + jnp.concatenate([dn_z, jnp.zeros((2 * EDGE, d), F32)], axis=0)
    grad_first = scatter_z(f2)
    for (axis, q), wait in zip(steps[1:], [f1, [dn]] + [[]] * len(steps)):
        csums = csums + after(swap(csums, axis, q), *wait)

    forward = [(i, i + 1) for i in range(ns - 1)]
    backward = [(i + 1, i) for i in range(ns - 1)]
    dn_hi = dn.astype(BF16)
    dn_lo = (dn - dn_hi.astype(F32)).astype(BF16)
    dn = dot_nt(dn_hi, perm) + dot_nt(dn_lo, perm)
    edges = after(dn[length:], f_got[0])
    prev_edge = lax.ppermute(edges[:EDGE], "seq", backward)
    next_edge = lax.ppermute(edges[EDGE:], "seq", forward)
    middle = jnp.zeros((length - 2 * EDGE, d), F32)
    dn = dn[:length] + jnp.concatenate([next_edge, middle, prev_edge], axis=0)
    u, inv = tokens.astype(F32), inv_in[:length]
    scaled = nat[:, n_small - share :].reshape(1, d) * dn
    in_grad = after(cotangent, *f2).astype(F32) + inv * scaled
    in_grad = in_grad - u * inv**3 * jnp.mean(scaled * u, axis=1, keepdims=True)

    grad_z = jnp.concatenate([r3[0], r3[1]], axis=1)
    grad_out = r3[2:].reshape(gshare, d)
    vec = lax.dynamic_slice(csums, (0, me * cshare), (8, cshare))
    pair = csums[:3, CHANNELS : CHANNELS + 2 * HEADS]
    head_grad = pair[:, :HEADS] + pair[:, HEADS:]
    grad_in = jnp.concatenate([grad_z, grad_first[:, : WIDE - spare]], axis=1)
    gain_grad = jnp.sum(in_weight.astype(F32) * grad_in, axis=1) / norm_gain.astype(F32)
    out_gain_grad = jnp.sum(out_weight.astype(F32) * grad_out, axis=1) / out_gain.astype(F32)
    return (
        layer_out,
        in_grad[None],
        gain_grad,
        grad_in,
        vec[:TAPS],
        vec[TAPS],
        head_grad,
        out_gain_grad,
        grad_out,
    )


def solution(mesh):
    rows = P(("seq", "wt"))
    table = P(("seq", "wt"), None)
    tokens = P("wt", "seq", None)
    taps = P(None, ("seq", "wt"))
    return jax.shard_map(
        per_device,
        mesh=mesh,
        in_specs=(tokens, rows, table, taps, rows, P(), rows, table, tokens),
        out_specs=(tokens, tokens, rows, table, taps, rows, P(), rows, table),
        check_vma=False,
    )
```
